32 devices in a mesh: head: 4 (over x, core), row: 8 (over z, y).
Axes of the slice: x: 2, y: 2, z: 4, core: 2. Of those that a mesh axis runs over, the one named last changes fastest.
Arguments:
- inputs: bfloat16 [8, 8192, 512], P('row', 'head'), may hold values from -6 to 6
- cotangent: bfloat16 [8, 8192, 512], P('row', 'head'), may hold values from -6 to 6
- segments: int32 [8, 8192], P('row'), may hold values from 0 to 31, never falling along the last dimension, each value on 1 to 1024 neighbouring positions
- feature_matrix: bfloat16 [256, 64], replicated, may hold values from -6 to 6
- w_qkv: float32 [512, 3, 512], P(('head', 'row')), may hold values from -0.25 to 0.25
- w_out: float32 [512, 512], P(('head', 'row')), may hold values from -1 to 1
- w_up: float32 [512, 2048], P(('head', 'row')), may hold values from -0.25 to 0.25
- w_down: float32 [2048, 512], P(('head', 'row')), may hold values from -0.125 to 0.125
- gains: float32 [512, 2], P(('head', 'row')), may hold values from 0.3 to 2.7
- first_qkv: float32 [512, 3, 512], P(('head', 'row')), may hold values from -0.0004272461 to 0.0004272461
- second_qkv: float32 [512, 3, 512], P(('head', 'row')), may hold values from 2.9802324e-11 to 4.768372e-10
- first_out: float32 [512, 512], P(('head', 'row')), may hold values from -0.00021362305 to 0.00021362305
- second_out: float32 [512, 512], P(('head', 'row')), may hold values from 7.6293945e-12 to 1.2207031e-10
- first_up: float32 [512, 2048], P(('head', 'row')), may hold values from -0.00021362305 to 0.00021362305
- second_up: float32 [512, 2048], P(('head', 'row')), may hold values from 7.6293945e-12 to 1.2207031e-10
- first_down: float32 [2048, 512], P(('head', 'row')), may hold values from -0.00030517578 to 0.00030517578
- second_down: float32 [2048, 512], P(('head', 'row')), may hold values from 1.9073486e-11 to 3.0517577e-10
- first_gains: float32 [512, 2], P(('head', 'row')), may hold values from -0.0012207031 to 0.0012207031
- second_gains: float32 [512, 2], P(('head', 'row')), may hold values from 3.0517577e-10 to 4.8828124e-09
- step_count: int32 [], replicated, may hold values from 1 to 20
Outputs:
- out_act: bfloat16 [8, 8192, 512], P('row', 'head')
- input_grad: float32 [8, 8192, 512], P('row', 'head')
- grad_norm: float32 [], replicated
- clipped_qkv: float32 [512, 3, 512], P(('head', 'row'))
- moment_qkv: float32 [512, 3, 512], P(('head', 'row'))
- square_qkv: float32 [512, 3, 512], P(('head', 'row'))
- updated_qkv: float32 [512, 3, 512], P(('head', 'row'))
- clipped_out: float32 [512, 512], P(('head', 'row'))
- moment_out: float32 [512, 512], P(('head', 'row'))
- square_out: float32 [512, 512], P(('head', 'row'))
- updated_out: float32 [512, 512], P(('head', 'row'))
- clipped_up: float32 [512, 2048], P(('head', 'row'))
- moment_up: float32 [512, 2048], P(('head', 'row'))
- square_up: float32 [512, 2048], P(('head', 'row'))
- updated_up: float32 [512, 2048], P(('head', 'row'))
- clipped_down: float32 [2048, 512], P(('head', 'row'))
- moment_down: float32 [2048, 512], P(('head', 'row'))
- square_down: float32 [2048, 512], P(('head', 'row'))
- updated_down: float32 [2048, 512], P(('head', 'row'))
- clipped_gains: float32 [512, 2], P(('head', 'row'))
- moment_gains: float32 [512, 2], P(('head', 'row'))
- square_gains: float32 [512, 2], P(('head', 'row'))
- updated_gains: float32 [512, 2], P(('head', 'row'))
The draws below stay inside these ranges and needn't reach their ends.
Inputs may be any that keep to these rules, and one draw needn't show every extreme that they name: `segments`: within a packed row segment numbers never fall; each segment spans 1 to 1024 positions and one spans exactly 1024.
All inputs are finite; a program needn't handle non-finite values.
Results may differ from the reference program's by a relative error of at most 0.028.
The reference program's roundings to bfloat16 on the way count: a program that leaves them out, or rounds other values in their place, can miss the bound.
Values may be sent and summed in bfloat16 or wider, within the bound.
No kernel may reach another device: no remote copies, remote signals or barrier semaphores. Data moves between devices by JAX's collectives and lax.ppermute only.
A program may use at most 320 MiB of HBM per device.

```python
import math
import jax
import jax.numpy as jnp
import numpy as np
from jax import lax

D = 512
HEADS = 8
HD = 64
FEATS = 256
FF = 2048
BLOCK = 512
LEN = 8192
ROWS = 8
SEGS = 32
SEG_MOST = 1024


def draw_gains(key, part):
    rising = 0.6 + 1.2 * jnp.arange(D, dtype=jnp.float32) / (D - 1)
    factors = 1.0 + 0.1 * jax.random.truncated_normal(key, -3.0, 3.0, (D, 2), jnp.float32)
    return rising[:, None] * factors


def shard_levels(rng, shape, cuts, smallest, top_value):
    def one(dim, parts):
        heights = jax.random.uniform(jax.random.fold_in(jax.random.fold_in(rng, 6), dim), (parts,), jnp.float32, smallest / len(cuts), top_value / len(cuts))
        return jnp.repeat(jnp.exp(heights), shape[dim] // parts).reshape((-1,) + (1,) * (len(shape) - dim - 1))

    gain = one(*cuts[0])
    for cut in cuts[1:]:
        gain = gain * one(*cut)
    return gain


def length_profile(amount, total, most, lean):
    portions = [(1 << 20) // math.isqrt(rank ** lean) + 1 for rank in range(2, amount + 1)]
    surplus, counts = total - most - (amount - 1), [1] * (amount - 1)
    while surplus > 0:
        movable = [i for i in range(amount - 1) if counts[i] < most]
        pool, remaining = sum([portions[i] for i in movable]), surplus
        for i in movable:
            addition = min(most - counts[i], max(1, remaining * portions[i] // pool), surplus)
            counts[i] = counts[i] + addition
            surplus = surplus - addition
    return np.array([most] + counts)


def uneven_parts(rng, count, total, most, lean):
    if count == 2:
        one = jax.random.randint(rng, (), max(1, total - most), min(most, total - 1) + 1)
        return jnp.stack([one, total - one])
    sizes = jnp.asarray(length_profile(count, total, most, lean), jnp.int32)
    twos = (count - 1) // 2
    donor, sink = sizes[1:1 + 2 * twos:2], sizes[2:2 + 2 * twos:2]
    room = jnp.minimum(donor - 1, most - sink)
    shifted = jax.random.randint(jax.random.fold_in(rng, 1), (twos,), 0, 1 << 20) % (room + 1)
    sizes = sizes.at[1:1 + 2 * twos:2].set(donor - shifted).at[2:2 + 2 * twos:2].set(sink + shifted)
    return sizes[jax.random.permutation(jax.random.fold_in(rng, 2), count)]


def bell_draw(stream_key, extent, spread, most, split=(), held_as=jnp.bfloat16):
    drawn = jax.random.normal(stream_key, extent, jnp.float32) * spread
    if len(split) > 0:
        drawn = shard_levels(stream_key, extent, split, -0.22, 0.18) * drawn
    return jnp.clip(drawn, min=-most, max=most).astype(held_as)


def setup_inputs(seed: int = 0) -> dict:
    keys = jax.random.split(jax.random.key(seed), 21)
    return {
        "inputs": bell_draw(keys[0], (ROWS, LEN, D), 1.0, 6.0, ((0, 8), (1, 4))),
        "cotangent": bell_draw(keys[1], (ROWS, LEN, D), 1.0, 6.0, ((0, 8), (1, 4))),
        "segments": jax.vmap(lambda own: jnp.searchsorted(jnp.cumsum(uneven_parts(own, SEGS, LEN, SEG_MOST, 1)), jnp.arange(LEN), side="right"))(jax.random.split(keys[2], ROWS)).reshape((ROWS, LEN)).astype(jnp.int32),
        "feature_matrix": bell_draw(keys[3], (FEATS, HD), 1.0, 6.0),
        "w_qkv": bell_draw(keys[4], (D, 3, D), D ** -0.5, 0.25, ((0, 32),), jnp.float32),
        "w_out": bell_draw(keys[5], (D, D), (D // 16) ** -0.5, 1.0, ((0, 32),), jnp.float32),
        "w_up": bell_draw(keys[6], (D, FF), D ** -0.5, 0.25, ((0, 32),), jnp.float32),
        "w_down": bell_draw(keys[7], (FF, D), FF ** -0.5, 0.125, ((0, 32),), jnp.float32),
        "gains": draw_gains(jax.random.fold_in(keys[20], 71), 0),
        "first_qkv": bell_draw(keys[9], (D, 3, D), (0.028 / (D * FF) ** 0.5), 0.0004272461, ((0, 32),), jnp.float32),
        "second_qkv": jnp.clip(jnp.exp(math.log(4.768371808516747e-10) - 2.7725887 * jax.random.uniform(keys[10], (D, 3, D), jnp.float32) ** shard_levels(keys[10], (D, 3, D), ((0, 32),), -0.2, 0.2)), 2.980232380322967e-11, 4.768371808516747e-10),
        "first_out": bell_draw(keys[11], (D, D), (0.014 / (D * FF) ** 0.5), 0.00021362305, ((0, 32),), jnp.float32),
        "second_out": jnp.clip(jnp.exp(math.log(1.220703121918021e-10) - 2.7725887 * jax.random.uniform(keys[12], (D, D), jnp.float32) ** shard_levels(keys[12], (D, D), ((0, 32),), -0.2, 0.2)), 7.62939451198763e-12, 1.220703121918021e-10),
        "first_up": bell_draw(keys[13], (D, FF), (0.014 / (D * FF) ** 0.5), 0.00021362305, ((0, 32),), jnp.float32),
        "second_up": jnp.clip(jnp.exp(math.log(1.220703121918021e-10) - 2.7725887 * jax.random.uniform(keys[14], (D, FF), jnp.float32) ** shard_levels(keys[14], (D, FF), ((0, 32),), -0.2, 0.2)), 7.62939451198763e-12, 1.220703121918021e-10),
        "first_down": bell_draw(keys[15], (FF, D), (0.022 / (D * FF) ** 0.5), 0.00030517578, ((0, 32),), jnp.float32),
        "second_down": jnp.clip(jnp.exp(math.log(3.051757735406113e-10) - 2.7725887 * jax.random.uniform(keys[16], (FF, D), jnp.float32) ** shard_levels(keys[16], (FF, D), ((0, 32),), -0.2, 0.2)), 1.9073485846288207e-11, 3.051757735406113e-10),
        "first_gains": bell_draw(keys[17], (D, 2), (0.089 / (D * FF) ** 0.5), 0.0012207031, ((0, 32),), jnp.float32),
        "second_gains": jnp.clip(jnp.exp(math.log(4.882812376649781e-09) - 2.7725887 * jax.random.uniform(keys[18], (D, 2), jnp.float32) ** shard_levels(keys[18], (D, 2), ((0, 32),), -0.2, 0.2)), 3.051757735406113e-10, 4.882812376649781e-09),
        "step_count": jax.random.randint(keys[19], (), 1, 21).astype(jnp.int32),
    }


@jax.custom_vjp
def low(v):
    return lax.optimization_barrier(v.astype(jnp.bfloat16)).astype(jnp.float32)

@jax.custom_vjp
def low_back(v):
    return v

def low_keep(v):
    return (low(v), None)

def low_pass(kept, grad):
    return (grad,)

def back_keep(v):
    return (v, None)

def back_low(kept, grad):
    return (low(grad),)
low.defvjp(low_keep, low_pass)
low_back.defvjp(back_keep, back_low)
finest_matmul_accuracy = lax.Precision.HIGHEST
norm_eps = 1e-06
beta_first = 0.9
beta_second = 0.999
adam_eps = 1e-08
max_norm = 1.0
matrix_rate = 0.08
output_rate = 0.3
gain_rate = 1.5
matrix_decay = 0.1

def rms_scale(values):
    return lax.rsqrt(lax.optimization_barrier(jnp.mean(values * values, axis=-1, keepdims=True)) + norm_eps)

def feature_map(projected, feature_matrix):
    feature_scale = HD ** (-0.25)
    logits = low_back(jnp.einsum('lhd,md->lhm', projected, feature_matrix, precision=finest_matmul_accuracy) * feature_scale)
    squares = 0.5 * feature_scale * feature_scale * lax.optimization_barrier(jnp.sum(projected * projected, axis=-1, keepdims=True))
    features = jnp.exp(logits - squares) / jnp.sqrt(jnp.float32(FEATS))
    return low(low_back(features))

def focus_single_line(phi_query, phi_key, values, segments):
    length = segments.shape[0]
    block_count = length // BLOCK
    query_blocks = phi_query.reshape(block_count, BLOCK, HEADS, FEATS)
    key_blocks = phi_key.reshape(block_count, BLOCK, HEADS, FEATS)
    value_blocks = values.reshape(block_count, BLOCK, HEADS, HD)
    segment_blocks = segments.reshape(block_count, BLOCK)
    position = jnp.arange(BLOCK, dtype=jnp.int32)
    causal = position[:, None] >= position[None, :]

    def one_block(carried, inputs):
        state_matrix, state_sum, previous = carried
        asking_slice, key_portion, value_portion, segment_part = inputs
        raw_scores = jnp.einsum('qhm,khm->hqk', asking_slice, key_portion, precision=finest_matmul_accuracy)
        same_segment = causal & (segment_part[:, None] == segment_part[None, :])
        scores = low(low_back(raw_scores)) * same_segment.astype(jnp.float32)[None]
        following_marker_mask = (segment_part == previous).astype(jnp.float32)
        memory_matrix_narrow = low(state_matrix)
        upper_accrued_whole = jnp.einsum('hqk,khd->qhd', scores, value_portion, precision=finest_matmul_accuracy)
        upper_accrued_whole = upper_accrued_whole + following_marker_mask[:, None, None] * jnp.einsum('ewx,wxt->ewt', asking_slice, memory_matrix_narrow, precision=finest_matmul_accuracy)
        denominator = lax.optimization_barrier(jnp.sum(scores, axis=-1)).T + following_marker_mask[:, None] * jnp.einsum('qhm,hm->qh', asking_slice, state_sum, precision=finest_matmul_accuracy)
        upper_accrued_whole = low_back(upper_accrued_whole)
        result = upper_accrued_whole / denominator[:, :, None]
        last_segment = segment_part[BLOCK - 1]
        carry_on = (last_segment == previous).astype(jnp.float32)
        chosen = (segment_part == last_segment).astype(jnp.float32)[:, None, None]
        weighted_values = key_portion * chosen
        appended_sum = low_back(jnp.einsum('gqx,gqr->qxr', weighted_values, value_portion, precision=finest_matmul_accuracy))
        next_matrix = carry_on * state_matrix + appended_sum
        next_sum = carry_on * state_sum + lax.optimization_barrier(jnp.sum(weighted_values, axis=0))
        return ((next_matrix, next_sum, last_segment), low(result))
    initial = (jnp.zeros((HEADS, FEATS, HD), jnp.float32), jnp.zeros((HEADS, FEATS), jnp.float32), jnp.int32(-1))
    finals, outputs = lax.scan(jax.checkpoint(one_block), initial, (query_blocks, key_blocks, value_blocks, segment_blocks))
    return outputs.reshape(length, HEADS * HD)

def layer(inputs, w_qkv, w_out, w_up, w_down, gains, segments, feature_matrix):
    length = inputs.shape[0]
    gains_low = low(gains)
    normed_first = inputs * rms_scale(inputs)
    hidden_first = low(normed_first * gains_low[:, 0])
    projected = jnp.einsum('ld,dcf->lcf', hidden_first, low(w_qkv), precision=finest_matmul_accuracy)
    projected = low(low_back(projected))
    query_proj = projected[:, 0].reshape(length, HEADS, HD)
    key_proj = projected[:, 1].reshape(length, HEADS, HD)
    value_proj = projected[:, 2].reshape(length, HEADS, HD)
    phi_query = feature_map(query_proj, feature_matrix)
    phi_key = feature_map(key_proj, feature_matrix)
    attended = focus_single_line(phi_query, phi_key, value_proj, segments)
    branch = low_back(jnp.einsum('lf,ef->le', attended, low(w_out), precision=finest_matmul_accuracy))
    middle = inputs + branch
    hidden_second = low(middle * rms_scale(middle) * gains_low[:, 1])
    upward = low_back(jnp.dot(hidden_second, low(w_up), precision=finest_matmul_accuracy))
    activated = low(jax.nn.gelu(upward, approximate=False))
    return middle + jnp.dot(activated, low(w_down), precision=finest_matmul_accuracy)

def adam_update(weight, gradient, first_moment, second_moment, clip_factor, step_value, step_rate, decay_rate):
    clipped = gradient * clip_factor
    next_first = beta_first * first_moment + (1.0 - beta_first) * clipped
    next_second = beta_second * second_moment + (1.0 - beta_second) * clipped * clipped
    first_hat = next_first / (1.0 - beta_first ** step_value)
    second_hat = next_second / (1.0 - beta_second ** step_value)
    updated = weight - step_rate * (first_hat / (jnp.sqrt(second_hat) + adam_eps) + decay_rate * weight)
    return (clipped, next_first, next_second, updated)

def reference(inputs, cotangent, segments, feature_matrix, w_qkv, w_out, w_up, w_down, gains, first_qkv, second_qkv, first_out, second_out, first_up, second_up, first_down, second_down, first_gains, second_gains, step_count):
    matrix_values = feature_matrix.astype(jnp.float32)
    weights = (w_qkv, w_out, w_up, w_down, gains)

    def one_row(totals, row_inputs):
        row_values, row_cotangent, row_segments = row_inputs

        def forward(values, *weights_now):
            return layer(values, *weights_now, row_segments, matrix_values)
        output, pullback = jax.vjp(forward, row_values.astype(jnp.float32), *weights)
        gradients = pullback(row_cotangent.astype(jnp.float32))
        totals = tuple((total + gradient for total, gradient in zip(totals, gradients[1:])))
        return (totals, (output.astype(jnp.bfloat16), gradients[0]))
    zero_grads = tuple((jnp.zeros_like(weight) for weight in weights))
    totals, (out_act, input_grad) = lax.scan(one_row, zero_grads, (inputs, cotangent, segments))
    total_squares = jnp.float32(0.0)
    for gradient in totals:
        total_squares = total_squares + jnp.sum(gradient * gradient)
    grad_norm = jnp.sqrt(total_squares)
    clip_factor = jnp.minimum(1.0, max_norm / (grad_norm + 1e-06))
    step_value = step_count.astype(jnp.float32)
    qkv_parts = adam_update(w_qkv, totals[0], first_qkv, second_qkv, clip_factor, step_value, matrix_rate, matrix_decay)
    out_parts = adam_update(w_out, totals[1], first_out, second_out, clip_factor, step_value, output_rate, matrix_decay)
    up_parts = adam_update(w_up, totals[2], first_up, second_up, clip_factor, step_value, matrix_rate, matrix_decay)
    down_parts = adam_update(w_down, totals[3], first_down, second_down, clip_factor, step_value, matrix_rate, matrix_decay)
    gain_parts = adam_update(gains, totals[4], first_gains, second_gains, clip_factor, step_value, gain_rate, 0.0)
    return (out_act, input_grad, grad_norm, qkv_parts[0], qkv_parts[1], qkv_parts[2], qkv_parts[3], out_parts[0], out_parts[1], out_parts[2], out_parts[3], up_parts[0], up_parts[1], up_parts[2], up_parts[3], down_parts[0], down_parts[1], down_parts[2], down_parts[3], gain_parts[0], gain_parts[1], gain_parts[2], gain_parts[3])
```

```python
import math
from functools import partial

import jax
import jax.numpy as jnp
from jax import lax
from jax.experimental import pallas as pl
from jax.experimental.pallas import tpu as pltpu
from jax.sharding import PartitionSpec as P

D = 512
HD = 64
FEATS = 256
FF = 2048
CHUNK = 256
SPAN = 1024
ROWS = 512
PAIRS = D // (2 * HD)

bf16 = jnp.bfloat16
f32 = jnp.float32
norm_eps = 1e-06
beta_first = 0.9
beta_second = 0.999
adam_eps = 1e-08
max_norm = 1.0
matrix_rate = 0.08
output_rate = 0.3
gain_rate = 1.5
matrix_decay = 0.1
feature_scale = HD ** (-0.25)
log2e = math.log2(math.e)
AXES = ("head", "row")


def dot(a, b, ca=1, cb=0):
    return lax.dot_general(a, b, (((ca,), (cb,)), ((), ())), preferred_element_type=f32)


def lanes(width):
    return lax.broadcasted_iota(jnp.int32, (1, width), 1)


def half_masks(width):
    first = (lanes(width) % 128 < HD).astype(f32)
    return first.astype(bf16), (1.0 - first).astype(bf16)


def rms_scale(values):
    return lax.rsqrt(jnp.mean(values * values, axis=-1, keepdims=True) + norm_eps)


def features(u, spread):
    raw = dot(u, spread)
    wide = u.astype(f32)
    squares = wide * wide
    own = lanes(2 * HD) < HD
    total_a = jnp.sum(jnp.where(own, squares, 0.0), axis=1, keepdims=True)
    total_b = jnp.sum(jnp.where(own, 0.0, squares), axis=1, keepdims=True)
    c1 = feature_scale * log2e
    c2 = 0.5 * feature_scale * feature_scale * log2e
    down_a = total_a * c2 + 4.0
    down_b = total_b * c2 + 4.0
    left = jnp.exp2(raw[:, :FEATS] * c1 - down_a)
    right = jnp.exp2(raw[:, FEATS:] * c1 - down_b)
    return jnp.concatenate([left, right], axis=1).astype(bf16)


def masked_pair(first, second, width):
    ma, mb = half_masks(width)
    return jnp.concatenate([first * ma, second * mb], axis=0)


def forward_kernel(
    before_ref, last_ref, xh_ref, xo_ref, segc_ref, segr_ref, wq_ref, gain_ref, spread_ref,
    h1_ref, qkv_ref, pq_ref, pk_ref, p_ref, t_ref, o_ref, of_ref, rden_ref,
    state_ref,
):
    step = pl.program_id(0)
    halo = SPAN // CHUNK
    before = before_ref[step]
    last = last_ref[step]
    ones = jnp.ones((CHUNK, 2 * HD), bf16)

    @pl.when(step == 0)
    def _():
        state_ref[...] = jnp.zeros_like(state_ref)

    @pl.when(step < halo)
    def _():
        x = xh_ref[...].astype(f32)
        h1 = (x * rms_scale(x) * gain_ref[...]).astype(bf16)
        kv = dot(h1, wq_ref[:, D:]).astype(bf16)
        chosen = (segc_ref[...] == last).astype(f32).astype(bf16)
        for p in range(PAIRS):
            k2 = kv[:, 128 * p : 128 * (p + 1)]
            v2 = kv[:, D + 128 * p : D + 128 * (p + 1)]
            pk = features(k2, spread_ref[...])
            vw = jnp.concatenate([v2, ones], axis=1) * chosen
            state_ref[p] = state_ref[p] + dot(pk, vw, 0, 0)

    @pl.when(step >= halo)
    def _():
        x = xo_ref[...].astype(f32)
        h1 = (x * rms_scale(x) * gain_ref[...]).astype(bf16)
        h1_ref[...] = h1
        qkv = dot(h1, wq_ref[...]).astype(bf16)
        qkv_ref[...] = qkv
        segc = segc_ref[...]
        segr = segr_ref[0]
        chosen = (segc == last).astype(f32).astype(bf16)
        follows = (segc == before).astype(f32).astype(bf16)
        keep = (last == before).astype(f32)
        rows = lax.broadcasted_iota(jnp.int32, (CHUNK, CHUNK), 0)
        cols = lax.broadcasted_iota(jnp.int32, (CHUNK, CHUNK), 1)
        allowed = ((rows >= cols) & (segc == segr)).astype(f32).astype(bf16)
        for p in range(PAIRS):
            cut = slice(128 * p, 128 * (p + 1))
            wide = slice(512 * p, 512 * (p + 1))
            q2 = qkv[:, 128 * p : 128 * (p + 1)]
            k2 = qkv[:, D + 128 * p : D + 128 * (p + 1)]
            v2 = qkv[:, 2 * D + 128 * p : 2 * D + 128 * (p + 1)]
            pq = features(q2, spread_ref[...])
            pk = features(k2, spread_ref[...])
            pq_ref[:, wide] = pq
            pk_ref[:, wide] = pk
            scores = jnp.concatenate(
                [
                    dot(pq[:, :FEATS], pk[:, :FEATS], 1, 1).astype(bf16) * allowed,
                    dot(pq[:, FEATS:], pk[:, FEATS:], 1, 1).astype(bf16) * allowed,
                ],
                axis=1,
            )
            p_ref[:, wide] = scores
            v1 = jnp.concatenate([v2, ones], axis=1)
            state = state_ref[p]
            narrow = state.astype(bf16)
            narrow = masked_pair(narrow[:FEATS], narrow[FEATS:], 256)
            t_ref[0, p] = narrow
            both = dot(scores, masked_pair(v1, v1, 256)) + dot(pq * follows, narrow)
            rden = 1.0 / both[:, 128:]
            of = both[:, :128] * rden
            rden_ref[:, cut] = rden
            of_ref[:, cut] = of
            o_ref[:, cut] = of.astype(bf16)
            state_ref[p] = keep * state + dot(pk, v1 * chosen, 0, 0)


def middle_kernel(
    before_ref, x_ref, g_ref, o_ref, of_ref, rden_ref, pq_ref, segc_ref, wo_ref, wu_ref, wd_ref,
    gain_ref,
    out_ref, dy1_ref, dn_ref, gup_ref, gdown_ref, gout_ref, gg_ref, back_ref,
    up_acc, down_acc, out_acc, gg_acc, back_acc, act_ref, dup_ref,
):
    step = pl.program_id(0)
    steps = pl.num_programs(0)

    @pl.when(step == 0)
    def _():
        up_acc[...] = jnp.zeros_like(up_acc)
        down_acc[...] = jnp.zeros_like(down_acc)
        out_acc[...] = jnp.zeros_like(out_acc)
        gg_acc[...] = jnp.zeros_like(gg_acc)
        back_acc[...] = jnp.zeros_like(back_acc)

    o = o_ref[...]
    g = g_ref[...]
    gain = gain_ref[...]
    y1 = x_ref[...].astype(f32) + dot(o, wo_ref[...], 1, 1)
    r2 = rms_scale(y1)
    n2 = y1 * r2
    h2 = (n2 * gain).astype(bf16)
    cut = 512
    for f in range(FF // cut):
        fs = slice(cut * f, cut * (f + 1))
        up = dot(h2, wu_ref[:, fs])
        d_act = dot(g, wd_ref[fs, :], 1, 1)
        cdf = 0.5 * (1.0 + lax.erf(up * math.sqrt(0.5)))
        density = jnp.exp(up * up * -0.5) * (1.0 / math.sqrt(2.0 * math.pi))
        act = (up * cdf).astype(bf16)
        d_up = (d_act * (cdf + up * density)).astype(bf16)
        act_ref[:, fs] = act
        dup_ref[:, fs] = d_up
        down_acc[fs, :] += dot(act, g, 0, 0)
        up_acc[:, fs] += dot(h2, d_up, 0, 0)
    out_ref[...] = (y1 + dot(act_ref[...], wd_ref[...])).astype(bf16)
    d_h2 = dot(dup_ref[...], wu_ref[...], 1, 1)
    gg_acc[...] += jnp.sum(d_h2 * n2, axis=0, keepdims=True)
    e2 = d_h2 * gain
    dy1 = g.astype(f32) + r2 * (e2 - n2 * jnp.mean(e2 * n2, axis=-1, keepdims=True))
    dy1_ref[...] = dy1
    da = dy1.astype(bf16)
    out_acc[...] += dot(da, o, 0, 0)
    d_o = dot(da, wo_ref[...])
    product = d_o * of_ref[...]
    high = product.astype(bf16)
    low = (product - high.astype(f32)).astype(bf16)
    rden = rden_ref[...]
    ma, mb = half_masks(128)
    same = jnp.concatenate(
        [jnp.broadcast_to(ma, (HD, 128)), jnp.broadcast_to(mb, (HD, 128))], axis=0
    )
    same = jnp.concatenate([same, same], axis=0)
    lane = lanes(128) % HD
    m0 = (lane == 0).astype(f32).astype(bf16)
    m1 = (lane == 1).astype(f32).astype(bf16)
    parts = []
    for p in range(PAIRS):
        ps = slice(128 * p, 128 * (p + 1))
        total = dot(jnp.concatenate([high[:, ps], low[:, ps]], axis=1), same)
        d_den = -total * rden[:, ps]
        d_hi = d_den.astype(bf16)
        d_lo = (d_den - d_hi.astype(f32)).astype(bf16)
        d_num = (d_o[:, ps] * rden[:, ps]).astype(bf16)
        dn = jnp.concatenate([d_num, d_hi * m0 + d_lo * m1], axis=1)
        dn_ref[:, 256 * p : 256 * (p + 1)] = dn
        parts.append(dn)

    @pl.when(step < SPAN // ROWS)
    def _():
        follows = (segc_ref[...] == before_ref[0]).astype(f32).astype(bf16)
        for p in range(PAIRS):
            back_acc[p] = back_acc[p] + dot(
                pq_ref[:, 512 * p : 512 * (p + 1)], dn_ref[:, 256 * p : 256 * (p + 1)] * follows, 0, 0
            )

    @pl.when(step == steps - 1)
    def _():
        gup_ref[...] = up_acc[...].astype(bf16)
        gdown_ref[...] = down_acc[...].astype(bf16)
        gout_ref[...] = out_acc[...].astype(bf16)
        gg_ref[...] = gg_acc[...]
        for p in range(PAIRS):
            back = back_acc[p].astype(bf16)
            back_ref[p] = masked_pair(back[:FEATS], back[FEATS:], 256)


def backward_kernel(
    before_ref, last_ref, p_ref, pq_ref, pk_ref, qkv_ref, dn_ref, t_ref, segc_ref, segr_ref,
    back_ref, gather_ref,
    dqkv_ref,
    state_ref,
):
    step = pl.program_id(0)
    chunk = pl.num_programs(0) - 1 - step
    before = before_ref[chunk]
    last = last_ref[chunk]

    @pl.when(step == 0)
    def _():
        state_ref[...] = back_ref[...].astype(f32)

    segc = segc_ref[...]
    segr = segr_ref[0]
    chosen = (segc == last).astype(f32).astype(bf16)
    follows = (segc == before).astype(f32).astype(bf16)
    keep = (last == before).astype(f32)
    rows = lax.broadcasted_iota(jnp.int32, (CHUNK, CHUNK), 0)
    cols = lax.broadcasted_iota(jnp.int32, (CHUNK, CHUNK), 1)
    allowed = ((rows >= cols) & (segc == segr)).astype(f32).astype(bf16)
    lane = lanes(128) % HD
    two = jnp.broadcast_to((lane < 2).astype(f32).astype(bf16), (CHUNK, 128))
    ones = jnp.ones((CHUNK, 128), bf16)
    ma, mb = half_masks(128)
    for p in range(PAIRS):
        wide = slice(512 * p, 512 * (p + 1))
        q2 = qkv_ref[:, 128 * p : 128 * (p + 1)]
        k2 = qkv_ref[:, D + 128 * p : D + 128 * (p + 1)]
        v2 = qkv_ref[:, 2 * D + 128 * p : 2 * D + 128 * (p + 1)]
        pq = pq_ref[:, wide]
        pk = pk_ref[:, wide]
        dn = dn_ref[:, 256 * p : 256 * (p + 1)]
        scores = p_ref[:, wide]
        narrow = t_ref[0, p]
        state = state_ref[p]
        back = state.astype(bf16)
        back = masked_pair(back[:FEATS], back[FEATS:], 256)
        v1 = jnp.concatenate([v2, two], axis=1)
        d_p = dot(dn, masked_pair(v1, v1, 256), 1, 1).astype(bf16)
        d_pa = d_p[:, :CHUNK] * allowed
        d_pb = d_p[:, CHUNK:] * allowed
        dn_f = dn * follows
        d_pq = dot(dn_f, narrow, 1, 1) + jnp.concatenate(
            [dot(d_pa, pk[:, :FEATS]), dot(d_pb, pk[:, FEATS:])], axis=1
        )
        vw = jnp.concatenate([v2, ones], axis=1) * chosen
        d_pk = dot(vw, back, 1, 1) + jnp.concatenate(
            [dot(d_pa, pq[:, :FEATS], 0, 0), dot(d_pb, pq[:, FEATS:], 0, 0)], axis=1
        )
        d_num = dn[:, :128]
        d_v = (
            dot(pk * chosen, back[:, :128])
            + dot(scores[:, :CHUNK], d_num * ma, 0, 0)
            + dot(scores[:, CHUNK:], d_num * mb, 0, 0)
        )
        through_q = dot(d_pq.astype(bf16) * pq, gather_ref[...])
        through_k = dot(d_pk.astype(bf16) * pk, gather_ref[...])
        scale2 = feature_scale * feature_scale
        d_q = through_q[:, :128] * feature_scale - q2.astype(f32) * through_q[:, 128:] * scale2
        d_k = through_k[:, :128] * feature_scale - k2.astype(f32) * through_k[:, 128:] * scale2
        dqkv_ref[:, 128 * p : 128 * (p + 1)] = d_q.astype(bf16)
        dqkv_ref[:, D + 128 * p : D + 128 * (p + 1)] = d_k.astype(bf16)
        dqkv_ref[:, 2 * D + 128 * p : 2 * D + 128 * (p + 1)] = d_v.astype(bf16)
        state_ref[p] = keep * state + dot(pq, dn_f, 0, 0)


def input_kernel(dqkv_ref, wq_ref, x_ref, dy1_ref, gain_ref, dx_ref, gg_ref, gg_acc):
    step = pl.program_id(0)

    @pl.when(step == 0)
    def _():
        gg_acc[...] = jnp.zeros_like(gg_acc)

    d_h1 = dot(dqkv_ref[...], wq_ref[...], 1, 1)
    x = x_ref[...].astype(f32)
    r1 = rms_scale(x)
    n1 = x * r1
    gg_acc[...] += jnp.sum(d_h1 * n1, axis=0, keepdims=True)
    e1 = d_h1 * gain_ref[...]
    dx_ref[...] = dy1_ref[...] + r1 * (e1 - n1 * jnp.mean(e1 * n1, axis=-1, keepdims=True))

    @pl.when(step == pl.num_programs(0) - 1)
    def _():
        gg_ref[...] = gg_acc[...]


def axis_bits():
    row_bits = (lax.axis_size("row") - 1).bit_length()
    head_bits = (lax.axis_size("head") - 1).bit_length()
    row = [("row", b, b) for b in range(row_bits)]
    head = [("head", b, row_bits + b) for b in range(head_bits)]
    return row, head


def swap(value, axis, bit):
    size = lax.axis_size(axis)
    return lax.ppermute(value, axis, [(i, i ^ (1 << bit)) for i in range(size)])


def gather_all(shard, order):
    held = []
    buf = shard
    for axis, bit, place in order:
        mine = (lax.axis_index(axis) >> bit) & 1
        other = swap(buf, axis, bit)
        at = sum(1 for h in held if h > place)
        buf = jnp.where(
            mine == 0, jnp.stack([buf, other], axis=at), jnp.stack([other, buf], axis=at)
        )
        held = sorted(held + [place], reverse=True)
    return buf.reshape((-1,) + shard.shape[1:])


def scatter_sum(whole, order):
    places = sorted([place for _, _, place in order], reverse=True)
    count = 1 << len(places)
    buf = whole.reshape((2,) * len(places) + (whole.shape[0] // count,) + whole.shape[1:])
    for axis, bit, place in order:
        at = places.index(place)
        places.remove(place)
        mine = (lax.axis_index(axis) >> bit) & 1
        low = lax.index_in_dim(buf, 0, at, keepdims=False)
        high = lax.index_in_dim(buf, 1, at, keepdims=False)
        send = jnp.where(mine == 0, high, low).astype(bf16)
        kept = jnp.where(mine == 0, low, high)
        buf = kept.astype(f32) + swap(send, axis, bit).astype(f32)
        if places:
            buf = buf.astype(bf16)
    return buf


def tree_sum(value):
    row, head = axis_bits()
    for axis, bit, _ in head + row:
        value = value + swap(value, axis, bit)
    return value


def adam_update(
    weight, gradient, first_moment, second_moment, clip_factor, step_value, step_rate, decay_rate
):
    clipped = gradient * clip_factor
    next_first = beta_first * first_moment + (1.0 - beta_first) * clipped
    next_second = beta_second * second_moment + (1.0 - beta_second) * clipped * clipped
    first_hat = next_first / (1.0 - beta_first**step_value)
    second_hat = next_second / (1.0 - beta_second**step_value)
    updated = weight - step_rate * (
        first_hat / (jnp.sqrt(second_hat) + adam_eps) + decay_rate * weight
    )
    return (clipped, next_first, next_second, updated)


def params(limit=60):
    return pltpu.CompilerParams(
        dimension_semantics=("arbitrary",), vmem_limit_bytes=limit << 20
    )


def fixed(shape):
    zeros = (0,) * len(shape)
    return pl.BlockSpec(shape, lambda *_: zeros, pipeline_mode=pl.Buffered(1))


def per_device(
    inputs,
    cotangent,
    segments,
    feature_matrix,
    w_qkv,
    w_out,
    w_up,
    w_down,
    gains,
    first_qkv,
    second_qkv,
    first_out,
    second_out,
    first_up,
    second_up,
    first_down,
    second_down,
    first_gains,
    second_gains,
    step_count,
):
    heads = lax.axis_size("head")
    row_bits, head_bits = axis_bits()
    x = inputs[0]
    g = cotangent[0]
    length = x.shape[0]
    chunks = length // CHUNK
    halo = SPAN // CHUNK

    share = w_qkv.shape[0]
    packed = jnp.concatenate(
        [
            w_qkv.reshape(share, 3 * D).astype(bf16),
            jnp.pad(gains.astype(bf16), ((0, 0), (0, 126))),
        ],
        axis=1,
    )
    forward_pairs = [(i, i + 1) for i in range(heads - 1)]
    backward_pairs = [(i + 1, i) for i in range(heads - 1)]
    x_ahead = lax.ppermute(x[length - SPAN :], "head", forward_pairs)
    order_a = row_bits[::-1] + head_bits[::-1]
    packed_full = gather_all(packed, order_a)
    wq = packed_full[:, : 3 * D]
    gain_first = packed_full[:, 3 * D].astype(f32).reshape(1, D)
    gain_second = packed_full[:, 3 * D + 1].astype(f32).reshape(1, D)
    w_out_full = gather_all(w_out.astype(bf16), order_a)
    w_up_full = gather_all(w_up.astype(bf16), order_a)
    w_down_full = gather_all(w_down.astype(bf16), order_a)

    row_segments = segments[0]
    padded = jnp.concatenate([jnp.full((SPAN,), -1, jnp.int32), row_segments])
    near = lax.dynamic_slice_in_dim(padded, lax.axis_index("head") * length, length + SPAN)
    seg_cols = near.reshape(-1, 1)
    seg_rows = near.reshape(-1, 1, CHUNK)
    ends = near[CHUNK - 1 :: CHUNK]
    own_before = ends[halo - 1 : -1]
    own_last = ends[halo:]
    ahead_last = jnp.full((halo,), 1, jnp.int32) * ends[halo - 1]
    all_before = jnp.concatenate([ahead_last, own_before])
    all_last = jnp.concatenate([ahead_last, own_last])
    own_cols = seg_cols[SPAN:]
    own_rows = seg_rows[halo:]

    fm = feature_matrix
    nothing = jnp.zeros_like(fm.T)
    spread = jnp.concatenate(
        [
            jnp.concatenate([fm.T, nothing], axis=1),
            jnp.concatenate([nothing, fm.T], axis=1),
        ],
        axis=0,
    )
    zero = jnp.zeros((FEATS, HD), bf16)
    one = jnp.ones((FEATS, HD), bf16)
    gather = jnp.concatenate(
        [
            jnp.concatenate([fm, zero, one, zero], axis=1),
            jnp.concatenate([zero, fm, zero, one], axis=1),
        ],
        axis=0,
    )

    def own(shape):
        rest = (0,) * (len(shape) - 1)
        return pl.BlockSpec(shape, lambda c, *_: (jnp.maximum(c - halo, 0),) + rest)

    wide = PAIRS * 2 * FEATS
    h1, qkv, pq, pk, scores, states, o, of, rden = pl.pallas_call(
        forward_kernel,
        grid_spec=pltpu.PrefetchScalarGridSpec(
            num_scalar_prefetch=2,
            grid=(halo + chunks,),
            in_specs=[
                pl.BlockSpec((CHUNK, D), lambda c, *_: (jnp.minimum(c, halo - 1), 0)),
                own((CHUNK, D)),
                pl.BlockSpec((CHUNK, 1), lambda c, *_: (c, 0)),
                pl.BlockSpec((1, 1, CHUNK), lambda c, *_: (c, 0, 0)),
                fixed((D, 3 * D)),
                fixed((1, D)),
                fixed((2 * HD, 2 * FEATS)),
            ],
            out_specs=[
                own((CHUNK, D)),
                own((CHUNK, 3 * D)),
                own((CHUNK, wide)),
                own((CHUNK, wide)),
                own((CHUNK, wide)),
                own((1, PAIRS, 2 * FEATS, 256)),
                own((CHUNK, D)),
                own((CHUNK, D)),
                own((CHUNK, D)),
            ],
            scratch_shapes=[pltpu.VMEM((PAIRS, 2 * FEATS, 256), f32)],
        ),
        out_shape=[
            jax.ShapeDtypeStruct((length, D), bf16),
            jax.ShapeDtypeStruct((length, 3 * D), bf16),
            jax.ShapeDtypeStruct((length, wide), bf16),
            jax.ShapeDtypeStruct((length, wide), bf16),
            jax.ShapeDtypeStruct((length, wide), bf16),
            jax.ShapeDtypeStruct((chunks, PAIRS, 2 * FEATS, 256), bf16),
            jax.ShapeDtypeStruct((length, D), bf16),
            jax.ShapeDtypeStruct((length, D), f32),
            jax.ShapeDtypeStruct((length, D), f32),
        ],
        compiler_params=params(),
        name="forward",
    )(all_before, all_last, x_ahead, x, seg_cols, seg_rows, wq, gain_first, spread)

    def by_step(shape):
        rest = (0,) * (len(shape) - 1)
        return pl.BlockSpec(shape, lambda c, *_: (c,) + rest)

    near_steps = SPAN // ROWS
    out_act, dy1, dn, g_up, g_down, g_out, gg_second, back = pl.pallas_call(
        middle_kernel,
        grid_spec=pltpu.PrefetchScalarGridSpec(
            num_scalar_prefetch=1,
            grid=(length // ROWS,),
            in_specs=[
                by_step((ROWS, D)),
                by_step((ROWS, D)),
                by_step((ROWS, D)),
                by_step((ROWS, D)),
                by_step((ROWS, D)),
                pl.BlockSpec((ROWS, wide), lambda c, *_: (jnp.minimum(c, near_steps - 1), 0)),
                by_step((ROWS, 1)),
                fixed((D, D)),
                fixed((D, FF)),
                fixed((FF, D)),
                fixed((1, D)),
            ],
            out_specs=[
                by_step((ROWS, D)),
                by_step((ROWS, D)),
                by_step((ROWS, PAIRS * 256)),
                fixed((D, FF)),
                fixed((FF, D)),
                fixed((D, D)),
                fixed((1, D)),
                fixed((PAIRS, 2 * FEATS, 256)),
            ],
            scratch_shapes=[
                pltpu.VMEM((D, FF), f32),
                pltpu.VMEM((FF, D), f32),
                pltpu.VMEM((D, D), f32),
                pltpu.VMEM((1, D), f32),
                pltpu.VMEM((PAIRS, 2 * FEATS, 256), f32),
                pltpu.VMEM((ROWS, FF), bf16),
                pltpu.VMEM((ROWS, FF), bf16),
            ],
        ),
        out_shape=[
            jax.ShapeDtypeStruct((length, D), bf16),
            jax.ShapeDtypeStruct((length, D), f32),
            jax.ShapeDtypeStruct((length, PAIRS * 256), bf16),
            jax.ShapeDtypeStruct((D, FF), bf16),
            jax.ShapeDtypeStruct((FF, D), bf16),
            jax.ShapeDtypeStruct((D, D), bf16),
            jax.ShapeDtypeStruct((1, D), f32),
            jax.ShapeDtypeStruct((PAIRS, 2 * FEATS, 256), bf16),
        ],
        compiler_params=params(),
        name="middle",
    )(own_before, x, g, o, of, rden, pq, own_cols, w_out_full, w_up_full, w_down_full, gain_second)

    back_in = lax.ppermute(back, "head", backward_pairs)

    def falling(shape):
        rest = (0,) * (len(shape) - 1)
        return pl.BlockSpec(shape, lambda c, *_: (chunks - 1 - c,) + rest)

    d_qkv = pl.pallas_call(
        backward_kernel,
        grid_spec=pltpu.PrefetchScalarGridSpec(
            num_scalar_prefetch=2,
            grid=(chunks,),
            in_specs=[
                falling((CHUNK, wide)),
                falling((CHUNK, wide)),
                falling((CHUNK, wide)),
                falling((CHUNK, 3 * D)),
                falling((CHUNK, PAIRS * 256)),
                falling((1, PAIRS, 2 * FEATS, 256)),
                falling((CHUNK, 1)),
                falling((1, 1, CHUNK)),
                fixed((PAIRS, 2 * FEATS, 256)),
                fixed((2 * FEATS, 256)),
            ],
            out_specs=falling((CHUNK, 3 * D)),
            scratch_shapes=[pltpu.VMEM((PAIRS, 2 * FEATS, 256), f32)],
        ),
        out_shape=jax.ShapeDtypeStruct((length, 3 * D), bf16),
        compiler_params=params(),
        name="backward",
    )(own_before, own_last, scores, pq, pk, qkv, dn, states, own_cols, own_rows, back_in, gather)

    g_qkv = dot(h1, d_qkv, 0, 0).astype(bf16)

    dx, gg_first = pl.pallas_call(
        input_kernel,
        grid=(length // ROWS,),
        in_specs=[
            by_step((ROWS, 3 * D)),
            fixed((D, 3 * D)),
            by_step((ROWS, D)),
            by_step((ROWS, D)),
            fixed((1, D)),
        ],
        out_specs=[by_step((ROWS, D)), fixed((1, D))],
        out_shape=[
            jax.ShapeDtypeStruct((length, D), f32),
            jax.ShapeDtypeStruct((1, D), f32),
        ],
        scratch_shapes=[pltpu.VMEM((1, D), f32)],
        compiler_params=params(),
        name="input_grad",
    )(d_qkv, wq, x, dy1, gain_first)

    order_g = head_bits[:1] + head_bits[1:] + row_bits
    sum_up = scatter_sum(g_up, order_g)
    sum_down = scatter_sum(g_down, order_g)
    sum_out = scatter_sum(g_out, order_g)
    sum_qkv = scatter_sum(g_qkv, order_g).reshape(share, 3, D)
    gg = tree_sum(jnp.concatenate([gg_first, gg_second], axis=0))
    place = lax.axis_index(AXES) * share
    sum_gains = lax.dynamic_slice_in_dim(gg, place, share, 1).T

    reduced = (sum_qkv, sum_out, sum_up, sum_down, sum_gains)
    local_squares = jnp.float32(0.0)
    for gradient in reduced:
        local_squares = local_squares + jnp.sum(gradient * gradient)
    total_squares = tree_sum(local_squares.reshape(1, 1))[0, 0]
    grad_norm = jnp.sqrt(total_squares)
    clip_factor = jnp.minimum(1.0, max_norm / (grad_norm + 1e-06))
    step_value = step_count.astype(f32)
    update = partial(adam_update, clip_factor=clip_factor, step_value=step_value)
    qkv_parts = update(
        w_qkv, reduced[0], first_qkv, second_qkv, step_rate=matrix_rate, decay_rate=matrix_decay
    )
    out_parts = update(
        w_out, reduced[1], first_out, second_out, step_rate=output_rate, decay_rate=matrix_decay
    )
    up_parts = update(
        w_up, reduced[2], first_up, second_up, step_rate=matrix_rate, decay_rate=matrix_decay
    )
    down_parts = update(
        w_down, reduced[3], first_down, second_down, step_rate=matrix_rate, decay_rate=matrix_decay
    )
    gain_parts = update(
        gains, reduced[4], first_gains, second_gains, step_rate=gain_rate, decay_rate=0.0
    )
    return (
        (out_act[None], dx[None], grad_norm)
        + qkv_parts
        + out_parts
        + up_parts
        + down_parts
        + gain_parts
    )


def solution(mesh):
    token = P("row", "head", None)
    three = P(AXES, None, None)
    two = P(AXES, None)
    placed = (token, token, P("row", None), P(), three, two, two, two, two)
    placed = placed + (three, three) + (two,) * 8 + (P(),)
    return jax.shard_map(
        per_device,
        mesh=mesh,
        in_specs=placed,
        out_specs=(token, token, P()) + (three,) * 4 + (two,) * 16,
        check_vma=False,
    )
```

```python
import math
from functools import partial

import jax
import jax.numpy as jnp
from jax import lax
from jax.experimental import pallas as pl
from jax.experimental.pallas import tpu as pltpu
from jax.sharding import PartitionSpec as P

D = 512
HD = 64
FEATS = 256
FF = 2048
CHUNK = 256
SPAN = 1024
ROWS = 512
PAIRS = D // (2 * HD)

bf16 = jnp.bfloat16
f32 = jnp.float32
norm_eps = 1e-06
beta_first = 0.9
beta_second = 0.999
adam_eps = 1e-08
max_norm = 1.0
matrix_rate = 0.08
output_rate = 0.3
gain_rate = 1.5
matrix_decay = 0.1
feature_scale = HD ** (-0.25)
log2e = math.log2(math.e)
AXES = ("head", "row")


def dot(a, b, ca=1, cb=0):
    return lax.dot_general(a, b, (((ca,), (cb,)), ((), ())), preferred_element_type=f32)


def lanes(width):
    return lax.broadcasted_iota(jnp.int32, (1, width), 1)


def half_masks(width):
    first = (lanes(width) % 128 < HD).astype(f32)
    return first.astype(bf16), (1.0 - first).astype(bf16)


def rms_scale(values):
    return lax.rsqrt(jnp.mean(values * values, axis=-1, keepdims=True) + norm_eps)


def features(u, spread):
    raw = dot(u, spread)
    wide = u.astype(f32)
    squares = wide * wide
    own = lanes(2 * HD) < HD
    total_a = jnp.sum(jnp.where(own, squares, 0.0), axis=1, keepdims=True)
    total_b = jnp.sum(jnp.where(own, 0.0, squares), axis=1, keepdims=True)
    c1 = feature_scale * log2e
    c2 = 0.5 * feature_scale * feature_scale * log2e
    down_a = total_a * c2 + 4.0
    down_b = total_b * c2 + 4.0
    left = jnp.exp2(raw[:, :FEATS] * c1 - down_a)
    right = jnp.exp2(raw[:, FEATS:] * c1 - down_b)
    return jnp.concatenate([left, right], axis=1).astype(bf16)


def masked_pair(first, second, width):
    ma, mb = half_masks(width)
    return jnp.concatenate([first * ma, second * mb], axis=0)


def as_column(row):
    return jnp.broadcast_to(row, (8, row.shape[1])).T[:, :1]


def flag(condition):
    return condition.astype(f32).astype(bf16)


def chunk_mask(seg_row):
    seg_col = as_column(seg_row)
    rows = lax.broadcasted_iota(jnp.int32, (CHUNK, CHUNK), 0)
    cols = lax.broadcasted_iota(jnp.int32, (CHUNK, CHUNK), 1)
    return seg_col, flag((rows >= cols) & (seg_col == seg_row))


def forward_kernel(
    ends_ref, xh_ref, xo_ref, seg_ref, wq_ref, spread_ref,
    h1_ref, qkv_ref, pq_ref, pk_ref, p_ref, t_ref, o_ref, of_ref, rden_ref, gains_ref,
    state_ref,
):
    step = pl.program_id(0)
    halo = SPAN // CHUNK
    ones = jnp.ones((CHUNK, 2 * HD), bf16)

    @pl.when(step == 0)
    def _():
        state_ref[...] = jnp.zeros_like(state_ref)
        gains_ref[...] = wq_ref[:, 3 * D :].astype(f32).T[:8]

    gain = gains_ref[0:1]

    @pl.when(step < halo)
    def _():
        x = xh_ref[...].astype(f32)
        h1 = (x * rms_scale(x) * gain).astype(bf16)
        chosen = flag(as_column(seg_ref[0]) == ends_ref[halo - 1])
        for p in range(PAIRS):
            kv = dot(h1, wq_ref[:, 384 * p + 128 : 384 * (p + 1)]).astype(bf16)
            pk = features(kv[:, :128], spread_ref[...])
            vw = jnp.concatenate([kv[:, 128:], ones], axis=1) * chosen
            state_ref[p] = state_ref[p] + dot(pk, vw, 0, 0)

    @pl.when(step >= halo)
    def _():
        before = ends_ref[step - 1]
        last = ends_ref[step]
        x = xo_ref[...].astype(f32)
        h1 = (x * rms_scale(x) * gain).astype(bf16)
        h1_ref[...] = h1
        qkv = dot(h1, wq_ref[:, : 3 * D]).astype(bf16)
        qkv_ref[...] = qkv
        seg_col, allowed = chunk_mask(seg_ref[0])
        chosen = flag(seg_col == last)
        follows = flag(seg_col == before)
        keep = (last == before).astype(f32)
        for p in range(PAIRS):
            cut = slice(128 * p, 128 * (p + 1))
            wide = slice(512 * p, 512 * (p + 1))
            q2 = qkv[:, 384 * p : 384 * p + 128]
            k2 = qkv[:, 384 * p + 128 : 384 * p + 256]
            v2 = qkv[:, 384 * p + 256 : 384 * p + 384]
            pq = features(q2, spread_ref[...])
            pk = features(k2, spread_ref[...])
            pq_ref[:, wide] = pq
            pk_ref[:, wide] = pk
            scores = jnp.concatenate(
                [
                    dot(pq[:, :FEATS], pk[:, :FEATS], 1, 1).astype(bf16) * allowed,
                    dot(pq[:, FEATS:], pk[:, FEATS:], 1, 1).astype(bf16) * allowed,
                ],
                axis=1,
            )
            p_ref[:, wide] = scores
            v1 = jnp.concatenate([v2, ones], axis=1)
            state = state_ref[p]
            narrow = state.astype(bf16)
            narrow = masked_pair(narrow[:FEATS], narrow[FEATS:], 256)
            t_ref[0, p] = narrow
            both = dot(scores, masked_pair(v1, v1, 256)) + dot(pq * follows, narrow)
            rden = 1.0 / both[:, 128:]
            of = both[:, :128] * rden
            rden_ref[:, cut] = rden
            of_ref[:, cut] = of
            o_ref[:, cut] = of.astype(bf16)
            state_ref[p] = keep * state + dot(pk, v1 * chosen, 0, 0)


def middle_kernel(
    group,
    ends_ref, core_ref, x_ref, g_ref, o_ref, of_ref, rden_ref, pq_ref, seg_ref, gains_ref,
    wu0_ref, wu1_ref, wu2_ref, wu3_ref, wd_ref, wo_ref,
    out_ref, dy1_ref, dn_ref, sent_up_ref, sent_rest_ref, kept_up_ref, kept_rest_ref, back_ref,
    up_acc, down_acc, out_acc, back_acc, act_ref, dup_ref,
):
    step = pl.program_id(0)
    steps = pl.num_programs(0)
    cut = 512
    wu_refs = (wu0_ref, wu1_ref, wu2_ref, wu3_ref)
    blocks = wd_ref.shape[0] // len(wu_refs)

    @pl.when(step == 0)
    def _():
        up_acc[...] = jnp.zeros_like(up_acc)
        down_acc[...] = jnp.zeros_like(down_acc)
        out_acc[...] = jnp.zeros_like(out_acc)
        back_acc[...] = jnp.zeros_like(back_acc)

    o = o_ref[...]
    g = g_ref[...]
    gain = gains_ref[1:2]
    wo = wo_ref[...].reshape(D, D)
    y1 = x_ref[...].astype(f32) + dot(o, wo, 1, 1)
    r2 = rms_scale(y1)
    n2 = y1 * r2
    h2 = (n2 * gain).astype(bf16)
    for f in range(FF // cut):
        fs = slice(cut * f, cut * (f + 1))
        wd = wd_ref[blocks * f : blocks * (f + 1)].reshape(cut, D)
        up = dot(h2, wu_refs[f][...].reshape(D, cut))
        d_act = dot(g, wd, 1, 1)
        cdf = 0.5 * (1.0 + lax.erf(up * math.sqrt(0.5)))
        density = jnp.exp(up * up * -0.5) * (1.0 / math.sqrt(2.0 * math.pi))
        act = (up * cdf).astype(bf16)
        d_up = (d_act * (cdf + up * density)).astype(bf16)
        act_ref[:, fs] = act
        dup_ref[:, fs] = d_up
        down_acc[fs, :] += dot(act, g, 0, 0)
        up_acc[:, fs] += dot(h2, d_up, 0, 0)
    out_ref[...] = (y1 + dot(act_ref[...], wd_ref[...].reshape(FF, D))).astype(bf16)
    d_h2 = dot(dup_ref[:, :cut], wu0_ref[...].reshape(D, cut), 1, 1)
    for f in range(1, FF // cut):
        d_h2 = d_h2 + dot(
            dup_ref[:, cut * f : cut * (f + 1)], wu_refs[f][...].reshape(D, cut), 1, 1
        )
    e2 = d_h2 * gain
    dy1 = g.astype(f32) + r2 * (e2 - n2 * jnp.mean(e2 * n2, axis=-1, keepdims=True))
    dy1_ref[...] = dy1
    da = dy1.astype(bf16)
    out_acc[...] += dot(da, o, 0, 0)
    d_o = dot(da, wo)
    product = d_o * of_ref[...]
    high = product.astype(bf16)
    low = (product - high.astype(f32)).astype(bf16)
    rden = rden_ref[...]
    ma, mb = half_masks(128)
    same = jnp.concatenate(
        [jnp.broadcast_to(ma, (HD, 128)), jnp.broadcast_to(mb, (HD, 128))], axis=0
    )
    same = jnp.concatenate([same, same], axis=0)
    lane = lanes(128) % HD
    m0 = (lane == 0).astype(f32).astype(bf16)
    m1 = (lane == 1).astype(f32).astype(bf16)
    for p in range(PAIRS):
        ps = slice(128 * p, 128 * (p + 1))
        total = dot(jnp.concatenate([high[:, ps], low[:, ps]], axis=1), same)
        d_den = -total * rden[:, ps]
        d_hi = d_den.astype(bf16)
        d_lo = (d_den - d_hi.astype(f32)).astype(bf16)
        d_num = (d_o[:, ps] * rden[:, ps]).astype(bf16)
        dn = jnp.concatenate([d_num, d_hi * m0 + d_lo * m1], axis=1)
        dn_ref[:, 256 * p : 256 * (p + 1)] = dn

    @pl.when(step < SPAN // ROWS)
    def _():
        follows = flag(as_column(seg_ref[0]) == ends_ref[SPAN // CHUNK - 1])
        for p in range(PAIRS):
            back_acc[p] = back_acc[p] + dot(
                pq_ref[:, 512 * p : 512 * (p + 1)], dn_ref[:, 256 * p : 256 * (p + 1)] * follows, 0, 0
            )

    @pl.when(step == steps - 1)
    def _():
        core = core_ref[0]
        for ups, others, side in (
            (sent_up_ref, sent_rest_ref, 1 - core),
            (kept_up_ref, kept_rest_ref, core),
        ):
            for far in range(ups.shape[0] // group):
                at = (2 * far + side) * group
                here = slice(group * far, group * (far + 1))
                thin = pl.ds(pl.multiple_of(at * 16, 16), group * 16)
                tall = pl.ds(pl.multiple_of(at * 64, 64), group * 64)
                for f in range(FF // cut):
                    piece = up_acc[thin, cut * f : cut * (f + 1)].astype(bf16)
                    ups[here, 16 * f : 16 * (f + 1)] = piece.reshape(group, 16, cut)
                others[here, :64] = down_acc[tall].astype(bf16).reshape(group, 64, D)
                others[here, 64:] = out_acc[thin].astype(bf16).reshape(group, 16, D)
        for p in range(PAIRS):
            back = back_acc[p].astype(bf16)
            ma2, mb2 = half_masks(256)
            back_ref[p] = back[:FEATS] * ma2 + back[FEATS:] * mb2


def backward_kernel(pairs, ends_ref, seg_ref, gather_ref, *refs):
    refs = refs[: 7 * pairs] + refs[-2:]
    halo = SPAN // CHUNK
    step = pl.program_id(0)
    chunk = pl.num_programs(0) - 1 - step
    before = ends_ref[chunk + halo - 1]
    last = ends_ref[chunk + halo]
    ma2, mb2 = half_masks(256)
    dqkv_ref, state_ref = refs[7 * pairs :]
    back_refs = refs[6 * pairs : 7 * pairs]

    @pl.when(step == 0)
    def _():
        for p in range(pairs):
            state_ref[p, :FEATS] = (back_refs[p][0] * ma2).astype(f32)
            state_ref[p, FEATS:] = (back_refs[p][0] * mb2).astype(f32)

    seg_col, allowed = chunk_mask(seg_ref[0])
    chosen = flag(seg_col == last)
    follows = flag(seg_col == before)
    keep = (last == before).astype(f32)
    two = jnp.broadcast_to(flag(lanes(128) % HD < 2), (CHUNK, 128))
    ones = jnp.ones((CHUNK, 128), bf16)
    ma, mb = half_masks(128)
    for p in range(pairs):
        scores, pq, pk, qkv, dn = [refs[i * pairs + p][...] for i in range(5)]
        narrow = refs[5 * pairs + p][0, 0]
        q2, k2, v2 = qkv[:, :128], qkv[:, 128:256], qkv[:, 256:]
        state = state_ref[p]
        back = state.astype(bf16)
        back = masked_pair(back[:FEATS], back[FEATS:], 256)
        v1 = jnp.concatenate([v2, two], axis=1)
        d_p = dot(dn, masked_pair(v1, v1, 256), 1, 1).astype(bf16)
        d_pa = d_p[:, :CHUNK] * allowed
        d_pb = d_p[:, CHUNK:] * allowed
        dn_f = dn * follows
        d_pq = dot(dn_f, narrow, 1, 1) + jnp.concatenate(
            [dot(d_pa, pk[:, :FEATS]), dot(d_pb, pk[:, FEATS:])], axis=1
        )
        vw = jnp.concatenate([v2, ones], axis=1) * chosen
        d_pk = dot(vw, back, 1, 1) + jnp.concatenate(
            [dot(d_pa, pq[:, :FEATS], 0, 0), dot(d_pb, pq[:, FEATS:], 0, 0)], axis=1
        )
        d_num = dn[:, :128]
        d_v = (
            dot(pk * chosen, back[:, :128])
            + dot(scores[:, :CHUNK], d_num * ma, 0, 0)
            + dot(scores[:, CHUNK:], d_num * mb, 0, 0)
        )
        through_q = dot(d_pq.astype(bf16) * pq, gather_ref[...])
        through_k = dot(d_pk.astype(bf16) * pk, gather_ref[...])
        scale2 = feature_scale * feature_scale
        d_q = through_q[:, :128] * feature_scale - q2.astype(f32) * through_q[:, 128:] * scale2
        d_k = through_k[:, :128] * feature_scale - k2.astype(f32) * through_k[:, 128:] * scale2
        dqkv_ref[:, 384 * p : 384 * p + 128] = d_q.astype(bf16)
        dqkv_ref[:, 384 * p + 128 : 384 * p + 256] = d_k.astype(bf16)
        dqkv_ref[:, 384 * p + 256 : 384 * p + 384] = d_v.astype(bf16)
        state_ref[p] = keep * state + dot(pq, dn_f, 0, 0)


def input_kernel(dqkv_ref, wq_ref, x_ref, dy1_ref, gains_ref, dx_ref):
    d_h1 = dot(dqkv_ref[...], wq_ref[:, : 3 * D], 1, 1)
    x = x_ref[...].astype(f32)
    r1 = rms_scale(x)
    n1 = x * r1
    e1 = d_h1 * gains_ref[0:1]
    dx_ref[...] = dy1_ref[...] + r1 * (e1 - n1 * jnp.mean(e1 * n1, axis=-1, keepdims=True))


def finish_kernel(q_ref, kept_ref, came_ref, packed_ref, later_ref, sq_ref, sr_ref, gg_ref, spread_ref):
    share = q_ref.shape[1]
    sum_q = jnp.sum(q_ref[...].astype(f32), axis=0)
    sum_r = kept_ref[...].astype(f32) + came_ref[...].astype(f32)
    sq_ref[...] = sum_q
    sr_ref[...] = sum_r
    packed = packed_ref[...].astype(f32)
    tops = jnp.sum(packed[:, : 3 * D] * sum_q, axis=1, keepdims=True)
    rows = jnp.sum(later_ref[: 4 * share].astype(f32) * sum_r[: 4 * share], axis=1, keepdims=True)
    lows = rows[:share]
    for f in range(1, 4):
        lows = lows + rows[share * f : share * (f + 1)]
    gg = jnp.concatenate([tops, lows], axis=1) / packed[:, 3 * D : 3 * D + 2]
    gg_ref[...] = gg
    total = jnp.sum(sum_q * sum_q) + jnp.sum(sum_r * sum_r) + jnp.sum(gg * gg)
    spread_ref[...] = jnp.full(spread_ref.shape, total, f32)


def axis_bits():
    row_bits = (lax.axis_size("row") - 1).bit_length()
    head_bits = (lax.axis_size("head") - 1).bit_length()
    row = [("row", b, b) for b in range(row_bits)]
    head = [("head", b, row_bits + b) for b in range(head_bits)]
    return row, head


def swap(value, axis, bit):
    size = lax.axis_size(axis)
    return lax.ppermute(value, axis, [(i, i ^ (1 << bit)) for i in range(size)])


def tied(value, *others):
    return lax.optimization_barrier((value,) + others)[0]


class Gather:
    def __init__(self, shard):
        self.shape = shard.shape
        self.buf = shard
        self.held = []

    def start(self, axis, bit, place):
        self.came = swap(self.buf, axis, bit)
        self.mine = (lax.axis_index(axis) >> bit) & 1
        self.place = place

    def finish(self, *others):
        own = tied(self.buf, *others) if others else self.buf
        at = sum(1 for h in self.held if h > self.place)
        self.buf = jnp.where(
            self.mine == 0,
            jnp.stack([own, self.came], axis=at),
            jnp.stack([self.came, own], axis=at),
        )
        self.held = sorted(self.held + [self.place], reverse=True)

    def whole(self):
        return self.buf.reshape((-1,) + self.shape[1:])


class Halving:
    def __init__(self, kept, came, places):
        self.places = sorted(places, reverse=True)
        self.parts = [kept] if came is None else [kept, came]
        self.parts = [self.split(part) for part in self.parts]

    def split(self, part):
        inner = part.shape[1:] if part.ndim == 3 else part.shape[-2:]
        return part.reshape((2,) * len(self.places) + inner)

    def take(self, index, at):
        total = sum(
            lax.dynamic_index_in_dim(part, index, at, keepdims=False).astype(f32)
            for part in self.parts
        )
        return total.astype(bf16)

    def after(self, *others):
        self.parts[0] = tied(self.parts[0], *others)
        return self

    def send(self, axis, bit, place):
        at = self.places.index(place)
        mine = (lax.axis_index(axis) >> bit) & 1
        sent = self.take(1 - mine, at)
        came = swap(sent, axis, bit)
        self.parts = [self.take(mine, at), came]
        self.places.remove(place)
        return sent

    def total(self):
        return sum(part.astype(f32) for part in self.parts)


def ups_by_device(blocks, share):
    ups = blocks.reshape(-1, 4, 16 // share, share, 512)
    return ups.transpose(0, 2, 1, 3, 4).reshape(-1, 4 * share, 512)


def rest_by_device(blocks, share):
    downs = blocks[:, :64].reshape(-1, 4 * share, 512)
    outs = blocks[:, 64:].reshape(-1, share, 512)
    return jnp.concatenate([downs, outs], axis=1)


def core_groups():
    heads, rows = lax.axis_size("head"), lax.axis_size("row")
    return [[h * rows + r for h in range(c, heads, 2) for r in range(rows)] for c in (0, 1)]


def exchange(blocks):
    return lax.all_to_all(
        blocks, AXES, split_axis=0, concat_axis=0, axis_index_groups=core_groups(), tiled=True
    )


def total_of(spread):
    came = lax.all_to_all(spread, AXES, split_axis=0, concat_axis=0, tiled=True)
    return jnp.sum(came[:, 0, 0])


def adam_update(
    weight, gradient, first_moment, second_moment, clip_factor, step_value, step_rate, decay_rate
):
    clipped = gradient * clip_factor
    next_first = beta_first * first_moment + (1.0 - beta_first) * clipped
    next_second = beta_second * second_moment + (1.0 - beta_second) * clipped * clipped
    first_hat = next_first / (1.0 - beta_first**step_value)
    second_hat = next_second / (1.0 - beta_second**step_value)
    updated = weight - step_rate * (
        first_hat / (jnp.sqrt(second_hat) + adam_eps) + decay_rate * weight
    )
    return (clipped, next_first, next_second, updated)


def params(limit=60):
    return pltpu.CompilerParams(
        dimension_semantics=("arbitrary",), vmem_limit_bytes=limit << 20
    )


def cost(us):
    return pl.CostEstimate(flops=us * 50000000, transcendentals=0, bytes_accessed=us * 150000)


def fixed(shape):
    zeros = (0,) * len(shape)
    return pl.BlockSpec(shape, lambda *_: zeros, pipeline_mode=pl.Buffered(1))


def per_device(
    inputs,
    cotangent,
    segments,
    feature_matrix,
    w_qkv,
    w_out,
    w_up,
    w_down,
    gains,
    first_qkv,
    second_qkv,
    first_out,
    second_out,
    first_up,
    second_up,
    first_down,
    second_down,
    first_gains,
    second_gains,
    step_count,
):
    heads = lax.axis_size("head")
    row_bits, head_bits = axis_bits()
    x = inputs[0]
    g = cotangent[0]
    length = x.shape[0]
    chunks = length // CHUNK
    halo = SPAN // CHUNK
    share = w_qkv.shape[0]
    group = lax.axis_size("row") * share // 16

    packed = jnp.concatenate(
        [
            w_qkv.reshape(share, 3, PAIRS, 128).transpose(0, 2, 1, 3).reshape(share, 3 * D),
            gains,
            jnp.zeros((share, 126), f32),
        ],
        axis=1,
    ).astype(bf16)
    forward_pairs = [(i, i + 1) for i in range(heads - 1)]
    backward_pairs = [(i + 1, i) for i in range(heads - 1)]
    weights = Gather(packed)
    order = row_bits[::-1] + head_bits[::-1]
    weights.start(*order[0])
    later = jnp.concatenate(
        [w_up[:, 512 * j : 512 * (j + 1)] for j in range(FF // 512)] + [w_down, w_out], axis=0
    ).astype(bf16)
    tail = x[length - SPAN :]
    x_ahead = lax.ppermute(tail, "head", forward_pairs)
    weights.finish(tail)
    later_own = tied(later, weights.buf)
    later = lax.all_gather(later_own, AXES, axis=0)
    if share != 16:
        parts = 16 // share
        later = later.reshape(D // 16, parts, 9 * share, 512)
        ups = later[:, :, : 4 * share].reshape(D // 16, parts, 4, share, 512)
        ups = ups.transpose(0, 2, 1, 3, 4).reshape(D // 16, 64, 512)
        downs = later[:, :, 4 * share : 8 * share].reshape(D // 16, 64, 512)
        outs = later[:, :, 8 * share :].reshape(D // 16, 16, 512)
        later = jnp.concatenate([ups, downs, outs], axis=1)

    weights.start(*order[1])
    row_segments = tied(segments[0], weights.buf)
    padded = jnp.concatenate([jnp.full((SPAN,), -1, jnp.int32), row_segments])
    near = lax.dynamic_slice_in_dim(padded, lax.axis_index("head") * length, length + SPAN)
    ends = near[CHUNK - 1 :: CHUNK]
    seg_rows = near.astype(f32).reshape(-1, 1, CHUNK)
    near_rows = near[SPAN : 2 * SPAN].astype(f32).reshape(-1, 1, ROWS)
    fm = feature_matrix
    nothing = jnp.zeros_like(fm.T)
    spread = jnp.concatenate(
        [
            jnp.concatenate([fm.T, nothing], axis=1),
            jnp.concatenate([nothing, fm.T], axis=1),
        ],
        axis=0,
    )
    zero = jnp.zeros((FEATS, HD), bf16)
    one = jnp.ones((FEATS, HD), bf16)
    gather = jnp.concatenate(
        [
            jnp.concatenate([fm, zero, one, zero], axis=1),
            jnp.concatenate([zero, fm, zero, one], axis=1),
        ],
        axis=0,
    )
    weights.finish(ends, seg_rows, near_rows)
    weights.start(*order[2])
    weights.finish(spread, gather, x_ahead)
    for stage in order[3:]:
        weights.start(*stage)
        weights.finish()
    wq = weights.whole()
    core = (lax.axis_index("head") & 1).reshape(1)

    def own(shape):
        rest = (0,) * (len(shape) - 1)
        return pl.BlockSpec(shape, lambda c, *_: (jnp.maximum(c - halo, 0),) + rest)

    wide = PAIRS * 2 * FEATS
    h1, qkv, pq, pk, scores, states, o, of, rden, gain_rows = pl.pallas_call(
        forward_kernel,
        grid_spec=pltpu.PrefetchScalarGridSpec(
            num_scalar_prefetch=1,
            grid=(halo + chunks,),
            in_specs=[
                pl.BlockSpec((CHUNK, D), lambda c, *_: (jnp.minimum(c, halo - 1), 0)),
                own((CHUNK, D)),
                pl.BlockSpec((1, 1, CHUNK), lambda c, *_: (c, 0, 0)),
                fixed((D, 3 * D + 128)),
                fixed((2 * HD, 2 * FEATS)),
            ],
            out_specs=[
                own((CHUNK, D)),
                own((CHUNK, 3 * D)),
                own((CHUNK, wide)),
                own((CHUNK, wide)),
                own((CHUNK, wide)),
                own((1, PAIRS, 2 * FEATS, 256)),
                own((CHUNK, D)),
                own((CHUNK, D)),
                own((CHUNK, D)),
                fixed((8, D)),
            ],
            scratch_shapes=[pltpu.VMEM((PAIRS, 2 * FEATS, 256), f32)],
        ),
        out_shape=[
            jax.ShapeDtypeStruct((length, D), bf16),
            jax.ShapeDtypeStruct((length, 3 * D), bf16),
            jax.ShapeDtypeStruct((length, wide), bf16),
            jax.ShapeDtypeStruct((length, wide), bf16),
            jax.ShapeDtypeStruct((length, wide), bf16),
            jax.ShapeDtypeStruct((chunks, PAIRS, 2 * FEATS, 256), bf16),
            jax.ShapeDtypeStruct((length, D), bf16),
            jax.ShapeDtypeStruct((length, D), f32),
            jax.ShapeDtypeStruct((length, D), f32),
            jax.ShapeDtypeStruct((8, D), f32),
        ],
        compiler_params=params(),
        cost_estimate=cost(35),
        name="forward",
    )(ends, x_ahead, x, seg_rows, wq, spread)

    def by_step(shape):
        rest = (0,) * (len(shape) - 1)
        return pl.BlockSpec(shape, lambda c, *_: (c,) + rest)

    near_steps = SPAN // ROWS

    def columns(block):
        return pl.BlockSpec(
            (D // 16, 16, 512), lambda *_: (0, block, 0), pipeline_mode=pl.Buffered(1)
        )

    out_act, dy1, dn, sent_up, sent_rest, kept_up, kept_rest, back = pl.pallas_call(
        partial(middle_kernel, group),
        grid_spec=pltpu.PrefetchScalarGridSpec(
            num_scalar_prefetch=2,
            grid=(length // ROWS,),
            in_specs=[
                by_step((ROWS, D)),
                by_step((ROWS, D)),
                by_step((ROWS, D)),
                by_step((ROWS, D)),
                by_step((ROWS, D)),
                pl.BlockSpec((ROWS, wide), lambda c, *_: (jnp.minimum(c, near_steps - 1), 0)),
                pl.BlockSpec((1, 1, ROWS), lambda c, *_: (jnp.minimum(c, near_steps - 1), 0, 0)),
                fixed((8, D)),
                columns(0),
                columns(1),
                columns(2),
                columns(3),
                pl.BlockSpec(
                    (D // 16, 64, 512), lambda *_: (0, 1, 0), pipeline_mode=pl.Buffered(1)
                ),
                columns(8),
            ],
            out_specs=[
                by_step((ROWS, D)),
                by_step((ROWS, D)),
                by_step((ROWS, PAIRS * 256)),
                fixed((D // 32, 64, 512)),
                fixed((D // 32, 80, 512)),
                fixed((D // 32, 64, 512)),
                fixed((D // 32, 80, 512)),
                fixed((PAIRS, FEATS, 256)),
            ],
            scratch_shapes=[
                pltpu.VMEM((D, FF), f32),
                pltpu.VMEM((FF, D), f32),
                pltpu.VMEM((D, D), f32),
                pltpu.VMEM((PAIRS, 2 * FEATS, 256), f32),
                pltpu.VMEM((ROWS, FF), bf16),
                pltpu.VMEM((ROWS, FF), bf16),
            ],
        ),
        out_shape=[
            jax.ShapeDtypeStruct((length, D), bf16),
            jax.ShapeDtypeStruct((length, D), f32),
            jax.ShapeDtypeStruct((length, PAIRS * 256), bf16),
            jax.ShapeDtypeStruct((D // 32, 64, 512), bf16),
            jax.ShapeDtypeStruct((D // 32, 80, 512), bf16),
            jax.ShapeDtypeStruct((D // 32, 64, 512), bf16),
            jax.ShapeDtypeStruct((D // 32, 80, 512), bf16),
            jax.ShapeDtypeStruct((PAIRS, FEATS, 256), bf16),
        ],
        compiler_params=params(),
        cost_estimate=cost(48),
        name="middle",
    )(
        ends, core, x, g, o, of, rden, pq, near_rows, gain_rows,
        later, later, later, later, later, later,
    )

    if share != 16:
        sent_up, kept_up = ups_by_device(sent_up, share), ups_by_device(kept_up, share)
        sent_rest, kept_rest = rest_by_device(sent_rest, share), rest_by_device(kept_rest, share)
    back_in = lax.ppermute(back, "head", backward_pairs)
    came_up = swap(sent_up, "head", 0)
    came_rest = swap(sent_rest, "head", 0)

    def attention_back(at, back_in, *written):
        chosen = range(at * PAIRS // 2, (at + 1) * PAIRS // 2)
        count = len(chosen)

        def falling(shape, at=0):
            rest = (0,) * (len(shape) - 2)
            return pl.BlockSpec(shape, lambda c, *_: (chunks - 1 - c, at) + rest)

        def state(at):
            return pl.BlockSpec(
                (1, FEATS, 256), lambda *_: (at, 0, 0), pipeline_mode=pl.Buffered(1)
            )

        specs = [pl.BlockSpec((1, 1, CHUNK), lambda c, *_: (chunks + halo - 1 - c, 0, 0))]
        specs += [fixed((2 * FEATS, 256))]
        for shape in ((CHUNK, 512),) * 3 + ((CHUNK, 384), (CHUNK, 256), (1, 1, 512, 256)):
            specs += [falling(shape, p) for p in chosen]
        specs += [state(p) for p in chosen]
        operands = []
        for array in (scores, pq, pk, qkv, dn, states, back_in):
            operands += [array] * count
        return pl.pallas_call(
            partial(backward_kernel, count),
            grid_spec=pltpu.PrefetchScalarGridSpec(
                num_scalar_prefetch=1,
                grid=(chunks,),
                in_specs=specs + [pl.BlockSpec(memory_space=pl.ANY)] * len(written),
                out_specs=falling((CHUNK, 384 * count), at),
                scratch_shapes=[pltpu.VMEM((count, 2 * FEATS, 256), f32)],
            ),
            out_shape=jax.ShapeDtypeStruct((length, 3 * D), bf16),
            input_output_aliases={3 + len(operands): 0} if written else {},
            compiler_params=params(),
            cost_estimate=cost(8 * count),
            name="backward",
        )(ends, seg_rows, gather, *operands, *written)

    core_bit, *far_bits = head_bits
    places = [place for _, _, place in far_bits + row_bits]
    lower = [(axis, bit, place - (place > core_bit[2])) for axis, bit, place in far_bits]
    first_order = lower + row_bits[:1]
    second_order = row_bits[:1] + lower
    last_order = row_bits[1:]
    places = [place for _, _, place in first_order + last_order]
    cut = 4 * share

    dqkv = attention_back(0, tied(back_in, sent_up, sent_rest))
    kept_up, kept_rest = tied(kept_up, dqkv), tied(kept_rest, dqkv)
    first = Halving(kept_up, came_up, places)
    second = Halving(kept_rest, came_rest, places)
    back_in = tied(back_in, first.send(*first_order[0]), second.send(*second_order[0]))
    dqkv = attention_back(1, back_in, dqkv)

    ready = tied(h1, dqkv, first.parts[1], second.parts[1])
    g_qkv = dot(ready, dqkv, 0, 0).astype(bf16).reshape(heads // 2, 2, -1, 3 * D)
    sent_qkv = lax.dynamic_index_in_dim(g_qkv, 1 - core[0], 1, False)
    came_qkv = swap(sent_qkv, "head", 0)
    moved = []
    for left, right in zip(first_order[1:], second_order[1:]):
        moved.append(first.after(sent_qkv).send(*left))
        moved.append(second.after(sent_qkv).send(*right))
    kept_qkv = tied(lax.dynamic_index_in_dim(g_qkv, core[0], 1, False), *moved)
    merged_qkv = (kept_qkv.astype(f32) + came_qkv.astype(f32)).astype(bf16)
    all_qkv = exchange(merged_qkv.reshape(-1, share, 3 * D))
    dx = pl.pallas_call(
        input_kernel,
        grid=(length // ROWS,),
        in_specs=[
            by_step((ROWS, 3 * D)),
            fixed((D, 3 * D + 128)),
            by_step((ROWS, D)),
            by_step((ROWS, D)),
            fixed((8, D)),
        ],
        out_specs=by_step((ROWS, D)),
        out_shape=jax.ShapeDtypeStruct((length, D), f32),
        compiler_params=params(),
        cost_estimate=cost(10),
        name="input_grad",
    )(dqkv, wq, x, tied(dy1, merged_qkv), gain_rows)
    left, right = [[tied(part, dx) for part in h.parts] for h in (first, second)]
    rest = Halving(jnp.concatenate([left[0], right[0]], axis=-2), None, first.places)
    rest.parts.append(jnp.concatenate([left[1], right[1]], axis=-2))
    for stage in last_order:
        rest.send(*stage)
    kept, came = rest.parts
    count = lax.axis_size(AXES)
    sum_qkv, sums, sum_gains, spread = pl.pallas_call(
        finish_kernel,
        out_shape=[
            jax.ShapeDtypeStruct((share, 3 * D), f32),
            jax.ShapeDtypeStruct((9 * share, 512), f32),
            jax.ShapeDtypeStruct((share, 2), f32),
            jax.ShapeDtypeStruct((count, 8, 128), f32),
        ],
        name="finish",
    )(all_qkv, kept, came, packed, later_own)
    total_squares = total_of(spread)
    sum_qkv = sum_qkv.reshape(share, PAIRS, 3, 128).transpose(0, 2, 1, 3).reshape(share, 3, D)
    sum_up = sums[: 4 * share].reshape(4, share, 512).transpose(1, 0, 2).reshape(share, FF)
    sum_down = sums[4 * share : 8 * share]
    sum_out = sums[8 * share :]
    reduced = (sum_qkv, sum_out, sum_up, sum_down, sum_gains)
    grad_norm = jnp.sqrt(total_squares)
    clip_factor = jnp.minimum(1.0, max_norm / (grad_norm + 1e-06))
    step_value = step_count.astype(f32)
    update = partial(adam_update, clip_factor=clip_factor, step_value=step_value)
    qkv_parts = update(
        w_qkv, reduced[0], first_qkv, second_qkv, step_rate=matrix_rate, decay_rate=matrix_decay
    )
    out_parts = update(
        w_out, reduced[1], first_out, second_out, step_rate=output_rate, decay_rate=matrix_decay
    )
    up_parts = update(
        w_up, reduced[2], first_up, second_up, step_rate=matrix_rate, decay_rate=matrix_decay
    )
    down_parts = update(
        w_down, reduced[3], first_down, second_down, step_rate=matrix_rate, decay_rate=matrix_decay
    )
    gain_parts = update(
        gains, reduced[4], first_gains, second_gains, step_rate=gain_rate, decay_rate=0.0
    )
    return (
        (out_act[None], dx[None], grad_norm)
        + qkv_parts
        + out_parts
        + up_parts
        + down_parts
        + gain_parts
    )


def solution(mesh):
    token = P("row", "head", None)
    three = P(AXES, None, None)
    two = P(AXES, None)
    placed = (token, token, P("row", None), P(), three, two, two, two, two)
    placed = placed + (three, three) + (two,) * 8 + (P(),)
    return jax.shard_map(
        per_device,
        mesh=mesh,
        in_specs=placed,
        out_specs=(token, token, P()) + (three,) * 4 + (two,) * 16,
        check_vma=False,
    )
```

```python
import math
from functools import partial

import jax
import jax.numpy as jnp
from jax import lax
from jax.experimental import pallas as pl
from jax.experimental.pallas import tpu as pltpu
from jax.sharding import PartitionSpec as P

D = 512
HD = 64
FEATS = 256
FF = 2048
CHUNK = 256
SPAN = 1024
ROWS = 512
PAIRS = D // (2 * HD)

bf16 = jnp.bfloat16
f32 = jnp.float32
norm_eps = 1e-06
beta_first = 0.9
beta_second = 0.999
adam_eps = 1e-08
max_norm = 1.0
matrix_rate = 0.08
output_rate = 0.3
gain_rate = 1.5
matrix_decay = 0.1
feature_scale = HD ** (-0.25)
log2e = math.log2(math.e)
AXES = ("head", "row")


def dot(a, b, ca=1, cb=0):
    return lax.dot_general(a, b, (((ca,), (cb,)), ((), ())), preferred_element_type=f32)


def lanes(width):
    return lax.broadcasted_iota(jnp.int32, (1, width), 1)


def half_masks(width):
    first = (lanes(width) % 128 < HD).astype(f32)
    return first.astype(bf16), (1.0 - first).astype(bf16)


def rms_scale(values):
    return lax.rsqrt(jnp.mean(values * values, axis=-1, keepdims=True) + norm_eps)


def features(u, spread):
    raw = dot(u, spread)
    wide = u.astype(f32)
    squares = wide * wide
    own = lanes(2 * HD) < HD
    total_a = jnp.sum(jnp.where(own, squares, 0.0), axis=1, keepdims=True)
    total_b = jnp.sum(jnp.where(own, 0.0, squares), axis=1, keepdims=True)
    c1 = feature_scale * log2e
    c2 = 0.5 * feature_scale * feature_scale * log2e
    down_a = total_a * c2 + 4.0
    down_b = total_b * c2 + 4.0
    left = jnp.exp2(raw[:, :FEATS] * c1 - down_a)
    right = jnp.exp2(raw[:, FEATS:] * c1 - down_b)
    return jnp.concatenate([left, right], axis=1).astype(bf16)


def masked_pair(first, second, width):
    ma, mb = half_masks(width)
    return jnp.concatenate([first * ma, second * mb], axis=0)


def as_column(row):
    return jnp.broadcast_to(row, (8, row.shape[1])).T[:, :1]


def flag(condition):
    return condition.astype(f32).astype(bf16)


def chunk_mask(seg_row):
    seg_col = as_column(seg_row)
    rows = lax.broadcasted_iota(jnp.int32, (CHUNK, CHUNK), 0)
    cols = lax.broadcasted_iota(jnp.int32, (CHUNK, CHUNK), 1)
    return seg_col, flag((rows >= cols) & (seg_col == seg_row))


def compacted(first, second):
    ma, mb = half_masks(256)
    return first * ma + second * mb


def forward_kernel(
    ends_ref, xh_ref, xo_ref, seg_ref, wq_ref, spread_ref,
    h1_ref, qkv_ref, pq_ref, pk_ref, p_ref, t_ref, o_ref, rden_ref, gains_ref,
    state_ref,
):
    step = pl.program_id(0)
    halo = SPAN // ROWS
    subs = ROWS // CHUNK
    ones = jnp.ones((ROWS, 2 * HD), bf16)

    @pl.when(step == 0)
    def _():
        state_ref[...] = jnp.zeros_like(state_ref)
        gains_ref[...] = wq_ref[:, 3 * D :].astype(f32).T[:8]

    gain = gains_ref[0:1]

    @pl.when(step < halo)
    def _():
        x = xh_ref[...].astype(f32)
        h1 = (x * rms_scale(x) * gain).astype(bf16)
        chosen = flag(as_column(seg_ref[0]) == ends_ref[halo * subs - 1])
        kvs = [dot(h1, wq_ref[:, 384 * p + 128 : 384 * (p + 1)]).astype(bf16) for p in range(PAIRS)]
        for p in range(PAIRS):
            pk_ref[:, 512 * p : 512 * (p + 1)] = features(kvs[p][:, :128], spread_ref[...])
        for p in range(PAIRS):
            vw = jnp.concatenate([kvs[p][:, 128:], ones], axis=1) * chosen
            state_ref[p] = state_ref[p] + dot(pk_ref[:, 512 * p : 512 * (p + 1)], vw, 0, 0)

    @pl.when(step >= halo)
    def _():
        x = xo_ref[...].astype(f32)
        h1 = (x * rms_scale(x) * gain).astype(bf16)
        h1_ref[...] = h1
        qkv_ref[...] = dot(h1, wq_ref[:, : 3 * D]).astype(bf16)
        for p in range(PAIRS):
            wide = slice(512 * p, 512 * (p + 1))
            pq_ref[:, wide] = features(qkv_ref[:, 384 * p : 384 * p + 128], spread_ref[...])
            pk_ref[:, wide] = features(qkv_ref[:, 384 * p + 128 : 384 * p + 256], spread_ref[...])
        seg = seg_ref[0]
        for j in range(subs):
            rows = slice(CHUNK * j, CHUNK * (j + 1))
            _, allowed = chunk_mask(seg[:, rows])
            for h in range(2 * PAIRS):
                cut = slice(FEATS * h, FEATS * (h + 1))
                p_ref[rows, CHUNK * h : CHUNK * (h + 1)] = (
                    dot(pq_ref[rows, cut], pk_ref[rows, cut], 1, 1).astype(bf16) * allowed
                )
        seg_col = as_column(seg)
        for j in range(subs):
            rows = slice(CHUNK * j, CHUNK * (j + 1))
            before = ends_ref[step * subs + j - 1]
            last = ends_ref[step * subs + j]
            chosen = flag(seg_col[rows] == last)
            follows = flag(seg_col[rows] == before)
            keep = (last == before).astype(f32)
            for p in range(PAIRS):
                cut = slice(128 * p, 128 * (p + 1))
                wide = slice(512 * p, 512 * (p + 1))
                v2 = qkv_ref[rows, 384 * p + 256 : 384 * p + 384]
                v1 = jnp.concatenate([v2, ones[:CHUNK]], axis=1)
                state = state_ref[p]
                narrow = state.astype(bf16)
                narrow = masked_pair(narrow[:FEATS], narrow[FEATS:], 256)
                t_ref[j, p] = narrow[:FEATS] + narrow[FEATS:]
                both = dot(p_ref[rows, wide], masked_pair(v1, v1, 256)) + dot(
                    pq_ref[rows, wide] * follows, narrow
                )
                state_ref[p] = keep * state + dot(pk_ref[rows, wide], v1 * chosen, 0, 0)
                rden = 1.0 / both[:, 128:]
                rden_ref[rows, cut] = rden
                o_ref[rows, cut] = (both[:, :128] * rden).astype(bf16)


def middle_kernel(
    group,
    ends_ref, core_ref, x_ref, g_ref, o_ref, rden_ref, pq_ref, seg_ref, gains_ref,
    wu0_ref, wu1_ref, wu2_ref, wu3_ref, wd_ref, wo_ref,
    out_ref, dy1_ref, dn_ref, sent_up_ref, sent_rest_ref, kept_up_ref, kept_rest_ref, back_ref,
    up_acc, down_acc, out_acc, back_acc, act_ref, dup_ref,
):
    step = pl.program_id(0)
    steps = pl.num_programs(0)
    cut = 512
    wu_refs = (wu0_ref, wu1_ref, wu2_ref, wu3_ref)
    blocks = wd_ref.shape[0] // len(wu_refs)

    @pl.when(step == 0)
    def _():
        up_acc[...] = jnp.zeros_like(up_acc)
        down_acc[...] = jnp.zeros_like(down_acc)
        out_acc[...] = jnp.zeros_like(out_acc)
        back_acc[...] = jnp.zeros_like(back_acc)

    o = o_ref[...]
    g = g_ref[...]
    gain = gains_ref[1:2]
    wo = wo_ref[...].reshape(D, D)
    y1 = x_ref[...].astype(f32) + dot(o, wo, 1, 1)
    r2 = rms_scale(y1)
    n2 = y1 * r2
    h2 = (n2 * gain).astype(bf16)
    for f in range(FF // cut):
        fs = slice(cut * f, cut * (f + 1))
        wd = wd_ref[blocks * f : blocks * (f + 1)].reshape(cut, D)
        up = dot(h2, wu_refs[f][...].reshape(D, cut))
        d_act = dot(g, wd, 1, 1)
        cdf = 0.5 * (1.0 + lax.erf(up * math.sqrt(0.5)))
        density = jnp.exp(up * up * -0.5) * (1.0 / math.sqrt(2.0 * math.pi))
        act = (up * cdf).astype(bf16)
        d_up = (d_act * (cdf + up * density)).astype(bf16)
        act_ref[:, fs] = act
        dup_ref[:, fs] = d_up
        down_acc[fs, :] += dot(act, g, 0, 0)
        up_acc[:, fs] += dot(h2, d_up, 0, 0)
    out_ref[...] = (y1 + dot(act_ref[...], wd_ref[...].reshape(FF, D))).astype(bf16)
    d_h2 = dot(dup_ref[:, :cut], wu0_ref[...].reshape(D, cut), 1, 1)
    for f in range(1, FF // cut):
        d_h2 = d_h2 + dot(
            dup_ref[:, cut * f : cut * (f + 1)], wu_refs[f][...].reshape(D, cut), 1, 1
        )
    e2 = d_h2 * gain
    dy1 = g.astype(f32) + r2 * (e2 - n2 * jnp.mean(e2 * n2, axis=-1, keepdims=True))
    dy1_ref[...] = dy1
    da = dy1.astype(bf16)
    out_acc[...] += dot(da, o, 0, 0)
    d_o = dot(da, wo)
    product = d_o * o.astype(f32)
    high = product.astype(bf16)
    low = (product - high.astype(f32)).astype(bf16)
    rden = rden_ref[...]
    ma, mb = half_masks(128)
    same = jnp.concatenate(
        [jnp.broadcast_to(ma, (HD, 128)), jnp.broadcast_to(mb, (HD, 128))], axis=0
    )
    same = jnp.concatenate([same, same], axis=0)
    lane = lanes(128) % HD
    m0 = (lane == 0).astype(f32).astype(bf16)
    m1 = (lane == 1).astype(f32).astype(bf16)
    for p in range(PAIRS):
        ps = slice(128 * p, 128 * (p + 1))
        total = dot(jnp.concatenate([high[:, ps], low[:, ps]], axis=1), same)
        d_den = -total * rden[:, ps]
        d_hi = d_den.astype(bf16)
        d_lo = (d_den - d_hi.astype(f32)).astype(bf16)
        d_num = (d_o[:, ps] * rden[:, ps]).astype(bf16)
        dn = jnp.concatenate([d_num, d_hi * m0 + d_lo * m1], axis=1)
        dn_ref[:, 256 * p : 256 * (p + 1)] = dn

    @pl.when(step < SPAN // ROWS)
    def _():
        follows = flag(as_column(seg_ref[0]) == ends_ref[SPAN // CHUNK - 1])
        for p in range(PAIRS):
            back_acc[p] = back_acc[p] + dot(
                pq_ref[:, 512 * p : 512 * (p + 1)], dn_ref[:, 256 * p : 256 * (p + 1)] * follows, 0, 0
            )

    @pl.when(step == steps - 1)
    def _():
        core = core_ref[0]
        for ups, others, side in (
            (sent_up_ref, sent_rest_ref, 1 - core),
            (kept_up_ref, kept_rest_ref, core),
        ):
            for far in range(ups.shape[0] // group):
                at = (2 * far + side) * group
                here = slice(group * far, group * (far + 1))
                thin = pl.ds(pl.multiple_of(at * 16, 16), group * 16)
                tall = pl.ds(pl.multiple_of(at * 64, 64), group * 64)
                for f in range(FF // cut):
                    piece = up_acc[thin, cut * f : cut * (f + 1)].astype(bf16)
                    ups[here, 16 * f : 16 * (f + 1)] = piece.reshape(group, 16, cut)
                others[here, :64] = down_acc[tall].astype(bf16).reshape(group, 64, D)
                others[here, 64:] = out_acc[thin].astype(bf16).reshape(group, 16, D)
        for p in range(PAIRS):
            back = back_acc[p].astype(bf16)
            back_ref[p] = compacted(back[:FEATS], back[FEATS:])


def backward_kernel(pairs, ends_ref, seg_ref, gather_ref, *refs):
    refs = refs[: 7 * pairs] + refs[-4:]
    subs = ROWS // CHUNK
    step = pl.program_id(0)
    steps = pl.num_programs(0)
    at = (SPAN // ROWS + steps - 1 - step) * subs
    dqkv_ref, state_ref, grad_ref, logit_ref = refs[7 * pairs :]
    p_refs, pq_refs, pk_refs, qkv_refs, dn_refs, t_refs, back_refs = [
        refs[i * pairs : (i + 1) * pairs] for i in range(7)
    ]
    ma2, mb2 = half_masks(256)

    @pl.when(step == 0)
    def _():
        for p in range(pairs):
            state_ref[p, :FEATS] = (back_refs[p][0] * ma2).astype(f32)
            state_ref[p, FEATS:] = (back_refs[p][0] * mb2).astype(f32)

    seg = seg_ref[0]
    seg_col = as_column(seg)
    two = jnp.broadcast_to(flag(lanes(128) % HD < 2), (CHUNK, 128))
    ones = jnp.ones((CHUNK, 128), bf16)
    ma, mb = half_masks(128)
    for j in reversed(range(subs)):
        rows = slice(CHUNK * j, CHUNK * (j + 1))
        _, allowed = chunk_mask(seg[:, rows])
        before = ends_ref[at + j - 1]
        last = ends_ref[at + j]
        chosen = flag(seg_col[rows] == last)
        follows = flag(seg_col[rows] == before)
        keep = (last == before).astype(f32)
        for p in range(pairs):
            v1 = jnp.concatenate([qkv_refs[p][rows, 256:], two], axis=1)
            d_p = dot(dn_refs[p][rows], masked_pair(v1, v1, 256), 1, 1).astype(bf16)
            grad_ref[p, :, :CHUNK] = d_p[:, :CHUNK] * allowed
            grad_ref[p, :, CHUNK:] = d_p[:, CHUNK:] * allowed
        for p in range(pairs):
            pq, pk, dn = pq_refs[p][rows], pk_refs[p][rows], dn_refs[p][rows]
            scores = p_refs[p][rows]
            v2 = qkv_refs[p][rows, 256:]
            compact = t_refs[p][j, 0]
            narrow = masked_pair(compact, compact, 256)
            state = state_ref[p]
            back = state.astype(bf16)
            back = masked_pair(back[:FEATS], back[FEATS:], 256)
            d_pa = grad_ref[p, :, :CHUNK]
            d_pb = grad_ref[p, :, CHUNK:]
            dn_f = dn * follows
            d_pq = dot(dn_f, narrow, 1, 1) + jnp.concatenate(
                [dot(d_pa, pk[:, :FEATS]), dot(d_pb, pk[:, FEATS:])], axis=1
            )
            logit_ref[0, p, rows] = d_pq.astype(bf16) * pq
            vw = jnp.concatenate([v2, ones], axis=1) * chosen
            d_pk = dot(vw, back, 1, 1) + jnp.concatenate(
                [dot(d_pa, pq[:, :FEATS], 0, 0), dot(d_pb, pq[:, FEATS:], 0, 0)], axis=1
            )
            logit_ref[1, p, rows] = d_pk.astype(bf16) * pk
            d_num = dn[:, :128]
            d_v = (
                dot(pk * chosen, back[:, :128])
                + dot(scores[:, :CHUNK], d_num * ma, 0, 0)
                + dot(scores[:, CHUNK:], d_num * mb, 0, 0)
            )
            dqkv_ref[rows, 384 * p + 256 : 384 * p + 384] = d_v.astype(bf16)
            state_ref[p] = keep * state + dot(pq, dn_f, 0, 0)
    scale2 = feature_scale * feature_scale
    for p in range(pairs):
        for i in range(2):
            u = qkv_refs[p][:, 128 * i : 128 * (i + 1)].astype(f32)
            through = dot(logit_ref[i, p], gather_ref[...])
            d_u = through[:, :128] * feature_scale - u * through[:, 128:] * scale2
            dqkv_ref[:, 384 * p + 128 * i : 384 * p + 128 * (i + 1)] = d_u.astype(bf16)


def input_kernel(dqkv_ref, wq_ref, x_ref, dy1_ref, gains_ref, dx_ref):
    d_h1 = dot(dqkv_ref[...], wq_ref[:, : 3 * D], 1, 1)
    x = x_ref[...].astype(f32)
    r1 = rms_scale(x)
    n1 = x * r1
    e1 = d_h1 * gains_ref[0:1]
    dx_ref[...] = dy1_ref[...] + r1 * (e1 - n1 * jnp.mean(e1 * n1, axis=-1, keepdims=True))


def finish_kernel(q_ref, kept_ref, came_ref, packed_ref, later_ref, sq_ref, sr_ref, gg_ref, spread_ref):
    share = q_ref.shape[1]
    sum_q = jnp.sum(q_ref[...].astype(f32), axis=0)
    sum_r = kept_ref[...].astype(f32) + came_ref[...].astype(f32)
    sq_ref[...] = sum_q
    sr_ref[...] = sum_r
    packed = packed_ref[...].astype(f32)
    tops = jnp.sum(packed[:, : 3 * D] * sum_q, axis=1, keepdims=True)
    rows = jnp.sum(later_ref[: 4 * share].astype(f32) * sum_r[: 4 * share], axis=1, keepdims=True)
    lows = rows[:share]
    for f in range(1, 4):
        lows = lows + rows[share * f : share * (f + 1)]
    gg = jnp.concatenate([tops, lows], axis=1) / packed[:, 3 * D : 3 * D + 2]
    gg_ref[...] = jnp.concatenate([gg, jnp.zeros((share, 126), f32)], axis=1).T[:2]
    total = jnp.sum(sum_q * sum_q) + jnp.sum(sum_r * sum_r) + jnp.sum(gg * gg)
    spread_ref[...] = jnp.full(spread_ref.shape, total, f32)


def axis_bits():
    row_bits = (lax.axis_size("row") - 1).bit_length()
    head_bits = (lax.axis_size("head") - 1).bit_length()
    row = [("row", b, b) for b in range(row_bits)]
    head = [("head", b, row_bits + b) for b in range(head_bits)]
    return row, head


def swap(value, axis, bit):
    size = lax.axis_size(axis)
    return lax.ppermute(value, axis, [(i, i ^ (1 << bit)) for i in range(size)])


def tied(value, *others):
    return lax.optimization_barrier((value,) + others)[0]


class Gather:
    def __init__(self, shard):
        self.shape = shard.shape
        self.buf = shard
        self.held = []

    def start(self, axis, bit, place):
        self.came = swap(self.buf, axis, bit)
        self.mine = (lax.axis_index(axis) >> bit) & 1
        self.place = place

    def finish(self, *others):
        own = tied(self.buf, *others) if others else self.buf
        at = sum(1 for h in self.held if h > self.place)
        self.buf = jnp.where(
            self.mine == 0,
            jnp.stack([own, self.came], axis=at),
            jnp.stack([self.came, own], axis=at),
        )
        self.held = sorted(self.held + [self.place], reverse=True)

    def whole(self):
        return self.buf.reshape((-1,) + self.shape[1:])


class Halving:
    def __init__(self, kept, came, places):
        self.places = sorted(places, reverse=True)
        self.parts = [kept] if came is None else [kept, came]
        self.parts = [self.split(part) for part in self.parts]

    def split(self, part):
        inner = part.shape[1:] if part.ndim == 3 else part.shape[-2:]
        return part.reshape((2,) * len(self.places) + inner)

    def take(self, index, at):
        total = sum(
            lax.dynamic_index_in_dim(part, index, at, keepdims=False).astype(f32)
            for part in self.parts
        )
        return total.astype(bf16)

    def after(self, *others):
        self.parts[0] = tied(self.parts[0], *others)
        return self

    def send(self, axis, bit, place):
        at = self.places.index(place)
        mine = (lax.axis_index(axis) >> bit) & 1
        sent = self.take(1 - mine, at)
        came = swap(sent, axis, bit)
        self.parts = [self.take(mine, at), came]
        self.places.remove(place)
        return sent

    def total(self):
        return sum(part.astype(f32) for part in self.parts)


def ups_by_device(blocks, share):
    ups = blocks.reshape(-1, 4, 16 // share, share, 512)
    return ups.transpose(0, 2, 1, 3, 4).reshape(-1, 4 * share, 512)


def rest_by_device(blocks, share):
    downs = blocks[:, :64].reshape(-1, 4 * share, 512)
    outs = blocks[:, 64:].reshape(-1, share, 512)
    return jnp.concatenate([downs, outs], axis=1)


def core_groups():
    heads, rows = lax.axis_size("head"), lax.axis_size("row")
    return [[h * rows + r for h in range(c, heads, 2) for r in range(rows)] for c in (0, 1)]


def exchange(blocks):
    return lax.all_to_all(
        blocks, AXES, split_axis=0, concat_axis=0, axis_index_groups=core_groups(), tiled=True
    )


def total_of(spread):
    came = lax.all_to_all(spread, AXES, split_axis=0, concat_axis=0, tiled=True)
    return jnp.sum(came[:, 0, 0])


def adam_update(
    weight, gradient, first_moment, second_moment, clip_factor, step_value, step_rate, decay_rate
):
    clipped = gradient * clip_factor
    next_first = beta_first * first_moment + (1.0 - beta_first) * clipped
    next_second = beta_second * second_moment + (1.0 - beta_second) * clipped * clipped
    first_hat = next_first / (1.0 - beta_first**step_value)
    second_hat = next_second / (1.0 - beta_second**step_value)
    updated = weight - step_rate * (
        first_hat / (jnp.sqrt(second_hat) + adam_eps) + decay_rate * weight
    )
    return (clipped, next_first, next_second, updated)


def params(limit=60):
    return pltpu.CompilerParams(
        dimension_semantics=("arbitrary",), vmem_limit_bytes=limit << 20
    )


def cost(us):
    return pl.CostEstimate(flops=us * 50000000, transcendentals=0, bytes_accessed=us * 150000)


def fixed(shape):
    zeros = (0,) * len(shape)
    return pl.BlockSpec(shape, lambda *_: zeros, pipeline_mode=pl.Buffered(1))


def first_at(shape, offset):
    rest = (0,) * (len(shape) - 1)
    return pl.BlockSpec(shape, lambda c, *_: (jnp.maximum(c - offset, 0),) + rest)


def by_step(shape):
    return first_at(shape, 0)


def forward_call(ends, x_ahead, x, seg_rows, wq, spread):
    length = x.shape[0]
    chunks, halo, wide = length // CHUNK, SPAN // ROWS, PAIRS * 2 * FEATS
    own = partial(first_at, offset=halo)
    outs = [
        ((ROWS, D), (length, D), bf16),
        ((ROWS, 3 * D), (length, 3 * D), bf16),
        ((ROWS, wide), (length, wide), bf16),
        ((ROWS, wide), (length, wide), bf16),
        ((ROWS, wide), (length, wide), bf16),
        ((ROWS // CHUNK, PAIRS, FEATS, 256), (chunks, PAIRS, FEATS, 256), bf16),
        ((ROWS, D), (length, D), bf16),
        ((ROWS, D), (length, D), f32),
    ]
    return pl.pallas_call(
        forward_kernel,
        grid_spec=pltpu.PrefetchScalarGridSpec(
            num_scalar_prefetch=1,
            grid=(halo + length // ROWS,),
            in_specs=[
                pl.BlockSpec((ROWS, D), lambda c, *_: (jnp.minimum(c, halo - 1), 0)),
                own((ROWS, D)),
                by_step((1, 1, ROWS)),
                fixed(wq.shape),
                fixed(spread.shape),
            ],
            out_specs=[own(block) for block, _, _ in outs] + [fixed((8, D))],
            scratch_shapes=[pltpu.VMEM((PAIRS, 2 * FEATS, 256), f32)],
        ),
        out_shape=[jax.ShapeDtypeStruct(shape, kind) for _, shape, kind in outs]
        + [jax.ShapeDtypeStruct((8, D), f32)],
        compiler_params=params(),
        cost_estimate=cost(35),
        name="forward",
    )(ends, x_ahead, x, seg_rows, wq, spread)


def middle_call(group, ends, core, x, g, o, rden, pq, seg_rows, gain_rows, later):
    length, wide = x.shape[0], pq.shape[1]
    near_steps = SPAN // ROWS
    by_step_ahead = pl.BlockSpec((1, 1, ROWS), lambda c, *_: (c + near_steps, 0, 0))

    def columns(block, height=16):
        return pl.BlockSpec(
            (D // 16, height, 512), lambda *_: (0, block, 0), pipeline_mode=pl.Buffered(1)
        )

    outs = [
        ((ROWS, D), (length, D), bf16),
        ((ROWS, D), (length, D), f32),
        ((ROWS, PAIRS * 256), (length, PAIRS * 256), bf16),
    ]
    sums = [(D // 32, 64, 512), (D // 32, 80, 512)] * 2 + [(PAIRS, FEATS, 256)]
    return pl.pallas_call(
        partial(middle_kernel, group),
        grid_spec=pltpu.PrefetchScalarGridSpec(
            num_scalar_prefetch=2,
            grid=(length // ROWS,),
            in_specs=[by_step((ROWS, D))] * 4
            + [
                pl.BlockSpec((ROWS, wide), lambda c, *_: (jnp.minimum(c, near_steps - 1), 0)),
                by_step_ahead,
                fixed((8, D)),
            ]
            + [columns(f) for f in range(4)]
            + [columns(1, 64), columns(8)],
            out_specs=[by_step(block) for block, _, _ in outs] + [fixed(shape) for shape in sums],
            scratch_shapes=[
                pltpu.VMEM((D, FF), f32),
                pltpu.VMEM((FF, D), f32),
                pltpu.VMEM((D, D), f32),
                pltpu.VMEM((PAIRS, 2 * FEATS, 256), f32),
                pltpu.VMEM((ROWS, FF), bf16),
                pltpu.VMEM((ROWS, FF), bf16),
            ],
        ),
        out_shape=[jax.ShapeDtypeStruct(shape, kind) for _, shape, kind in outs]
        + [jax.ShapeDtypeStruct(shape, bf16) for shape in sums],
        compiler_params=params(),
        cost_estimate=cost(48),
        name="middle",
    )(ends, core, x, g, o, rden, pq, seg_rows, gain_rows, *[later] * 6)


def backward_call(at, parts, ends, seg_rows, gather, arrays, *written):
    length = arrays[0].shape[0]
    steps, halo = length // ROWS, SPAN // ROWS
    count = PAIRS // parts
    chosen = range(at * count, (at + 1) * count)

    def falling(shape, at=0):
        rest = (0,) * (len(shape) - 2)
        return pl.BlockSpec(shape, lambda c, *_: (steps - 1 - c, at) + rest)

    def state(at):
        return pl.BlockSpec((1, FEATS, 256), lambda *_: (at, 0, 0), pipeline_mode=pl.Buffered(1))

    specs = [pl.BlockSpec((1, 1, ROWS), lambda c, *_: (steps + halo - 1 - c, 0, 0))]
    specs += [fixed(gather.shape)]
    for shape in ((ROWS, 512),) * 3 + ((ROWS, 384), (ROWS, 256), (ROWS // CHUNK, 1, 256, 256)):
        specs += [falling(shape, p) for p in chosen]
    specs += [state(p) for p in chosen]
    operands = [array for array in arrays for _ in chosen]
    return pl.pallas_call(
        partial(backward_kernel, count),
        grid_spec=pltpu.PrefetchScalarGridSpec(
            num_scalar_prefetch=1,
            grid=(steps,),
            in_specs=specs + [pl.BlockSpec(memory_space=pl.ANY)] * len(written),
            out_specs=falling((ROWS, 384 * count), at),
            scratch_shapes=[
                pltpu.VMEM((count, 2 * FEATS, 256), f32),
                pltpu.VMEM((count, CHUNK, 2 * CHUNK), bf16),
                pltpu.VMEM((2, count, ROWS, 2 * FEATS), bf16),
            ],
        ),
        out_shape=jax.ShapeDtypeStruct((length, 3 * D), bf16),
        input_output_aliases={3 + len(operands): 0} if written else {},
        compiler_params=params(),
        cost_estimate=cost(8 * count),
        name="backward",
    )(ends, seg_rows, gather, *operands, *written)


def input_call(dqkv, wq, x, dy1, gain_rows):
    length = x.shape[0]
    return pl.pallas_call(
        input_kernel,
        grid=(length // ROWS,),
        in_specs=[
            by_step((ROWS, 3 * D)),
            fixed(wq.shape),
            by_step((ROWS, D)),
            by_step((ROWS, D)),
            fixed((8, D)),
        ],
        out_specs=by_step((ROWS, D)),
        out_shape=jax.ShapeDtypeStruct((length, D), f32),
        compiler_params=params(),
        cost_estimate=cost(10),
        name="input_grad",
    )(dqkv, wq, x, dy1, gain_rows)


def per_device(
    inputs,
    cotangent,
    segments,
    feature_matrix,
    w_qkv,
    w_out,
    w_up,
    w_down,
    gains,
    first_qkv,
    second_qkv,
    first_out,
    second_out,
    first_up,
    second_up,
    first_down,
    second_down,
    first_gains,
    second_gains,
    step_count,
):
    heads = lax.axis_size("head")
    row_bits, head_bits = axis_bits()
    x = inputs[0]
    g = cotangent[0]
    length = x.shape[0]
    share = w_qkv.shape[0]
    group = lax.axis_size("row") * share // 16

    packed = jnp.concatenate(
        [
            w_qkv.reshape(share, 3, PAIRS, 128).transpose(0, 2, 1, 3).reshape(share, 3 * D),
            gains,
            jnp.zeros((share, 126), f32),
        ],
        axis=1,
    ).astype(bf16)
    forward_pairs = [(i, i + 1) for i in range(heads - 1)]
    backward_pairs = [(i + 1, i) for i in range(heads - 1)]
    weights = Gather(packed)
    core_bit, *far_bits = head_bits
    order = row_bits[::-1] + far_bits + [core_bit]
    later = jnp.concatenate(
        [w_up[:, 512 * j : 512 * (j + 1)] for j in range(FF // 512)] + [w_down, w_out], axis=0
    ).astype(bf16)
    tail = x[length - SPAN :]
    weights.buf = tied(packed, tail)
    x_ahead = lax.ppermute(tail, "head", forward_pairs)
    weights.start(*order[0])
    weights.finish(later)
    later_own = tied(later, weights.buf)
    later = lax.all_gather(later_own, AXES, axis=0)
    if share != 16:
        parts = 16 // share
        later = later.reshape(D // 16, parts, 9 * share, 512)
        ups = later[:, :, : 4 * share].reshape(D // 16, parts, 4, share, 512)
        ups = ups.transpose(0, 2, 1, 3, 4).reshape(D // 16, 64, 512)
        downs = later[:, :, 4 * share : 8 * share].reshape(D // 16, 64, 512)
        outs = later[:, :, 8 * share :].reshape(D // 16, 16, 512)
        later = jnp.concatenate([ups, downs, outs], axis=1)

    weights.start(*order[1])
    row_segments = tied(segments[0], weights.buf)
    padded = jnp.concatenate([jnp.full((SPAN,), -1, jnp.int32), row_segments])
    near = lax.dynamic_slice_in_dim(padded, lax.axis_index("head") * length, length + SPAN)
    ends = near[CHUNK - 1 :: CHUNK]
    seg_rows = near.astype(f32).reshape(-1, 1, ROWS)
    fm = feature_matrix
    nothing = jnp.zeros_like(fm.T)
    spread = jnp.concatenate(
        [
            jnp.concatenate([fm.T, nothing], axis=1),
            jnp.concatenate([nothing, fm.T], axis=1),
        ],
        axis=0,
    )
    zero = jnp.zeros((FEATS, HD), bf16)
    one = jnp.ones((FEATS, HD), bf16)
    gather = jnp.concatenate(
        [
            jnp.concatenate([fm, zero, one, zero], axis=1),
            jnp.concatenate([zero, fm, zero, one], axis=1),
        ],
        axis=0,
    )
    weights.finish(ends, seg_rows)
    weights.start(*order[2])
    weights.finish(spread, gather, x_ahead)
    for stage in order[3:]:
        weights.start(*stage)
        weights.finish()
    wq = weights.whole()
    core = (lax.axis_index("head") & 1).reshape(1)

    h1, qkv, pq, pk, scores, states, o, rden, gain_rows = forward_call(
        ends, x_ahead, x, seg_rows, wq, spread
    )
    out_act, dy1, dn, sent_up, sent_rest, kept_up, kept_rest, back = middle_call(
        group, ends, core, x, g, o, rden, pq, seg_rows, gain_rows, later
    )
    if share != 16:
        sent_up, kept_up = ups_by_device(sent_up, share), ups_by_device(kept_up, share)
        sent_rest, kept_rest = rest_by_device(sent_rest, share), rest_by_device(kept_rest, share)
    back_in = lax.ppermute(back, "head", backward_pairs)
    came_up = swap(sent_up, "head", 0)
    came_rest = swap(sent_rest, "head", 0)

    def attention_back(at, back_in, *written):
        arrays = (scores, pq, pk, qkv, dn, states, back_in)
        return backward_call(at, 2, ends, seg_rows, gather, arrays, *written)

    lower = [(axis, bit, place - (place > core_bit[2])) for axis, bit, place in far_bits]
    first_order = lower + row_bits[:1]
    second_order = row_bits[:1] + lower
    last_order = row_bits[1:]
    places = [place for _, _, place in first_order + last_order]
    cut = 4 * share

    dqkv = attention_back(0, tied(back_in, sent_up, sent_rest))
    kept_up, kept_rest = tied(kept_up, dqkv), tied(kept_rest, dqkv)
    first = Halving(kept_up, came_up, places)
    second = Halving(kept_rest, came_rest, places)
    back_in = tied(back_in, first.send(*first_order[0]), second.send(*second_order[0]))
    dqkv = attention_back(1, back_in, dqkv)

    moved = []
    for i, (left, right) in enumerate(zip(first_order[1:], second_order[1:])):
        for half, stage in ((first, left), (second, right)):
            half.parts = [tied(part, dqkv) for part in half.parts]
            moved.append(half.send(*stage))
    g_qkv = dot(tied(h1, dqkv, *moved), dqkv, 0, 0).astype(bf16).reshape(heads // 2, 2, -1, 3 * D)
    left, right = [[tied(part, g_qkv) for part in half.parts] for half in (first, second)]
    rest = Halving(jnp.concatenate([left[0], right[0]], axis=-2), None, first.places)
    rest.parts.append(jnp.concatenate([left[1], right[1]], axis=-2))
    moved = rest.send(*last_order[0])
    g_qkv = tied(g_qkv, moved)
    sent_qkv = lax.dynamic_index_in_dim(g_qkv, 1 - core[0], 1, False)
    came_qkv = swap(sent_qkv, "head", 0)
    kept_qkv = tied(lax.dynamic_index_in_dim(g_qkv, core[0], 1, False), *rest.parts)
    merged_qkv = (kept_qkv.astype(f32) + came_qkv.astype(f32)).astype(bf16)
    all_qkv = exchange(merged_qkv.reshape(-1, share, 3 * D))
    dx = input_call(dqkv, wq, x, tied(dy1, merged_qkv), gain_rows)
    for stage in last_order[1:]:
        rest.parts = [tied(part, dx) for part in rest.parts]
        rest.send(*stage)
    kept, came = rest.parts
    count = lax.axis_size(AXES)
    sum_qkv, sums, sum_gains, spread = pl.pallas_call(
        finish_kernel,
        out_shape=[
            jax.ShapeDtypeStruct((share, 3 * D), f32),
            jax.ShapeDtypeStruct((9 * share, 512), f32),
            jax.ShapeDtypeStruct((2, share), f32),
            jax.ShapeDtypeStruct((count, 8, 128), f32),
        ],
        name="finish",
    )(all_qkv, kept, came, packed, later_own)
    sum_qkv = sum_qkv.reshape(share, PAIRS, 3, 128).transpose(0, 2, 1, 3).reshape(share, 3, D)
    sum_up = sums[: 4 * share].reshape(4, share, 512).transpose(1, 0, 2).reshape(share, FF)
    sum_down = sums[4 * share : 8 * share]
    sum_out = sums[8 * share :]
    reduced = lax.optimization_barrier((sum_qkv, sum_out, sum_up, sum_down, sum_gains))
    reduced = reduced[:4] + (reduced[4].T,)
    total_squares = total_of(spread)
    grad_norm = jnp.sqrt(total_squares)
    clip_factor = jnp.minimum(1.0, max_norm / (grad_norm + 1e-06))
    step_value = step_count.astype(f32)
    update = partial(adam_update, clip_factor=clip_factor, step_value=step_value)
    qkv_parts = update(
        w_qkv, reduced[0], first_qkv, second_qkv, step_rate=matrix_rate, decay_rate=matrix_decay
    )
    out_parts = update(
        w_out, reduced[1], first_out, second_out, step_rate=output_rate, decay_rate=matrix_decay
    )
    up_parts = update(
        w_up, reduced[2], first_up, second_up, step_rate=matrix_rate, decay_rate=matrix_decay
    )
    down_parts = update(
        w_down, reduced[3], first_down, second_down, step_rate=matrix_rate, decay_rate=matrix_decay
    )
    gain_parts = update(
        gains, reduced[4], first_gains, second_gains, step_rate=gain_rate, decay_rate=0.0
    )
    return (
        (out_act[None], dx[None], grad_norm)
        + qkv_parts
        + out_parts
        + up_parts
        + down_parts
        + gain_parts
    )


def solution(mesh):
    token = P("row", "head", None)
    three = P(AXES, None, None)
    two = P(AXES, None)
    placed = (token, token, P("row", None), P(), three, two, two, two, two)
    placed = placed + (three, three) + (two,) * 8 + (P(),)
    return jax.shard_map(
        per_device,
        mesh=mesh,
        in_specs=placed,
        out_specs=(token, token, P()) + (three,) * 4 + (two,) * 16,
        check_vma=False,
    )
```

```python
import math
from functools import partial

import jax
import jax.numpy as jnp
from jax import lax
from jax.experimental import pallas as pl
from jax.experimental.pallas import tpu as pltpu
from jax.sharding import PartitionSpec as P

D = 512
HD = 64
FEATS = 256
FF = 2048
CHUNK = 256
SPAN = 1024
ROWS = 512
PAIRS = D // (2 * HD)

bf16 = jnp.bfloat16
f32 = jnp.float32
norm_eps = 1e-06
beta_first = 0.9
beta_second = 0.999
adam_eps = 1e-08
max_norm = 1.0
matrix_rate = 0.08
output_rate = 0.3
gain_rate = 1.5
matrix_decay = 0.1
feature_scale = HD ** (-0.25)
log2e = math.log2(math.e)
AXES = ("head", "row")


def dot(a, b, ca=1, cb=0):
    return lax.dot_general(a, b, (((ca,), (cb,)), ((), ())), preferred_element_type=f32)


def lanes(width):
    return lax.broadcasted_iota(jnp.int32, (1, width), 1)


def half_masks(width):
    first = (lanes(width) % 128 < HD).astype(f32)
    return first.astype(bf16), (1.0 - first).astype(bf16)


def rms_scale(values):
    return lax.rsqrt(jnp.mean(values * values, axis=-1, keepdims=True) + norm_eps)


def features(u, spread):
    raw = dot(u, spread)
    wide = u.astype(f32)
    squares = wide * wide
    own = lanes(2 * HD) < HD
    total_a = jnp.sum(jnp.where(own, squares, 0.0), axis=1, keepdims=True)
    total_b = jnp.sum(jnp.where(own, 0.0, squares), axis=1, keepdims=True)
    c1 = feature_scale * log2e
    c2 = 0.5 * feature_scale * feature_scale * log2e
    down_a = total_a * c2 + 4.0
    down_b = total_b * c2 + 4.0
    left = jnp.exp2(raw[:, :FEATS] * c1 - down_a)
    right = jnp.exp2(raw[:, FEATS:] * c1 - down_b)
    return jnp.concatenate([left, right], axis=1).astype(bf16)


def masked_pair(first, second, width):
    ma, mb = half_masks(width)
    return jnp.concatenate([first * ma, second * mb], axis=0)


def as_column(row):
    return jnp.broadcast_to(row, (8, row.shape[1])).T[:, :1]


def flag(condition):
    return condition.astype(f32).astype(bf16)


def chunk_mask(seg_row):
    seg_col = as_column(seg_row)
    rows = lax.broadcasted_iota(jnp.int32, (CHUNK, CHUNK), 0)
    cols = lax.broadcasted_iota(jnp.int32, (CHUNK, CHUNK), 1)
    return seg_col, flag((rows >= cols) & (seg_col == seg_row))


def forward_kernel(
    ends_ref, xh_ref, xo_ref, seg_ref, wq_ref, spread_ref,
    h1_ref, qkv_ref, pq_ref, pk_ref, p_ref, t_ref, o_ref, rden_ref, gains_ref,
    state_ref,
):
    step = pl.program_id(0)
    halo = SPAN // ROWS
    subs = ROWS // CHUNK
    ones = jnp.ones((ROWS, 2 * HD), bf16)

    @pl.when(step == 0)
    def _():
        state_ref[...] = jnp.zeros_like(state_ref)
        gains_ref[...] = wq_ref[:, 3 * D :].astype(f32).T[:8]

    gain = gains_ref[0:1]

    @pl.when(step < halo)
    def _():
        x = xh_ref[...].astype(f32)
        h1 = (x * rms_scale(x) * gain).astype(bf16)
        chosen = flag(as_column(seg_ref[0]) == ends_ref[halo * subs - 1])
        kvs = [dot(h1, wq_ref[:, 384 * p + 128 : 384 * (p + 1)]).astype(bf16) for p in range(PAIRS)]
        for p in range(PAIRS):
            pk_ref[:, 512 * p : 512 * (p + 1)] = features(kvs[p][:, :128], spread_ref[...])
        for p in range(PAIRS):
            vw = jnp.concatenate([kvs[p][:, 128:], ones], axis=1) * chosen
            state_ref[p] = state_ref[p] + dot(pk_ref[:, 512 * p : 512 * (p + 1)], vw, 0, 0)

    @pl.when(step >= halo)
    def _():
        x = xo_ref[...].astype(f32)
        h1 = (x * rms_scale(x) * gain).astype(bf16)
        h1_ref[...] = h1
        qkv_ref[...] = dot(h1, wq_ref[:, : 3 * D]).astype(bf16)
        for p in range(PAIRS):
            wide = slice(512 * p, 512 * (p + 1))
            pq_ref[:, wide] = features(qkv_ref[:, 384 * p : 384 * p + 128], spread_ref[...])
            pk_ref[:, wide] = features(qkv_ref[:, 384 * p + 128 : 384 * p + 256], spread_ref[...])
        seg = seg_ref[0]
        for j in range(subs):
            rows = slice(CHUNK * j, CHUNK * (j + 1))
            _, allowed = chunk_mask(seg[:, rows])
            for h in range(2 * PAIRS):
                cut = slice(FEATS * h, FEATS * (h + 1))
                p_ref[rows, CHUNK * h : CHUNK * (h + 1)] = (
                    dot(pq_ref[rows, cut], pk_ref[rows, cut], 1, 1).astype(bf16) * allowed
                )
        seg_col = as_column(seg)
        for j in range(subs):
            rows = slice(CHUNK * j, CHUNK * (j + 1))
            before = ends_ref[step * subs + j - 1]
            last = ends_ref[step * subs + j]
            chosen = flag(seg_col[rows] == last)
            follows = flag(seg_col[rows] == before)
            keep = (last == before).astype(f32)
            for p in range(PAIRS):
                cut = slice(128 * p, 128 * (p + 1))
                wide = slice(512 * p, 512 * (p + 1))
                v2 = qkv_ref[rows, 384 * p + 256 : 384 * p + 384]
                v1 = jnp.concatenate([v2, ones[:CHUNK]], axis=1)
                state = state_ref[p]
                narrow = state.astype(bf16)
                narrow = masked_pair(narrow[:FEATS], narrow[FEATS:], 256)
                t_ref[j, p] = narrow[:FEATS] + narrow[FEATS:]
                both = dot(p_ref[rows, wide], masked_pair(v1, v1, 256)) + dot(
                    pq_ref[rows, wide] * follows, narrow
                )
                state_ref[p] = keep * state + dot(pk_ref[rows, wide], v1 * chosen, 0, 0)
                rden = 1.0 / both[:, 128:]
                rden_ref[rows, cut] = rden
                o_ref[rows, cut] = (both[:, :128] * rden).astype(bf16)


def middle_kernel(
    group,
    ends_ref, core_ref, x_ref, g_ref, o_ref, rden_ref, pq_ref, seg_ref, gains_ref,
    wu0_ref, wu1_ref, wu2_ref, wu3_ref, wd_ref, wo_ref,
    out_ref, dy1_ref, dn_ref, sent_up_ref, sent_rest_ref, kept_up_ref, kept_rest_ref, back_ref,
    up_acc, down_acc, out_acc, back_acc, act_ref, dup_ref,
):
    step = pl.program_id(0)
    steps = pl.num_programs(0)
    cut = 512
    wu_refs = (wu0_ref, wu1_ref, wu2_ref, wu3_ref)
    blocks = wd_ref.shape[0] // len(wu_refs)

    @pl.when(step == 0)
    def _():
        back_acc[...] = jnp.zeros_like(back_acc)

    def so_far(value):
        return jnp.where(step == 0, 0.0, value)

    o = o_ref[...]
    g = g_ref[...]
    gain = gains_ref[1:2]
    wo = wo_ref[...].reshape(D, D)
    y1 = x_ref[...].astype(f32) + dot(o, wo, 1, 1)
    r2 = rms_scale(y1)
    n2 = y1 * r2
    h2 = (n2 * gain).astype(bf16)
    for f in range(FF // cut):
        fs = slice(cut * f, cut * (f + 1))
        wd = wd_ref[blocks * f : blocks * (f + 1)].reshape(cut, D)
        up = dot(h2, wu_refs[f][...].reshape(D, cut))
        d_act = dot(g, wd, 1, 1)
        cdf = 0.5 * (1.0 + lax.erf(up * math.sqrt(0.5)))
        density = jnp.exp(up * up * -0.5) * (1.0 / math.sqrt(2.0 * math.pi))
        act = (up * cdf).astype(bf16)
        d_up = (d_act * (cdf + up * density)).astype(bf16)
        act_ref[:, fs] = act
        dup_ref[:, fs] = d_up
        down_acc[fs, :] = so_far(down_acc[fs, :]) + dot(act, g, 0, 0)
        up_acc[:, fs] = so_far(up_acc[:, fs]) + dot(h2, d_up, 0, 0)
    out_ref[...] = (y1 + dot(act_ref[...], wd_ref[...].reshape(FF, D))).astype(bf16)
    d_h2 = dot(dup_ref[:, :cut], wu0_ref[...].reshape(D, cut), 1, 1)
    for f in range(1, FF // cut):
        d_h2 = d_h2 + dot(
            dup_ref[:, cut * f : cut * (f + 1)], wu_refs[f][...].reshape(D, cut), 1, 1
        )
    e2 = d_h2 * gain
    dy1 = g.astype(f32) + r2 * (e2 - n2 * jnp.mean(e2 * n2, axis=-1, keepdims=True))
    dy1_ref[...] = dy1
    da = dy1.astype(bf16)
    out_acc[...] = so_far(out_acc[...]) + dot(da, o, 0, 0)
    d_o = dot(da, wo)
    product = d_o * o.astype(f32)
    high = product.astype(bf16)
    low = (product - high.astype(f32)).astype(bf16)
    rden = rden_ref[...]
    ma, mb = half_masks(128)
    same = jnp.concatenate(
        [jnp.broadcast_to(ma, (HD, 128)), jnp.broadcast_to(mb, (HD, 128))], axis=0
    )
    same = jnp.concatenate([same, same], axis=0)
    lane = lanes(128) % HD
    m0 = (lane == 0).astype(f32).astype(bf16)
    m1 = (lane == 1).astype(f32).astype(bf16)
    for p in range(PAIRS):
        ps = slice(128 * p, 128 * (p + 1))
        total = dot(jnp.concatenate([high[:, ps], low[:, ps]], axis=1), same)
        d_den = -total * rden[:, ps]
        d_hi = d_den.astype(bf16)
        d_lo = (d_den - d_hi.astype(f32)).astype(bf16)
        d_num = (d_o[:, ps] * rden[:, ps]).astype(bf16)
        dn = jnp.concatenate([d_num, d_hi * m0 + d_lo * m1], axis=1)
        dn_ref[:, 256 * p : 256 * (p + 1)] = dn

    @pl.when(step < SPAN // ROWS)
    def _():
        follows = flag(as_column(seg_ref[0]) == ends_ref[SPAN // CHUNK - 1])
        for p in range(PAIRS):
            back_acc[p] = back_acc[p] + dot(
                pq_ref[:, 512 * p : 512 * (p + 1)], dn_ref[:, 256 * p : 256 * (p + 1)] * follows, 0, 0
            )

    @pl.when(step == steps - 1)
    def _():
        core = core_ref[0]
        for ups, others, side in (
            (sent_up_ref, sent_rest_ref, 1 - core),
            (kept_up_ref, kept_rest_ref, core),
        ):
            for far in range(ups.shape[0] // group):
                at = (2 * far + side) * group
                here = slice(group * far, group * (far + 1))
                thin = pl.ds(pl.multiple_of(at * 16, 16), group * 16)
                tall = pl.ds(pl.multiple_of(at * 64, 64), group * 64)
                for f in range(FF // cut):
                    piece = up_acc[thin, cut * f : cut * (f + 1)].astype(bf16)
                    ups[here, 16 * f : 16 * (f + 1)] = piece.reshape(group, 16, cut)
                others[here, :64] = down_acc[tall].astype(bf16).reshape(group, 64, D)
                others[here, 64:] = out_acc[thin].astype(bf16).reshape(group, 16, D)
        ma, mb = half_masks(128)
        for p in range(PAIRS):
            first, second = back_acc[p, :FEATS], back_acc[p, FEATS:]
            back_ref[p, :FEATS] = first[:, :128].astype(bf16) * ma + second[:, :128].astype(bf16) * mb
            rows = []
            for side, lane in ((first, 0), (second, HD)):
                turned = side[:, 128:].T
                total = turned[lane : lane + 1] + turned[lane + 1 : lane + 2]
                high = total.astype(bf16).astype(f32)
                for part in (high, total - high):
                    rows += [part[:, :128], part[:, 128:]]
            rows.append(jnp.zeros((8, 128), f32))
            back_ref[p, FEATS:] = jnp.concatenate(rows, axis=0).astype(bf16)


def backward_kernel(pairs, ends_ref, seg_ref, gather_ref, *refs):
    refs = refs[: 7 * pairs] + refs[-4:]
    subs = ROWS // CHUNK
    step = pl.program_id(0)
    steps = pl.num_programs(0)
    at = (SPAN // ROWS + steps - 1 - step) * subs
    dqkv_ref, state_ref, grad_ref, logit_ref = refs[7 * pairs :]
    p_refs, pq_refs, pk_refs, qkv_refs, dn_refs, t_refs, back_refs = [
        refs[i * pairs : (i + 1) * pairs] for i in range(7)
    ]

    @pl.when(step == 0)
    def _():
        lane = lanes(128)
        for p in range(pairs):
            extra = back_refs[p][0, FEATS:].astype(f32)
            for i, mask in enumerate(half_masks(128)):
                rows = slice(FEATS * i, FEATS * (i + 1))
                state_ref[p, rows, :128] = (back_refs[p][0, :FEATS] * mask).astype(f32)
                total = jnp.zeros((FEATS, 128), f32)
                for t in range(2):
                    at_row = 4 * i + 2 * t
                    row = jnp.concatenate([extra[at_row : at_row + 1], extra[at_row + 1 : at_row + 2]], axis=1)
                    total = jnp.where(lane == HD * i + t, as_column(row), total)
                state_ref[p, rows, 128:] = total

    seg = seg_ref[0]
    seg_col = as_column(seg)
    two = jnp.broadcast_to(flag(lanes(128) % HD < 2), (CHUNK, 128))
    ones = jnp.ones((CHUNK, 128), bf16)
    ma, mb = half_masks(128)
    for j in reversed(range(subs)):
        rows = slice(CHUNK * j, CHUNK * (j + 1))
        _, allowed = chunk_mask(seg[:, rows])
        before = ends_ref[at + j - 1]
        last = ends_ref[at + j]
        chosen = flag(seg_col[rows] == last)
        follows = flag(seg_col[rows] == before)
        keep = (last == before).astype(f32)
        for p in range(pairs):
            v1 = jnp.concatenate([qkv_refs[p][rows, 256:], two], axis=1)
            d_p = dot(dn_refs[p][rows], masked_pair(v1, v1, 256), 1, 1).astype(bf16)
            grad_ref[p, :, :CHUNK] = d_p[:, :CHUNK] * allowed
            grad_ref[p, :, CHUNK:] = d_p[:, CHUNK:] * allowed
        for p in range(pairs):
            pq, pk, dn = pq_refs[p][rows], pk_refs[p][rows], dn_refs[p][rows]
            scores = p_refs[p][rows]
            v2 = qkv_refs[p][rows, 256:]
            compact = t_refs[p][j, 0]
            narrow = masked_pair(compact, compact, 256)
            state = state_ref[p]
            back = state.astype(bf16)
            back = masked_pair(back[:FEATS], back[FEATS:], 256)
            d_pa = grad_ref[p, :, :CHUNK]
            d_pb = grad_ref[p, :, CHUNK:]
            dn_f = dn * follows
            d_pq = dot(dn_f, narrow, 1, 1) + jnp.concatenate(
                [dot(d_pa, pk[:, :FEATS]), dot(d_pb, pk[:, FEATS:])], axis=1
            )
            logit_ref[0, p, rows] = d_pq.astype(bf16) * pq
            vw = jnp.concatenate([v2, ones], axis=1) * chosen
            d_pk = dot(vw, back, 1, 1) + jnp.concatenate(
                [dot(d_pa, pq[:, :FEATS], 0, 0), dot(d_pb, pq[:, FEATS:], 0, 0)], axis=1
            )
            logit_ref[1, p, rows] = d_pk.astype(bf16) * pk
            d_num = dn[:, :128]
            d_v = (
                dot(pk * chosen, back[:, :128])
                + dot(scores[:, :CHUNK], d_num * ma, 0, 0)
                + dot(scores[:, CHUNK:], d_num * mb, 0, 0)
            )
            dqkv_ref[rows, 384 * p + 256 : 384 * p + 384] = d_v.astype(bf16)
            state_ref[p] = keep * state + dot(pq, dn_f, 0, 0)
    scale2 = feature_scale * feature_scale
    for p in range(pairs):
        for i in range(2):
            u = qkv_refs[p][:, 128 * i : 128 * (i + 1)].astype(f32)
            through = dot(logit_ref[i, p], gather_ref[...])
            d_u = through[:, :128] * feature_scale - u * through[:, 128:] * scale2
            dqkv_ref[:, 384 * p + 128 * i : 384 * p + 128 * (i + 1)] = d_u.astype(bf16)


def input_kernel(dqkv_ref, wq_ref, x_ref, dy1_ref, gains_ref, dx_ref):
    d_h1 = dot(dqkv_ref[...], wq_ref[:, : 3 * D], 1, 1)
    x = x_ref[...].astype(f32)
    r1 = rms_scale(x)
    n1 = x * r1
    e1 = d_h1 * gains_ref[0:1]
    dx_ref[...] = dy1_ref[...] + r1 * (e1 - n1 * jnp.mean(e1 * n1, axis=-1, keepdims=True))


def finish_kernel(q_ref, kept_ref, came_ref, packed_ref, later_ref, sq_ref, sr_ref, gg_ref, spread_ref):
    share = q_ref.shape[1]
    sum_q = jnp.sum(q_ref[...].astype(f32), axis=0)
    sum_r = kept_ref[...].astype(f32) + came_ref[...].astype(f32)
    sq_ref[...] = sum_q
    sr_ref[...] = sum_r
    packed = packed_ref[...].astype(f32)
    tops = jnp.sum(packed[:, : 3 * D] * sum_q, axis=1, keepdims=True)
    rows = jnp.sum(later_ref[: 4 * share].astype(f32) * sum_r[: 4 * share], axis=1, keepdims=True)
    lows = rows[:share]
    for f in range(1, 4):
        lows = lows + rows[share * f : share * (f + 1)]
    gg = jnp.concatenate([tops, lows], axis=1) / packed[:, 3 * D : 3 * D + 2]
    gg_ref[...] = jnp.concatenate([gg, jnp.zeros((share, 126), f32)], axis=1).T[:2]
    total = jnp.sum(sum_q * sum_q) + jnp.sum(sum_r * sum_r) + jnp.sum(gg * gg)
    spread_ref[...] = jnp.full(spread_ref.shape, total, f32)


def axis_bits():
    row_bits = (lax.axis_size("row") - 1).bit_length()
    head_bits = (lax.axis_size("head") - 1).bit_length()
    row = [("row", b, b) for b in range(row_bits)]
    head = [("head", b, row_bits + b) for b in range(head_bits)]
    return row, head


def swap(value, axis, bit):
    size = lax.axis_size(axis)
    return lax.ppermute(value, axis, [(i, i ^ (1 << bit)) for i in range(size)])


def tied(value, *others):
    return lax.optimization_barrier((value,) + others)[0]


class Gather:
    def __init__(self, shard):
        self.shape = shard.shape
        self.buf = shard
        self.held = []

    def start(self, axis, bit, place):
        self.came = swap(self.buf, axis, bit)
        self.mine = (lax.axis_index(axis) >> bit) & 1
        self.place = place

    def finish(self, *others):
        own = tied(self.buf, *others) if others else self.buf
        at = sum(1 for h in self.held if h > self.place)
        self.buf = jnp.where(
            self.mine == 0,
            jnp.stack([own, self.came], axis=at),
            jnp.stack([self.came, own], axis=at),
        )
        self.held = sorted(self.held + [self.place], reverse=True)

    def whole(self):
        return self.buf.reshape((-1,) + self.shape[1:])


class Halving:
    def __init__(self, kept, came, places):
        self.places = sorted(places, reverse=True)
        self.parts = [kept] if came is None else [kept, came]
        self.parts = [self.split(part) for part in self.parts]

    def split(self, part):
        inner = part.shape[1:] if part.ndim == 3 else part.shape[-2:]
        return part.reshape((2,) * len(self.places) + inner)

    def take(self, index, at):
        total = sum(
            lax.dynamic_index_in_dim(part, index, at, keepdims=False).astype(f32)
            for part in self.parts
        )
        return total.astype(bf16)

    def after(self, *others):
        self.parts[0] = tied(self.parts[0], *others)
        return self

    def send(self, axis, bit, place):
        at = self.places.index(place)
        mine = (lax.axis_index(axis) >> bit) & 1
        sent = self.take(1 - mine, at)
        came = swap(sent, axis, bit)
        self.parts = [self.take(mine, at), came]
        self.places.remove(place)
        return sent

    def total(self):
        return sum(part.astype(f32) for part in self.parts)


def ups_by_device(blocks, share):
    ups = blocks.reshape(-1, 4, 16 // share, share, 512)
    return ups.transpose(0, 2, 1, 3, 4).reshape(-1, 4 * share, 512)


def rest_by_device(blocks, share):
    downs = blocks[:, :64].reshape(-1, 4 * share, 512)
    outs = blocks[:, 64:].reshape(-1, share, 512)
    return jnp.concatenate([downs, outs], axis=1)


def core_groups():
    heads, rows = lax.axis_size("head"), lax.axis_size("row")
    return [[h * rows + r for h in range(c, heads, 2) for r in range(rows)] for c in (0, 1)]


def exchange(blocks):
    return lax.all_to_all(
        blocks, AXES, split_axis=0, concat_axis=0, axis_index_groups=core_groups(), tiled=True
    )


def total_of(spread):
    came = lax.all_to_all(spread, AXES, split_axis=0, concat_axis=0, tiled=True)
    return jnp.sum(came[:, 0, 0])


def adam_update(
    weight, gradient, first_moment, second_moment, clip_factor, step_value, step_rate, decay_rate
):
    clipped = gradient * clip_factor
    next_first = beta_first * first_moment + (1.0 - beta_first) * clipped
    next_second = beta_second * second_moment + (1.0 - beta_second) * clipped * clipped
    first_hat = next_first / (1.0 - beta_first**step_value)
    second_hat = next_second / (1.0 - beta_second**step_value)
    updated = weight - step_rate * (
        first_hat / (jnp.sqrt(second_hat) + adam_eps) + decay_rate * weight
    )
    return (clipped, next_first, next_second, updated)


def params(limit=60):
    return pltpu.CompilerParams(
        dimension_semantics=("arbitrary",), vmem_limit_bytes=limit << 20
    )


def cost(us):
    return pl.CostEstimate(flops=us * 50000000, transcendentals=0, bytes_accessed=us * 150000)


def fixed(shape):
    zeros = (0,) * len(shape)
    return pl.BlockSpec(shape, lambda *_: zeros, pipeline_mode=pl.Buffered(1))


def first_at(shape, offset):
    rest = (0,) * (len(shape) - 1)
    return pl.BlockSpec(shape, lambda c, *_: (jnp.maximum(c - offset, 0),) + rest)


def by_step(shape):
    return first_at(shape, 0)


def forward_call(ends, x_ahead, x, seg_rows, wq, spread):
    length = x.shape[0]
    chunks, halo, wide = length // CHUNK, SPAN // ROWS, PAIRS * 2 * FEATS
    own = partial(first_at, offset=halo)
    outs = [
        ((ROWS, D), (length, D), bf16),
        ((ROWS, 3 * D), (length, 3 * D), bf16),
        ((ROWS, wide), (length, wide), bf16),
        ((ROWS, wide), (length, wide), bf16),
        ((ROWS, wide), (length, wide), bf16),
        ((ROWS // CHUNK, PAIRS, FEATS, 256), (chunks, PAIRS, FEATS, 256), bf16),
        ((ROWS, D), (length, D), bf16),
        ((ROWS, D), (length, D), f32),
    ]
    return pl.pallas_call(
        forward_kernel,
        grid_spec=pltpu.PrefetchScalarGridSpec(
            num_scalar_prefetch=1,
            grid=(halo + length // ROWS,),
            in_specs=[
                pl.BlockSpec((ROWS, D), lambda c, *_: (jnp.minimum(c, halo - 1), 0)),
                own((ROWS, D)),
                by_step((1, 1, ROWS)),
                fixed(wq.shape),
                fixed(spread.shape),
            ],
            out_specs=[own(block) for block, _, _ in outs] + [fixed((8, D))],
            scratch_shapes=[pltpu.VMEM((PAIRS, 2 * FEATS, 256), f32)],
        ),
        out_shape=[jax.ShapeDtypeStruct(shape, kind) for _, shape, kind in outs]
        + [jax.ShapeDtypeStruct((8, D), f32)],
        compiler_params=params(),
        cost_estimate=cost(35),
        name="forward",
    )(ends, x_ahead, x, seg_rows, wq, spread)


def middle_call(group, ends, core, x, g, o, rden, pq, seg_rows, gain_rows, later):
    length, wide = x.shape[0], pq.shape[1]
    near_steps = SPAN // ROWS
    by_step_ahead = pl.BlockSpec((1, 1, ROWS), lambda c, *_: (c + near_steps, 0, 0))

    def columns(block, height=16):
        return pl.BlockSpec(
            (D // 16, height, 512), lambda *_: (0, block, 0), pipeline_mode=pl.Buffered(1)
        )

    outs = [
        ((ROWS, D), (length, D), bf16),
        ((ROWS, D), (length, D), f32),
        ((ROWS, PAIRS * 256), (length, PAIRS * 256), bf16),
    ]
    sums = [(D // 32, 64, 512), (D // 32, 80, 512)] * 2 + [(PAIRS, FEATS + 16, 128)]
    return pl.pallas_call(
        partial(middle_kernel, group),
        grid_spec=pltpu.PrefetchScalarGridSpec(
            num_scalar_prefetch=2,
            grid=(length // ROWS,),
            in_specs=[by_step((ROWS, D))] * 4
            + [
                pl.BlockSpec((ROWS, wide), lambda c, *_: (jnp.minimum(c, near_steps - 1), 0)),
                by_step_ahead,
                fixed((8, D)),
            ]
            + [columns(f) for f in range(4)]
            + [columns(1, 64), columns(8)],
            out_specs=[by_step(block) for block, _, _ in outs] + [fixed(shape) for shape in sums],
            scratch_shapes=[
                pltpu.VMEM((D, FF), f32),
                pltpu.VMEM((FF, D), f32),
                pltpu.VMEM((D, D), f32),
                pltpu.VMEM((PAIRS, 2 * FEATS, 256), f32),
                pltpu.VMEM((ROWS, FF), bf16),
                pltpu.VMEM((ROWS, FF), bf16),
            ],
        ),
        out_shape=[jax.ShapeDtypeStruct(shape, kind) for _, shape, kind in outs]
        + [jax.ShapeDtypeStruct(shape, bf16) for shape in sums],
        compiler_params=params(),
        cost_estimate=cost(48),
        name="middle",
    )(ends, core, x, g, o, rden, pq, seg_rows, gain_rows, *[later] * 6)


def backward_call(at, parts, ends, seg_rows, gather, arrays, *written):
    length = arrays[0].shape[0]
    steps, halo = length // ROWS, SPAN // ROWS
    count = PAIRS // parts
    chosen = range(at * count, (at + 1) * count)

    def falling(shape, at=0):
        rest = (0,) * (len(shape) - 2)
        return pl.BlockSpec(shape, lambda c, *_: (steps - 1 - c, at) + rest)

    def state(at):
        return pl.BlockSpec(
            (1, FEATS + 16, 128), lambda *_: (at, 0, 0), pipeline_mode=pl.Buffered(1)
        )

    specs = [pl.BlockSpec((1, 1, ROWS), lambda c, *_: (steps + halo - 1 - c, 0, 0))]
    specs += [fixed(gather.shape)]
    for shape in ((ROWS, 512),) * 3 + ((ROWS, 384), (ROWS, 256), (ROWS // CHUNK, 1, 256, 256)):
        specs += [falling(shape, p) for p in chosen]
    specs += [state(p) for p in chosen]
    operands = [array for array in arrays for _ in chosen]
    return pl.pallas_call(
        partial(backward_kernel, count),
        grid_spec=pltpu.PrefetchScalarGridSpec(
            num_scalar_prefetch=1,
            grid=(steps,),
            in_specs=specs + [pl.BlockSpec(memory_space=pl.ANY)] * len(written),
            out_specs=falling((ROWS, 384 * count), at),
            scratch_shapes=[
                pltpu.VMEM((count, 2 * FEATS, 256), f32),
                pltpu.VMEM((count, CHUNK, 2 * CHUNK), bf16),
                pltpu.VMEM((2, count, ROWS, 2 * FEATS), bf16),
            ],
        ),
        out_shape=jax.ShapeDtypeStruct((length, 3 * D), bf16),
        input_output_aliases={3 + len(operands): 0} if written else {},
        compiler_params=params(),
        cost_estimate=cost(8 * count),
        name="backward",
    )(ends, seg_rows, gather, *operands, *written)


def input_call(dqkv, wq, x, dy1, gain_rows):
    length = x.shape[0]
    return pl.pallas_call(
        input_kernel,
        grid=(length // ROWS,),
        in_specs=[
            by_step((ROWS, 3 * D)),
            fixed(wq.shape),
            by_step((ROWS, D)),
            by_step((ROWS, D)),
            fixed((8, D)),
        ],
        out_specs=by_step((ROWS, D)),
        out_shape=jax.ShapeDtypeStruct((length, D), f32),
        compiler_params=params(),
        cost_estimate=cost(10),
        name="input_grad",
    )(dqkv, wq, x, dy1, gain_rows)


def per_device(
    inputs,
    cotangent,
    segments,
    feature_matrix,
    w_qkv,
    w_out,
    w_up,
    w_down,
    gains,
    first_qkv,
    second_qkv,
    first_out,
    second_out,
    first_up,
    second_up,
    first_down,
    second_down,
    first_gains,
    second_gains,
    step_count,
):
    heads = lax.axis_size("head")
    row_bits, head_bits = axis_bits()
    x = inputs[0]
    g = cotangent[0]
    length = x.shape[0]
    share = w_qkv.shape[0]
    group = lax.axis_size("row") * share // 16

    packed = jnp.concatenate(
        [
            w_qkv.reshape(share, 3, PAIRS, 128).transpose(0, 2, 1, 3).reshape(share, 3 * D),
            gains,
            jnp.zeros((share, 126), f32),
        ],
        axis=1,
    ).astype(bf16)
    forward_pairs = [(i, i + 1) for i in range(heads - 1)]
    backward_pairs = [(i + 1, i) for i in range(heads - 1)]
    weights = Gather(packed)
    core_bit, *far_bits = head_bits
    order = row_bits[::-1] + far_bits + [core_bit]
    later = jnp.concatenate(
        [w_up[:, 512 * j : 512 * (j + 1)] for j in range(FF // 512)] + [w_down, w_out], axis=0
    ).astype(bf16)
    tail = x[length - SPAN :]
    weights.buf = tied(packed, tail)
    x_ahead = lax.ppermute(tail, "head", forward_pairs)
    weights.start(*order[0])
    weights.finish(later)
    later_own = tied(later, weights.buf)
    later = lax.all_gather(later_own, AXES, axis=0)
    if share != 16:
        parts = 16 // share
        later = later.reshape(D // 16, parts, 9 * share, 512)
        ups = later[:, :, : 4 * share].reshape(D // 16, parts, 4, share, 512)
        ups = ups.transpose(0, 2, 1, 3, 4).reshape(D // 16, 64, 512)
        downs = later[:, :, 4 * share : 8 * share].reshape(D // 16, 64, 512)
        outs = later[:, :, 8 * share :].reshape(D // 16, 16, 512)
        later = jnp.concatenate([ups, downs, outs], axis=1)

    weights.start(*order[1])
    row_segments = tied(segments[0], weights.buf)
    padded = jnp.concatenate([jnp.full((SPAN,), -1, jnp.int32), row_segments])
    near = lax.dynamic_slice_in_dim(padded, lax.axis_index("head") * length, length + SPAN)
    ends = near[CHUNK - 1 :: CHUNK]
    seg_rows = near.astype(f32).reshape(-1, 1, ROWS)
    fm = feature_matrix
    nothing = jnp.zeros_like(fm.T)
    spread = jnp.concatenate(
        [
            jnp.concatenate([fm.T, nothing], axis=1),
            jnp.concatenate([nothing, fm.T], axis=1),
        ],
        axis=0,
    )
    zero = jnp.zeros((FEATS, HD), bf16)
    one = jnp.ones((FEATS, HD), bf16)
    gather = jnp.concatenate(
        [
            jnp.concatenate([fm, zero, one, zero], axis=1),
            jnp.concatenate([zero, fm, zero, one], axis=1),
        ],
        axis=0,
    )
    weights.finish(ends, seg_rows)
    weights.start(*order[2])
    weights.finish(spread, gather, x_ahead)
    for stage in order[3:]:
        weights.start(*stage)
        weights.finish()
    wq = weights.whole()
    core = (lax.axis_index("head") & 1).reshape(1)

    h1, qkv, pq, pk, scores, states, o, rden, gain_rows = forward_call(
        ends, x_ahead, x, seg_rows, wq, spread
    )
    out_act, dy1, dn, sent_up, sent_rest, kept_up, kept_rest, back = middle_call(
        group, ends, core, x, g, o, rden, pq, seg_rows, gain_rows, later
    )
    if share != 16:
        sent_up, kept_up = ups_by_device(sent_up, share), ups_by_device(kept_up, share)
        sent_rest, kept_rest = rest_by_device(sent_rest, share), rest_by_device(kept_rest, share)
    back_in = lax.ppermute(back, "head", backward_pairs)
    came_up = swap(sent_up, "head", 0)
    came_rest = swap(sent_rest, "head", 0)

    def attention_back(at, back_in, *written):
        arrays = (scores, pq, pk, qkv, dn, states, back_in)
        return backward_call(at, 1, ends, seg_rows, gather, arrays, *written)

    lower = [(axis, bit, place - (place > core_bit[2])) for axis, bit, place in far_bits]
    first_order = lower + row_bits[:1]
    second_order = row_bits[:1] + lower
    last_order = row_bits[1:]
    places = [place for _, _, place in first_order + last_order]
    cut = 4 * share

    kept_up, kept_rest = tied(kept_up, back_in), tied(kept_rest, back_in)
    first = Halving(kept_up, came_up, places)
    second = Halving(kept_rest, came_rest, places)
    back_in = tied(back_in, first.send(*first_order[0]), second.send(*second_order[0]))
    dqkv = attention_back(0, back_in)

    moved = []
    for i, (left, right) in enumerate(zip(first_order[1:], second_order[1:])):
        for half, stage in ((first, left), (second, right)):
            half.parts = [tied(part, dqkv) for part in half.parts]
            moved.append(half.send(*stage))
    g_qkv = dot(tied(h1, dqkv, *moved), dqkv, 0, 0).astype(bf16).reshape(heads // 2, 2, -1, 3 * D)
    left, right = [[tied(part, g_qkv) for part in half.parts] for half in (first, second)]
    rest = Halving(jnp.concatenate([left[0], right[0]], axis=-2), None, first.places)
    rest.parts.append(jnp.concatenate([left[1], right[1]], axis=-2))
    moved = rest.send(*last_order[0])
    g_qkv = tied(g_qkv, moved)
    sent_qkv = lax.dynamic_index_in_dim(g_qkv, 1 - core[0], 1, False)
    came_qkv = swap(sent_qkv, "head", 0)
    kept_qkv = tied(lax.dynamic_index_in_dim(g_qkv, core[0], 1, False), *rest.parts)
    merged_qkv = (kept_qkv.astype(f32) + came_qkv.astype(f32)).astype(bf16)
    all_qkv = exchange(merged_qkv.reshape(-1, share, 3 * D))
    dx = input_call(dqkv, wq, x, tied(dy1, merged_qkv), gain_rows)
    for stage in last_order[1:]:
        rest.parts = [tied(part, dx) for part in rest.parts]
        rest.send(*stage)
    kept, came = rest.parts
    count = lax.axis_size(AXES)
    sum_qkv, sums, sum_gains, spread = pl.pallas_call(
        finish_kernel,
        out_shape=[
            jax.ShapeDtypeStruct((share, 3 * D), f32),
            jax.ShapeDtypeStruct((9 * share, 512), f32),
            jax.ShapeDtypeStruct((2, share), f32),
            jax.ShapeDtypeStruct((count, 8, 128), f32),
        ],
        name="finish",
    )(all_qkv, kept, came, packed, later_own)
    sum_qkv = sum_qkv.reshape(share, PAIRS, 3, 128).transpose(0, 2, 1, 3).reshape(share, 3, D)
    sum_up = sums[: 4 * share].reshape(4, share, 512).transpose(1, 0, 2).reshape(share, FF)
    sum_down = sums[4 * share : 8 * share]
    sum_out = sums[8 * share :]
    reduced = lax.optimization_barrier((sum_qkv, sum_out, sum_up, sum_down, sum_gains))
    reduced = reduced[:4] + (reduced[4].T,)
    total_squares = total_of(spread)
    grad_norm = jnp.sqrt(total_squares)
    clip_factor = jnp.minimum(1.0, max_norm / (grad_norm + 1e-06))
    step_value = step_count.astype(f32)
    update = partial(adam_update, clip_factor=clip_factor, step_value=step_value)
    qkv_parts = update(
        w_qkv, reduced[0], first_qkv, second_qkv, step_rate=matrix_rate, decay_rate=matrix_decay
    )
    out_parts = update(
        w_out, reduced[1], first_out, second_out, step_rate=output_rate, decay_rate=matrix_decay
    )
    up_parts = update(
        w_up, reduced[2], first_up, second_up, step_rate=matrix_rate, decay_rate=matrix_decay
    )
    down_parts = update(
        w_down, reduced[3], first_down, second_down, step_rate=matrix_rate, decay_rate=matrix_decay
    )
    gain_parts = update(
        gains, reduced[4], first_gains, second_gains, step_rate=gain_rate, decay_rate=0.0
    )
    return (
        (out_act[None], dx[None], grad_norm)
        + qkv_parts
        + out_parts
        + up_parts
        + down_parts
        + gain_parts
    )


def solution(mesh):
    token = P("row", "head", None)
    three = P(AXES, None, None)
    two = P(AXES, None)
    placed = (token, token, P("row", None), P(), three, two, two, two, two)
    placed = placed + (three, three) + (two,) * 8 + (P(),)
    return jax.shard_map(
        per_device,
        mesh=mesh,
        in_specs=placed,
        out_specs=(token, token, P()) + (three,) * 4 + (two,) * 16,
        check_vma=False,
    )
```

```python
import math
from functools import partial

import jax
import jax.numpy as jnp
from jax import lax
from jax.experimental import pallas as pl
from jax.experimental.pallas import tpu as pltpu
from jax.sharding import PartitionSpec as P

D = 512
HD = 64
FEATS = 256
FF = 2048
CHUNK = 256
SPAN = 1024
ROWS = 512
PAIRS = D // (2 * HD)

bf16 = jnp.bfloat16
f32 = jnp.float32
norm_eps = 1e-06
beta_first = 0.9
beta_second = 0.999
adam_eps = 1e-08
max_norm = 1.0
matrix_rate = 0.08
output_rate = 0.3
gain_rate = 1.5
matrix_decay = 0.1
feature_scale = HD ** (-0.25)
log2e = math.log2(math.e)
AXES = ("head", "row")


def dot(a, b, ca=1, cb=0):
    return lax.dot_general(a, b, (((ca,), (cb,)), ((), ())), preferred_element_type=f32)


def lanes(width):
    return lax.broadcasted_iota(jnp.int32, (1, width), 1)


def half_masks(width):
    first = (lanes(width) % 128 < HD).astype(f32)
    return first.astype(bf16), (1.0 - first).astype(bf16)


def rms_scale(values):
    return lax.rsqrt(jnp.mean(values * values, axis=-1, keepdims=True) + norm_eps)


def features(u, spread):
    raw = dot(u, spread)
    wide = u.astype(f32)
    squares = wide * wide
    own = lanes(2 * HD) < HD
    total_a = jnp.sum(jnp.where(own, squares, 0.0), axis=1, keepdims=True)
    total_b = jnp.sum(jnp.where(own, 0.0, squares), axis=1, keepdims=True)
    c1 = feature_scale * log2e
    c2 = 0.5 * feature_scale * feature_scale * log2e
    down_a = total_a * c2 + 4.0
    down_b = total_b * c2 + 4.0
    left = jnp.exp2(raw[:, :FEATS] * c1 - down_a)
    right = jnp.exp2(raw[:, FEATS:] * c1 - down_b)
    return jnp.concatenate([left, right], axis=1).astype(bf16)


def masked_pair(first, second, width):
    ma, mb = half_masks(width)
    return jnp.concatenate([first * ma, second * mb], axis=0)


def as_column(row):
    return jnp.broadcast_to(row, (8, row.shape[1])).T[:, :1]


def flag(condition):
    return condition.astype(f32).astype(bf16)


def chunk_mask(seg_row):
    seg_col = as_column(seg_row)
    rows = lax.broadcasted_iota(jnp.int32, (CHUNK, CHUNK), 0)
    cols = lax.broadcasted_iota(jnp.int32, (CHUNK, CHUNK), 1)
    return seg_col, flag((rows >= cols) & (seg_col == seg_row))


def block_copies(runs, pieces, dest_ref, target, sem, first_row=0):
    rows = slice(first_row, first_row + target.shape[1])
    return [
        pltpu.make_async_copy(
            pieces[piece].at[pl.ds(start, size), rows],
            target.at[pl.ds(dest_ref[i], size)],
            sem.at[i],
        )
        for i, (piece, start, size) in enumerate(runs)
    ]


def forward_kernel(runs, ends_ref, dest_ref, xh_ref, xo_ref, seg_ref, spread_ref, *refs):
    count = 1 + max(piece for piece, _, _ in runs)
    pieces = refs[:count]
    h1_ref, qkv_ref, pq_ref, pk_ref, p_ref, t_ref, o_ref, rden_ref, gains_ref = refs[
        count : count + 9
    ]
    state_ref, wq_ref, sem = refs[count + 9 :]
    step = pl.program_id(0)
    halo = SPAN // ROWS
    subs = ROWS // CHUNK
    ones = jnp.ones((ROWS, 2 * HD), bf16)

    def weights(low, high):
        return wq_ref[:, :, low:high].reshape(D, high - low)

    @pl.when(step == 0)
    def _():
        copies = block_copies(runs, pieces, dest_ref, wq_ref, sem)
        for copy in copies:
            copy.start()
        state_ref[...] = jnp.zeros_like(state_ref)
        for copy in copies:
            copy.wait()
        gains_ref[...] = weights(3 * D, 3 * D + 128).astype(f32).T[:8]

    gain = gains_ref[0:1]

    @pl.when(step < halo)
    def _():
        x = xh_ref[...].astype(f32)
        h1 = (x * rms_scale(x) * gain).astype(bf16)
        chosen = flag(as_column(seg_ref[0]) == ends_ref[halo * subs - 1])
        kvs = [dot(h1, weights(384 * p + 128, 384 * (p + 1))).astype(bf16) for p in range(PAIRS)]
        for p in range(PAIRS):
            pk_ref[:, 512 * p : 512 * (p + 1)] = features(kvs[p][:, :128], spread_ref[...])
        for p in range(PAIRS):
            vw = jnp.concatenate([kvs[p][:, 128:], ones], axis=1) * chosen
            state_ref[p] = state_ref[p] + dot(pk_ref[:, 512 * p : 512 * (p + 1)], vw, 0, 0)

    @pl.when(step >= halo)
    def _():
        x = xo_ref[...].astype(f32)
        h1 = (x * rms_scale(x) * gain).astype(bf16)
        h1_ref[...] = h1
        qkv_ref[...] = dot(h1, weights(0, 3 * D)).astype(bf16)
        for p in range(PAIRS):
            wide = slice(512 * p, 512 * (p + 1))
            pq_ref[:, wide] = features(qkv_ref[:, 384 * p : 384 * p + 128], spread_ref[...])
            pk_ref[:, wide] = features(qkv_ref[:, 384 * p + 128 : 384 * p + 256], spread_ref[...])
        seg = seg_ref[0]
        for j in range(subs):
            rows = slice(CHUNK * j, CHUNK * (j + 1))
            _, allowed = chunk_mask(seg[:, rows])
            for h in range(2 * PAIRS):
                cut = slice(FEATS * h, FEATS * (h + 1))
                p_ref[rows, CHUNK * h : CHUNK * (h + 1)] = (
                    dot(pq_ref[rows, cut], pk_ref[rows, cut], 1, 1).astype(bf16) * allowed
                )
        seg_col = as_column(seg)
        for j in range(subs):
            rows = slice(CHUNK * j, CHUNK * (j + 1))
            before = ends_ref[step * subs + j - 1]
            last = ends_ref[step * subs + j]
            chosen = flag(seg_col[rows] == last)
            follows = flag(seg_col[rows] == before)
            keep = (last == before).astype(f32)
            for p in range(PAIRS):
                cut = slice(128 * p, 128 * (p + 1))
                wide = slice(512 * p, 512 * (p + 1))
                v2 = qkv_ref[rows, 384 * p + 256 : 384 * p + 384]
                v1 = jnp.concatenate([v2, ones[:CHUNK]], axis=1)
                state = state_ref[p]
                narrow = state.astype(bf16)
                narrow = masked_pair(narrow[:FEATS], narrow[FEATS:], 256)
                t_ref[j, p] = narrow[:FEATS] + narrow[FEATS:]
                both = dot(p_ref[rows, wide], masked_pair(v1, v1, 256)) + dot(
                    pq_ref[rows, wide] * follows, narrow
                )
                state_ref[p] = keep * state + dot(pk_ref[rows, wide], v1 * chosen, 0, 0)
                rden = 1.0 / both[:, 128:]
                rden_ref[rows, cut] = rden
                o_ref[rows, cut] = (both[:, :128] * rden).astype(bf16)


def middle_kernel(
    group, runs,
    ends_ref, core_ref, dest_ref, x_ref, g_ref, o_ref, rden_ref, pq_ref, seg_ref, gains_ref,
    *refs,
):
    count = 1 + max(piece for piece, _, _ in runs)
    pieces = refs[:count]
    act_ref, dy1_ref, dn_ref, sent_up_ref, sent_rest_ref, kept_up_ref, kept_rest_ref, back_ref = refs[
        count : count + 8
    ]
    up_acc, down_acc, out_acc, back_acc, dup_ref, w_ref, in_sem = refs[count + 8 :]
    step = pl.program_id(0)
    steps = pl.num_programs(0)
    cut = 512
    blocks = w_ref.shape[0] // (FF // cut)

    @pl.when(step == 0)
    def _():
        copies = block_copies(runs, pieces, dest_ref, w_ref, in_sem)
        for copy in copies:
            copy.start()
        back_acc[...] = jnp.zeros_like(back_acc)
        for copy in copies:
            copy.wait()

    def so_far(value):
        return jnp.where(step == 0, 0.0, value)

    o = o_ref[...]
    g = g_ref[...]
    gain = gains_ref[1:2]
    wo = w_ref[:, 128:144].reshape(D, D)
    y1 = x_ref[...].astype(f32) + dot(o, wo, 1, 1)
    r2 = rms_scale(y1)
    n2 = y1 * r2
    h2 = (n2 * gain).astype(bf16)
    for f in range(FF // cut):
        fs = slice(cut * f, cut * (f + 1))
        wd = w_ref[blocks * f : blocks * (f + 1), 64:128].reshape(cut, D)
        up = dot(h2, w_ref[:, 16 * f : 16 * (f + 1)].reshape(D, cut))
        d_act = dot(g, wd, 1, 1)
        cdf = 0.5 * (1.0 + lax.erf(up * math.sqrt(0.5)))
        density = jnp.exp(up * up * -0.5) * (1.0 / math.sqrt(2.0 * math.pi))
        act = (up * cdf).astype(bf16)
        d_up = (d_act * (cdf + up * density)).astype(bf16)
        act_ref[:, fs] = act
        dup_ref[:, fs] = d_up
        down_acc[fs, :] = so_far(down_acc[fs, :]) + dot(act, g, 0, 0)
        up_acc[:, fs] = so_far(up_acc[:, fs]) + dot(h2, d_up, 0, 0)
    d_h2 = dot(dup_ref[:, :cut], w_ref[:, :16].reshape(D, cut), 1, 1)
    for f in range(1, FF // cut):
        d_h2 = d_h2 + dot(
            dup_ref[:, cut * f : cut * (f + 1)],
            w_ref[:, 16 * f : 16 * (f + 1)].reshape(D, cut),
            1,
            1,
        )
    e2 = d_h2 * gain
    dy1 = g.astype(f32) + r2 * (e2 - n2 * jnp.mean(e2 * n2, axis=-1, keepdims=True))
    dy1_ref[...] = dy1
    da = dy1.astype(bf16)
    out_acc[...] = so_far(out_acc[...]) + dot(da, o, 0, 0)
    d_o = dot(da, wo)
    product = d_o * o.astype(f32)
    high = product.astype(bf16)
    low = (product - high.astype(f32)).astype(bf16)
    rden = rden_ref[...]
    ma, mb = half_masks(128)
    same = jnp.concatenate(
        [jnp.broadcast_to(ma, (HD, 128)), jnp.broadcast_to(mb, (HD, 128))], axis=0
    )
    same = jnp.concatenate([same, same], axis=0)
    lane = lanes(128) % HD
    m0 = (lane == 0).astype(f32).astype(bf16)
    m1 = (lane == 1).astype(f32).astype(bf16)
    for p in range(PAIRS):
        ps = slice(128 * p, 128 * (p + 1))
        total = dot(jnp.concatenate([high[:, ps], low[:, ps]], axis=1), same)
        d_den = -total * rden[:, ps]
        d_hi = d_den.astype(bf16)
        d_lo = (d_den - d_hi.astype(f32)).astype(bf16)
        d_num = (d_o[:, ps] * rden[:, ps]).astype(bf16)
        dn = jnp.concatenate([d_num, d_hi * m0 + d_lo * m1], axis=1)
        dn_ref[:, 256 * p : 256 * (p + 1)] = dn

    @pl.when(step < SPAN // ROWS)
    def _():
        follows = flag(as_column(seg_ref[0]) == ends_ref[SPAN // CHUNK - 1])
        for p in range(PAIRS):
            back_acc[p] = back_acc[p] + dot(
                pq_ref[:, 512 * p : 512 * (p + 1)], dn_ref[:, 256 * p : 256 * (p + 1)] * follows, 0, 0
            )

    @pl.when(step == steps - 1)
    def _():
        core = core_ref[0]
        for ups, others, side in (
            (sent_up_ref, sent_rest_ref, 1 - core),
            (kept_up_ref, kept_rest_ref, core),
        ):
            for far in range(ups.shape[0] // group):
                at = (2 * far + side) * group
                here = slice(group * far, group * (far + 1))
                thin = pl.ds(pl.multiple_of(at * 16, 16), group * 16)
                tall = pl.ds(pl.multiple_of(at * 64, 64), group * 64)
                for f in range(FF // cut):
                    piece = up_acc[thin, cut * f : cut * (f + 1)].astype(bf16)
                    ups[here, 16 * f : 16 * (f + 1)] = piece.reshape(group, 16, cut)
                others[here, :64] = down_acc[tall].astype(bf16).reshape(group, 64, D)
                others[here, 64:] = out_acc[thin].astype(bf16).reshape(group, 16, D)
        ma, mb = half_masks(128)
        for p in range(PAIRS):
            first, second = back_acc[p, :FEATS], back_acc[p, FEATS:]
            back_ref[p, :FEATS] = first[:, :128].astype(bf16) * ma + second[:, :128].astype(bf16) * mb
            rows = []
            for side, lane in ((first, 0), (second, HD)):
                turned = side[:, 128:].T
                total = turned[lane : lane + 1] + turned[lane + 1 : lane + 2]
                high = total.astype(bf16).astype(f32)
                for part in (high, total - high):
                    rows += [part[:, :128], part[:, 128:]]
            rows.append(jnp.zeros((8, 128), f32))
            back_ref[p, FEATS:] = jnp.concatenate(rows, axis=0).astype(bf16)


def output_kernel(runs, dest_ref, x_ref, o_ref, act_ref, *refs):
    out_ref, w_ref, sem = refs[-3:]
    pieces = refs[: 1 + max(piece for piece, _, _ in runs)]

    @pl.when(pl.program_id(0) == 0)
    def _():
        copies = block_copies(runs, pieces, dest_ref, w_ref, sem, 64)
        for copy in copies:
            copy.start()
        for copy in copies:
            copy.wait()

    y1 = x_ref[...].astype(f32) + dot(o_ref[...], w_ref[:, 64:].reshape(D, D), 1, 1)
    out_ref[...] = (y1 + dot(act_ref[...], w_ref[:, :64].reshape(FF, D))).astype(bf16)


def backward_kernel(pairs, ends_ref, seg_ref, gather_ref, *refs):
    refs = refs[: 7 * pairs] + refs[-4:]
    subs = ROWS // CHUNK
    step = pl.program_id(0)
    steps = pl.num_programs(0)
    at = (SPAN // ROWS + steps - 1 - step) * subs
    dqkv_ref, state_ref, grad_ref, logit_ref = refs[7 * pairs :]
    p_refs, pq_refs, pk_refs, qkv_refs, dn_refs, t_refs, back_refs = [
        refs[i * pairs : (i + 1) * pairs] for i in range(7)
    ]

    @pl.when(step == 0)
    def _():
        lane = lanes(128)
        for p in range(pairs):
            extra = back_refs[p][0, FEATS:].astype(f32)
            for i, mask in enumerate(half_masks(128)):
                rows = slice(FEATS * i, FEATS * (i + 1))
                state_ref[p, rows, :128] = (back_refs[p][0, :FEATS] * mask).astype(f32)
                total = jnp.zeros((FEATS, 128), f32)
                for t in range(2):
                    at_row = 4 * i + 2 * t
                    row = jnp.concatenate([extra[at_row : at_row + 1], extra[at_row + 1 : at_row + 2]], axis=1)
                    total = jnp.where(lane == HD * i + t, as_column(row), total)
                state_ref[p, rows, 128:] = total

    seg = seg_ref[0]
    seg_col = as_column(seg)
    two = jnp.broadcast_to(flag(lanes(128) % HD < 2), (CHUNK, 128))
    ones = jnp.ones((CHUNK, 128), bf16)
    ma, mb = half_masks(128)
    for j in reversed(range(subs)):
        rows = slice(CHUNK * j, CHUNK * (j + 1))
        _, allowed = chunk_mask(seg[:, rows])
        before = ends_ref[at + j - 1]
        last = ends_ref[at + j]
        chosen = flag(seg_col[rows] == last)
        follows = flag(seg_col[rows] == before)
        keep = (last == before).astype(f32)
        for p in range(pairs):
            v1 = jnp.concatenate([qkv_refs[p][rows, 256:], two], axis=1)
            d_p = dot(dn_refs[p][rows], masked_pair(v1, v1, 256), 1, 1).astype(bf16)
            grad_ref[p, :, :CHUNK] = d_p[:, :CHUNK] * allowed
            grad_ref[p, :, CHUNK:] = d_p[:, CHUNK:] * allowed
        for p in range(pairs):
            pq, pk, dn = pq_refs[p][rows], pk_refs[p][rows], dn_refs[p][rows]
            scores = p_refs[p][rows]
            v2 = qkv_refs[p][rows, 256:]
            compact = t_refs[p][j, 0]
            narrow = masked_pair(compact, compact, 256)
            state = state_ref[p]
            back = state.astype(bf16)
            back = masked_pair(back[:FEATS], back[FEATS:], 256)
            d_pa = grad_ref[p, :, :CHUNK]
            d_pb = grad_ref[p, :, CHUNK:]
            dn_f = dn * follows
            d_pq = dot(dn_f, narrow, 1, 1) + jnp.concatenate(
                [dot(d_pa, pk[:, :FEATS]), dot(d_pb, pk[:, FEATS:])], axis=1
            )
            logit_ref[0, p, rows] = d_pq.astype(bf16) * pq
            vw = jnp.concatenate([v2, ones], axis=1) * chosen
            d_pk = dot(vw, back, 1, 1) + jnp.concatenate(
                [dot(d_pa, pq[:, :FEATS], 0, 0), dot(d_pb, pq[:, FEATS:], 0, 0)], axis=1
            )
            logit_ref[1, p, rows] = d_pk.astype(bf16) * pk
            d_num = dn[:, :128]
            d_v = (
                dot(pk * chosen, back[:, :128])
                + dot(scores[:, :CHUNK], d_num * ma, 0, 0)
                + dot(scores[:, CHUNK:], d_num * mb, 0, 0)
            )
            dqkv_ref[rows, 384 * p + 256 : 384 * p + 384] = d_v.astype(bf16)
            state_ref[p] = keep * state + dot(pq, dn_f, 0, 0)
    scale2 = feature_scale * feature_scale
    for p in range(pairs):
        for i in range(2):
            u = qkv_refs[p][:, 128 * i : 128 * (i + 1)].astype(f32)
            through = dot(logit_ref[i, p], gather_ref[...])
            d_u = through[:, :128] * feature_scale - u * through[:, 128:] * scale2
            dqkv_ref[:, 384 * p + 128 * i : 384 * p + 128 * (i + 1)] = d_u.astype(bf16)


def input_kernel(runs, dest_ref, dqkv_ref, x_ref, dy1_ref, gains_ref, *refs):
    *pieces, dx_ref, wq_ref, sem = refs

    @pl.when(pl.program_id(0) == 0)
    def _():
        copies = block_copies(runs, pieces, dest_ref, wq_ref, sem)
        for copy in copies:
            copy.start()
        for copy in copies:
            copy.wait()

    d_h1 = dot(dqkv_ref[...], wq_ref[:, :, : 3 * D].reshape(D, 3 * D), 1, 1)
    x = x_ref[...].astype(f32)
    r1 = rms_scale(x)
    n1 = x * r1
    e1 = d_h1 * gains_ref[0:1]
    dx_ref[...] = dy1_ref[...] + r1 * (e1 - n1 * jnp.mean(e1 * n1, axis=-1, keepdims=True))


def finish_kernel(q_ref, kept_ref, came_ref, packed_ref, later_ref, sq_ref, sr_ref, gg_ref, spread_ref):
    share = q_ref.shape[1]
    sum_q = jnp.sum(q_ref[...].astype(f32), axis=0)
    sum_r = kept_ref[...].astype(f32) + came_ref[...].astype(f32)
    sq_ref[...] = sum_q
    sr_ref[...] = sum_r
    packed = packed_ref[...].astype(f32)
    tops = jnp.sum(packed[:, : 3 * D] * sum_q, axis=1, keepdims=True)
    rows = jnp.sum(later_ref[: 4 * share].astype(f32) * sum_r[: 4 * share], axis=1, keepdims=True)
    lows = rows[:share]
    for f in range(1, 4):
        lows = lows + rows[share * f : share * (f + 1)]
    gg = jnp.concatenate([tops, lows], axis=1) / packed[:, 3 * D : 3 * D + 2]
    gg_ref[...] = jnp.concatenate([gg, jnp.zeros((share, 126), f32)], axis=1).T[:2]
    total = jnp.sum(sum_q * sum_q) + jnp.sum(sum_r * sum_r) + jnp.sum(gg * gg)
    spread_ref[...] = jnp.full(spread_ref.shape, total, f32)


def axis_bits():
    row_bits = (lax.axis_size("row") - 1).bit_length()
    head_bits = (lax.axis_size("head") - 1).bit_length()
    row = [("row", b, b) for b in range(row_bits)]
    head = [("head", b, row_bits + b) for b in range(head_bits)]
    return row, head


def swap(value, axis, bit):
    return lax.ppermute(value, axis, [(i, i ^ (1 << bit)) for i in range(lax.axis_size(axis))])


def swap_far(value, mask):
    return lax.ppermute(value, AXES, [(i, i ^ mask) for i in range(lax.axis_size(AXES))])


def tied(value, *others):
    return lax.optimization_barrier((value,) + others)[0]


class Gather:
    def __init__(self, shard):
        self.buf = shard[None]
        self.offsets = [0]

    def start(self, axis, bit, place):
        self.came = swap(self.buf, axis, bit)
        self.mask = 1 << place

    def finish(self, *others):
        own = tied(self.buf, *others) if others else self.buf
        self.buf = jnp.concatenate([own, self.came], axis=0)
        self.offsets = self.offsets + [offset ^ self.mask for offset in self.offsets]


def device_index():
    return lax.axis_index("head") * lax.axis_size("row") + lax.axis_index("row")


def doubled(order, offsets=(0,)):
    offsets = list(offsets)
    for _, _, place in order:
        offsets += [offset ^ (1 << place) for offset in offsets]
    return offsets


def block_places(offsets):
    return (device_index() ^ jnp.asarray(offsets, jnp.int32)).astype(jnp.int32)


def in_order(pieces, offsets):
    slots = [0] * len(offsets)
    for slot, offset in enumerate(offsets):
        slots[offset] = slot
    every = jnp.arange(len(offsets), dtype=jnp.int32) ^ device_index()
    order = jnp.asarray(slots, jnp.int32)[every]
    return jnp.take(jnp.concatenate(pieces, axis=0), order, axis=0)


def single_runs(pieces):
    return [(i, k, 1) for i, piece in enumerate(pieces) for k in range(piece.shape[0])]


class Halving:
    def __init__(self, kept, came, places):
        self.places = sorted(places, reverse=True)
        self.parts = [kept] if came is None else [kept, came]
        self.parts = [self.split(part) for part in self.parts]

    def split(self, part):
        inner = part.shape[1:] if part.ndim == 3 else part.shape[-2:]
        return part.reshape((2,) * len(self.places) + inner)

    def take(self, index, at):
        total = sum(
            lax.dynamic_index_in_dim(part, index, at, keepdims=False).astype(f32)
            for part in self.parts
        )
        return total.astype(bf16)

    def after(self, *others):
        self.parts[0] = tied(self.parts[0], *others)
        return self

    def send(self, axis, bit, place):
        at = self.places.index(place)
        mine = (lax.axis_index(axis) >> bit) & 1
        sent = self.take(1 - mine, at)
        came = swap(sent, axis, bit)
        self.parts = [self.take(mine, at), came]
        self.places.remove(place)
        return sent

    def total(self):
        return sum(part.astype(f32) for part in self.parts)


def late_in_order(pieces, offsets, share):
    whole = in_order(pieces, offsets)
    parts = 16 // share
    whole = whole.reshape(D // 16, parts, 9 * share, 512)
    ups = whole[:, :, : 4 * share].reshape(D // 16, parts, 4, share, 512)
    ups = ups.transpose(0, 2, 1, 3, 4).reshape(D // 16, 64, 512)
    downs = whole[:, :, 4 * share : 8 * share].reshape(D // 16, 64, 512)
    outs = whole[:, :, 8 * share :].reshape(D // 16, 16, 512)
    return jnp.concatenate([ups, downs, outs], axis=1)


def ups_by_device(blocks, share):
    ups = blocks.reshape(-1, 4, 16 // share, share, 512)
    return ups.transpose(0, 2, 1, 3, 4).reshape(-1, 4 * share, 512)


def rest_by_device(blocks, share):
    downs = blocks[:, :64].reshape(-1, 4 * share, 512)
    outs = blocks[:, 64:].reshape(-1, share, 512)
    return jnp.concatenate([downs, outs], axis=1)


def core_groups():
    heads, rows = lax.axis_size("head"), lax.axis_size("row")
    return [[h * rows + r for h in range(c, heads, 2) for r in range(rows)] for c in (0, 1)]


def exchange(blocks):
    return lax.all_to_all(
        blocks, AXES, split_axis=0, concat_axis=0, axis_index_groups=core_groups(), tiled=True
    )


def total_of(spread):
    came = lax.all_to_all(spread, AXES, split_axis=0, concat_axis=0, tiled=True)
    return jnp.sum(came[:, 0, 0])


def adam_update(
    weight, gradient, first_moment, second_moment, clip_factor, step_value, step_rate, decay_rate
):
    clipped = gradient * clip_factor
    next_first = beta_first * first_moment + (1.0 - beta_first) * clipped
    next_second = beta_second * second_moment + (1.0 - beta_second) * clipped * clipped
    first_hat = next_first / (1.0 - beta_first**step_value)
    second_hat = next_second / (1.0 - beta_second**step_value)
    updated = weight - step_rate * (
        first_hat / (jnp.sqrt(second_hat) + adam_eps) + decay_rate * weight
    )
    return (clipped, next_first, next_second, updated)


def params(limit=60):
    return pltpu.CompilerParams(
        dimension_semantics=("arbitrary",), vmem_limit_bytes=limit << 20
    )


def cost(us):
    return pl.CostEstimate(flops=us * 50000000, transcendentals=0, bytes_accessed=us * 150000)


def fixed(shape):
    zeros = (0,) * len(shape)
    return pl.BlockSpec(shape, lambda *_: zeros, pipeline_mode=pl.Buffered(1))


def first_at(shape, offset):
    rest = (0,) * (len(shape) - 1)
    return pl.BlockSpec(shape, lambda c, *_: (jnp.maximum(c - offset, 0),) + rest)


def by_step(shape):
    return first_at(shape, 0)


def forward_call(runs, ends, dest, x_ahead, x, seg_rows, spread, pieces):
    length = x.shape[0]
    chunks, halo, wide = length // CHUNK, SPAN // ROWS, PAIRS * 2 * FEATS
    own = partial(first_at, offset=halo)
    outs = [
        ((ROWS, D), (length, D), bf16),
        ((ROWS, 3 * D), (length, 3 * D), bf16),
        ((ROWS, wide), (length, wide), bf16),
        ((ROWS, wide), (length, wide), bf16),
        ((ROWS, wide), (length, wide), bf16),
        ((ROWS // CHUNK, PAIRS, FEATS, 256), (chunks, PAIRS, FEATS, 256), bf16),
        ((ROWS, D), (length, D), bf16),
        ((ROWS, D), (length, D), f32),
    ]
    return pl.pallas_call(
        partial(forward_kernel, runs),
        grid_spec=pltpu.PrefetchScalarGridSpec(
            num_scalar_prefetch=2,
            grid=(halo + length // ROWS,),
            in_specs=[
                pl.BlockSpec((ROWS, D), lambda c, *_: (jnp.minimum(c, halo - 1), 0)),
                own((ROWS, D)),
                by_step((1, 1, ROWS)),
                fixed(spread.shape),
            ]
            + [pl.BlockSpec(memory_space=pl.ANY)] * len(pieces),
            out_specs=[own(block) for block, _, _ in outs] + [fixed((8, D))],
            scratch_shapes=[
                pltpu.VMEM((PAIRS, 2 * FEATS, 256), f32),
                pltpu.VMEM((D // 16, 16, 3 * D + 128), bf16),
                pltpu.SemaphoreType.DMA((len(runs),)),
            ],
        ),
        out_shape=[jax.ShapeDtypeStruct(shape, kind) for _, shape, kind in outs]
        + [jax.ShapeDtypeStruct((8, D), f32)],
        compiler_params=params(),
        cost_estimate=cost(35),
        name="forward",
    )(ends, dest, x_ahead, x, seg_rows, spread, *pieces)


def middle_call(group, runs, ends, core, dest, x, g, o, rden, pq, seg_rows, gain_rows, pieces):
    length, wide = x.shape[0], pq.shape[1]
    near_steps = SPAN // ROWS
    by_step_ahead = pl.BlockSpec((1, 1, ROWS), lambda c, *_: (c + near_steps, 0, 0))

    outs = [
        ((ROWS, FF), (length, FF), bf16),
        ((ROWS, D), (length, D), f32),
        ((ROWS, PAIRS * 256), (length, PAIRS * 256), bf16),
    ]
    sums = [(D // 32, 64, 512), (D // 32, 80, 512)] * 2 + [(PAIRS, FEATS + 16, 128)]
    return pl.pallas_call(
        partial(middle_kernel, group, runs),
        grid_spec=pltpu.PrefetchScalarGridSpec(
            num_scalar_prefetch=3,
            grid=(length // ROWS,),
            in_specs=[by_step((ROWS, D))] * 4
            + [
                pl.BlockSpec((ROWS, wide), lambda c, *_: (jnp.minimum(c, near_steps - 1), 0)),
                by_step_ahead,
                fixed((8, D)),
            ]
            + [pl.BlockSpec(memory_space=pl.ANY)] * len(pieces),
            out_specs=[by_step(block) for block, _, _ in outs] + [fixed(shape) for shape in sums],
            scratch_shapes=[
                pltpu.VMEM((D, FF), f32),
                pltpu.VMEM((FF, D), f32),
                pltpu.VMEM((D, D), f32),
                pltpu.VMEM((PAIRS, 2 * FEATS, 256), f32),
                pltpu.VMEM((ROWS, FF), bf16),
                pltpu.VMEM((D // 16, 144, 512), bf16),
                pltpu.SemaphoreType.DMA((len(runs),)),
            ],
        ),
        out_shape=[jax.ShapeDtypeStruct(shape, kind) for _, shape, kind in outs]
        + [jax.ShapeDtypeStruct(shape, bf16) for shape in sums],
        compiler_params=params(),
        cost_estimate=cost(48),
        name="middle",
    )(ends, core, dest, x, g, o, rden, pq, seg_rows, gain_rows, *pieces)


def backward_call(at, parts, ends, seg_rows, gather, arrays, *written):
    length = arrays[0].shape[0]
    steps, halo = length // ROWS, SPAN // ROWS
    count = PAIRS // parts
    chosen = range(at * count, (at + 1) * count)

    def falling(shape, at=0):
        rest = (0,) * (len(shape) - 2)
        return pl.BlockSpec(shape, lambda c, *_: (steps - 1 - c, at) + rest)

    def state(at):
        return pl.BlockSpec(
            (1, FEATS + 16, 128), lambda *_: (at, 0, 0), pipeline_mode=pl.Buffered(1)
        )

    specs = [pl.BlockSpec((1, 1, ROWS), lambda c, *_: (steps + halo - 1 - c, 0, 0))]
    specs += [fixed(gather.shape)]
    for shape in ((ROWS, 512),) * 3 + ((ROWS, 384), (ROWS, 256), (ROWS // CHUNK, 1, 256, 256)):
        specs += [falling(shape, p) for p in chosen]
    specs += [state(p) for p in chosen]
    operands = [array for array in arrays for _ in chosen]
    return pl.pallas_call(
        partial(backward_kernel, count),
        grid_spec=pltpu.PrefetchScalarGridSpec(
            num_scalar_prefetch=1,
            grid=(steps,),
            in_specs=specs + [pl.BlockSpec(memory_space=pl.ANY)] * len(written),
            out_specs=falling((ROWS, 384 * count), at),
            scratch_shapes=[
                pltpu.VMEM((count, 2 * FEATS, 256), f32),
                pltpu.VMEM((count, CHUNK, 2 * CHUNK), bf16),
                pltpu.VMEM((2, count, ROWS, 2 * FEATS), bf16),
            ],
        ),
        out_shape=jax.ShapeDtypeStruct((length, 3 * D), bf16),
        input_output_aliases={3 + len(operands): 0} if written else {},
        compiler_params=params(),
        cost_estimate=cost(8 * count),
        name="backward",
    )(ends, seg_rows, gather, *operands, *written)


def input_call(runs, dest, dqkv, x, dy1, gain_rows, pieces):
    length = x.shape[0]
    return pl.pallas_call(
        partial(input_kernel, runs),
        grid_spec=pltpu.PrefetchScalarGridSpec(
            num_scalar_prefetch=1,
            grid=(length // ROWS,),
            in_specs=[
                by_step((ROWS, 3 * D)),
                by_step((ROWS, D)),
                by_step((ROWS, D)),
                fixed((8, D)),
            ]
            + [pl.BlockSpec(memory_space=pl.ANY)] * len(pieces),
            out_specs=by_step((ROWS, D)),
            scratch_shapes=[
                pltpu.VMEM((D // 16, 16, 3 * D + 128), bf16),
                pltpu.SemaphoreType.DMA((len(runs),)),
            ],
        ),
        out_shape=jax.ShapeDtypeStruct((length, D), f32),
        compiler_params=params(),
        cost_estimate=cost(10),
        name="input_grad",
    )(dest, dqkv, x, dy1, gain_rows, *pieces)


def output_call(half, runs, dest, x, o, act, pieces, *written):
    length = x.shape[0]
    steps = length // ROWS // 2

    def rows(shape):
        return pl.BlockSpec(shape, lambda c, *_: (c + half * steps, 0))

    others = len(pieces) + len(written)
    return pl.pallas_call(
        partial(output_kernel, runs),
        grid_spec=pltpu.PrefetchScalarGridSpec(
            num_scalar_prefetch=1,
            grid=(steps,),
            in_specs=[rows((ROWS, D)), rows((ROWS, D)), rows((ROWS, FF))]
            + [pl.BlockSpec(memory_space=pl.ANY)] * others,
            out_specs=rows((ROWS, D)),
            scratch_shapes=[
                pltpu.VMEM((D // 16, 80, 512), bf16),
                pltpu.SemaphoreType.DMA((len(runs),)),
            ],
        ),
        out_shape=jax.ShapeDtypeStruct((length, D), bf16),
        input_output_aliases={4 + len(pieces): 0} if written else {},
        compiler_params=params(),
        cost_estimate=cost(6),
        name="output",
    )(dest, x, o, act, *pieces, *written)


def per_device(
    inputs,
    cotangent,
    segments,
    feature_matrix,
    w_qkv,
    w_out,
    w_up,
    w_down,
    gains,
    first_qkv,
    second_qkv,
    first_out,
    second_out,
    first_up,
    second_up,
    first_down,
    second_down,
    first_gains,
    second_gains,
    step_count,
):
    heads = lax.axis_size("head")
    row_bits, head_bits = axis_bits()
    x = inputs[0]
    g = cotangent[0]
    length = x.shape[0]
    share = w_qkv.shape[0]
    group = lax.axis_size("row") * share // 16

    packed = jnp.concatenate(
        [
            w_qkv.reshape(share, 3, PAIRS, 128).transpose(0, 2, 1, 3).reshape(share, 3 * D),
            gains,
            jnp.zeros((share, 126), f32),
        ],
        axis=1,
    ).astype(bf16)
    forward_pairs = [(i, i + 1) for i in range(heads - 1)]
    backward_pairs = [(i + 1, i) for i in range(heads - 1)]
    weights = Gather(packed)
    core_bit, *far_bits = head_bits
    order = row_bits[:0:-1] + far_bits + row_bits[:1] + [core_bit]
    tail = x[length - SPAN :]
    up, down, out = [tied(weight, tail) for weight in (w_up, w_down, w_out)]
    later_own = jnp.concatenate(
        [up[:, 512 * j : 512 * (j + 1)] for j in range(FF // 512)] + [down, out], axis=0
    ).astype(bf16)
    later = Gather(later_own)
    later_order = row_bits[:1:-1] + row_bits[:1] + far_bits[:-1]
    quad = [row_bits[1], far_bits[-1]]
    weights.buf = tied(weights.buf, tail)
    x_ahead = lax.ppermute(tail, "head", forward_pairs)
    weights.start(*order[0])
    later.start(*later_order[0])
    weights.finish()
    weights.start(*order[1])
    later.finish()
    later.start(*later_order[1])
    row_segments = tied(segments[0], weights.buf)
    padded = jnp.concatenate([jnp.full((SPAN,), -1, jnp.int32), row_segments])
    near = lax.dynamic_slice_in_dim(padded, lax.axis_index("head") * length, length + SPAN)
    ends = near[CHUNK - 1 :: CHUNK]
    seg_rows = near.astype(f32).reshape(-1, 1, ROWS)
    fm = feature_matrix
    nothing = jnp.zeros_like(fm.T)
    spread = jnp.concatenate(
        [
            jnp.concatenate([fm.T, nothing], axis=1),
            jnp.concatenate([nothing, fm.T], axis=1),
        ],
        axis=0,
    )
    zero = jnp.zeros((FEATS, HD), bf16)
    one = jnp.ones((FEATS, HD), bf16)
    gather = jnp.concatenate(
        [
            jnp.concatenate([fm, zero, one, zero], axis=1),
            jnp.concatenate([zero, fm, zero, one], axis=1),
        ],
        axis=0,
    )
    weights.finish(ends, seg_rows, later.buf)
    weights.start(*order[2])
    offsets = doubled(order)
    late_offsets = doubled(quad + [core_bit], doubled(later_order))
    dest, late_dest = block_places(offsets), block_places(late_offsets)
    weights.finish(spread, gather, x_ahead, dest, late_dest)
    for stage in later_order[1:]:
        later.finish()
        if stage != later_order[-1]:
            later.start(*later_order[later_order.index(stage) + 1])
    flips = [1 << place for _, _, place in quad]
    late = [later.buf] + [swap(later.buf, axis, bit) for axis, bit, _ in quad]
    late.append(swap_far(later.buf, sum(flips)))
    near = [swap(later.buf, "head", 0)]
    for stage in order[3:-1]:
        weights.start(*stage)
        weights.finish(later.buf)
    pieces = [weights.buf]
    weights.start(*order[-1])
    pieces.append(weights.came)
    if share == 16:
        runs = single_runs(pieces)
    else:
        pieces = [in_order(pieces, offsets).reshape(D // 16, 16, 3 * D + 128)]
        runs, dest = [(0, 0, D // 16)], jnp.zeros((1,), jnp.int32)
        late_dest = dest
    core = (lax.axis_index("head") & 1).reshape(1)

    h1, qkv, pq, pk, scores, states, o, rden, gain_rows = forward_call(
        runs, ends, dest, tied(x_ahead, later.buf, late_dest), x, seg_rows, spread, pieces
    )
    late[1:] = [tied(piece, o) for piece in late[1:]]
    near = [tied(near[0], o)] + [swap(piece, "head", 0) for piece in late[1:]]
    late = late + near
    late_runs = single_runs(late)
    if share != 16:
        late = [late_in_order(late, late_offsets, share)]
        late_runs = [(0, 0, D // 16)]
    act, dy1, dn, sent_up, sent_rest, kept_up, kept_rest, back = middle_call(
        group, late_runs, ends, core, late_dest, x, g, o, rden, pq, seg_rows, gain_rows, late
    )
    if share != 16:
        sent_up, kept_up = ups_by_device(sent_up, share), ups_by_device(kept_up, share)
        sent_rest, kept_rest = rest_by_device(sent_rest, share), rest_by_device(kept_rest, share)
    back_in = lax.ppermute(back, "head", backward_pairs)
    came_up = swap(sent_up, "head", 0)
    came_rest = swap(sent_rest, "head", 0)

    def attention_back(at, back_in, *written):
        arrays = (scores, pq, pk, qkv, dn, states, back_in)
        return backward_call(at, 1, ends, seg_rows, gather, arrays, *written)

    lower = [(axis, bit, place - (place > core_bit[2])) for axis, bit, place in far_bits]
    first_order = lower + row_bits[:1]
    second_order = row_bits[:1] + lower
    last_order = row_bits[1:]
    places = [place for _, _, place in first_order + last_order]
    cut = 4 * share

    kept_up, kept_rest = tied(kept_up, back_in), tied(kept_rest, back_in)
    first = Halving(kept_up, came_up, places)
    second = Halving(kept_rest, came_rest, places)
    back_in = tied(back_in, first.send(*first_order[0]), second.send(*second_order[0]))
    dqkv = attention_back(0, back_in)

    moved = []
    for i, (left, right) in enumerate(zip(first_order[1:], second_order[1:])):
        for half, stage in ((first, left), (second, right)):
            half.parts = [tied(part, dqkv) for part in half.parts]
            moved.append(half.send(*stage))
    g_qkv = dot(tied(h1, dqkv, *moved), dqkv, 0, 0).astype(bf16).reshape(heads // 2, 2, -1, 3 * D)
    left, right = [[tied(part, g_qkv) for part in half.parts] for half in (first, second)]
    rest = Halving(jnp.concatenate([left[0], right[0]], axis=-2), None, first.places)
    rest.parts.append(jnp.concatenate([left[1], right[1]], axis=-2))
    moved = rest.send(*last_order[0])
    g_qkv = tied(g_qkv, moved)
    sent_qkv = lax.dynamic_index_in_dim(g_qkv, 1 - core[0], 1, False)
    came_qkv = swap(sent_qkv, "head", 0)
    out_act = output_call(0, late_runs, late_dest, tied(x, sent_qkv, moved), o, act, late)
    kept_qkv = lax.dynamic_index_in_dim(g_qkv, core[0], 1, False)
    kept_qkv = tied(kept_qkv, out_act, *rest.parts)
    merged_qkv = (kept_qkv.astype(f32) + came_qkv.astype(f32)).astype(bf16)
    all_qkv = exchange(merged_qkv.reshape(-1, share, 3 * D))
    dx = input_call(runs, dest, dqkv, x, tied(dy1, merged_qkv), gain_rows, pieces)
    for stage in last_order[1:]:
        rest.parts = [tied(part, dx) for part in rest.parts]
        moved = rest.send(*stage)
    out_act = output_call(1, late_runs, late_dest, tied(x, moved), o, act, late, out_act)
    rest.parts[0] = tied(rest.parts[0], out_act)
    kept, came = rest.parts
    count = lax.axis_size(AXES)
    sum_qkv, sums, sum_gains, spread = pl.pallas_call(
        finish_kernel,
        out_shape=[
            jax.ShapeDtypeStruct((share, 3 * D), f32),
            jax.ShapeDtypeStruct((9 * share, 512), f32),
            jax.ShapeDtypeStruct((2, share), f32),
            jax.ShapeDtypeStruct((count, 8, 128), f32),
        ],
        name="finish",
    )(all_qkv, kept, came, packed, later_own)
    sum_qkv = sum_qkv.reshape(share, PAIRS, 3, 128).transpose(0, 2, 1, 3).reshape(share, 3, D)
    sum_up = sums[: 4 * share].reshape(4, share, 512).transpose(1, 0, 2).reshape(share, FF)
    sum_down = sums[4 * share : 8 * share]
    sum_out = sums[8 * share :]
    reduced = lax.optimization_barrier((sum_qkv, sum_out, sum_up, sum_down, sum_gains))
    reduced = reduced[:4] + (reduced[4].T,)
    total_squares = total_of(spread)
    grad_norm = jnp.sqrt(total_squares)
    clip_factor = jnp.minimum(1.0, max_norm / (grad_norm + 1e-06))
    step_value = step_count.astype(f32)
    update = partial(adam_update, clip_factor=clip_factor, step_value=step_value)
    qkv_parts = update(
        w_qkv, reduced[0], first_qkv, second_qkv, step_rate=matrix_rate, decay_rate=matrix_decay
    )
    out_parts = update(
        w_out, reduced[1], first_out, second_out, step_rate=output_rate, decay_rate=matrix_decay
    )
    up_parts = update(
        w_up, reduced[2], first_up, second_up, step_rate=matrix_rate, decay_rate=matrix_decay
    )
    down_parts = update(
        w_down, reduced[3], first_down, second_down, step_rate=matrix_rate, decay_rate=matrix_decay
    )
    gain_parts = update(
        gains, reduced[4], first_gains, second_gains, step_rate=gain_rate, decay_rate=0.0
    )
    return (
        (out_act[None], dx[None], grad_norm)
        + qkv_parts
        + out_parts
        + up_parts
        + down_parts
        + gain_parts
    )


def solution(mesh):
    token = P("row", "head", None)
    three = P(AXES, None, None)
    two = P(AXES, None)
    placed = (token, token, P("row", None), P(), three, two, two, two, two)
    placed = placed + (three, three) + (two,) * 8 + (P(),)
    return jax.shard_map(
        per_device,
        mesh=mesh,
        in_specs=placed,
        out_specs=(token, token, P()) + (three,) * 4 + (two,) * 16,
        check_vma=False,
    )
```

```python
import math
from functools import partial

import jax
import jax.numpy as jnp
from jax import lax
from jax.experimental import pallas as pl
from jax.experimental.pallas import tpu as pltpu
from jax.sharding import PartitionSpec as P

D = 512
HD = 64
FEATS = 256
FF = 2048
CHUNK = 256
SPAN = 1024
ROWS = 512
PAIRS = D // (2 * HD)

bf16 = jnp.bfloat16
f32 = jnp.float32
norm_eps = 1e-06
beta_first = 0.9
beta_second = 0.999
adam_eps = 1e-08
max_norm = 1.0
matrix_rate = 0.08
output_rate = 0.3
gain_rate = 1.5
matrix_decay = 0.1
feature_scale = HD ** (-0.25)
log2e = math.log2(math.e)
AXES = ("head", "row")


def dot(a, b, ca=1, cb=0):
    return lax.dot_general(a, b, (((ca,), (cb,)), ((), ())), preferred_element_type=f32)


def lanes(width):
    return lax.broadcasted_iota(jnp.int32, (1, width), 1)


def half_masks(width):
    first = (lanes(width) % 128 < HD).astype(f32)
    return first.astype(bf16), (1.0 - first).astype(bf16)


def rms_scale(values):
    return lax.rsqrt(jnp.mean(values * values, axis=-1, keepdims=True) + norm_eps)


def features(u, spread):
    raw = dot(u, spread)
    wide = u.astype(f32)
    squares = wide * wide
    own = lanes(2 * HD) < HD
    total_a = jnp.sum(jnp.where(own, squares, 0.0), axis=1, keepdims=True)
    total_b = jnp.sum(jnp.where(own, 0.0, squares), axis=1, keepdims=True)
    c1 = feature_scale * log2e
    c2 = 0.5 * feature_scale * feature_scale * log2e
    down_a = total_a * c2 + 4.0
    down_b = total_b * c2 + 4.0
    left = jnp.exp2(raw[:, :FEATS] * c1 - down_a)
    right = jnp.exp2(raw[:, FEATS:] * c1 - down_b)
    return jnp.concatenate([left, right], axis=1).astype(bf16)


def masked_pair(first, second, width):
    ma, mb = half_masks(width)
    return jnp.concatenate([first * ma, second * mb], axis=0)


def as_column(row):
    return jnp.broadcast_to(row, (8, row.shape[1])).T[:, :1]


def flag(condition):
    return condition.astype(f32).astype(bf16)


def chunk_mask(seg_row):
    seg_col = as_column(seg_row)
    rows = lax.broadcasted_iota(jnp.int32, (CHUNK, CHUNK), 0)
    cols = lax.broadcasted_iota(jnp.int32, (CHUNK, CHUNK), 1)
    return seg_col, flag((rows >= cols) & (seg_col == seg_row))


def copy_blocks(runs, pieces, dest_ref, target, sem, first_row=0):
    rows = slice(first_row, first_row + target.shape[1])

    def each(act):
        base = 0
        for i, piece in enumerate(pieces):
            own = [size for which, _, size in runs if which == i]
            size, first = own[0], base

            def body(k, carry, piece=piece, size=size, first=first):
                copy = pltpu.make_async_copy(
                    piece.at[pl.ds(k * size, size), rows],
                    target.at[pl.ds(dest_ref[first + k], size)],
                    sem.at[first + k],
                )
                act(copy)
                return carry

            lax.fori_loop(0, len(own), body, 0)
            base += len(own)

    each(lambda copy: copy.start())
    return lambda: each(lambda copy: copy.wait())


def forward_kernel(runs, ends_ref, dest_ref, xh_ref, xo_ref, seg_ref, spread_ref, *refs):
    count = 1 + max(piece for piece, _, _ in runs)
    pieces = refs[:count]
    h1_ref, qkv_ref, pq_ref, pk_ref, p_ref, t_ref, o_ref, rden_ref, gains_ref = refs[
        count : count + 9
    ]
    state_ref, wq_ref, sem = refs[count + 9 :]
    step = pl.program_id(0)
    halo = SPAN // ROWS
    subs = ROWS // CHUNK
    ones = jnp.ones((ROWS, 2 * HD), bf16)

    def weights(low, high):
        return wq_ref[:, :, low:high].reshape(D, high - low)

    @pl.when(step == 0)
    def _():
        wait = copy_blocks(runs, pieces, dest_ref, wq_ref, sem)
        state_ref[...] = jnp.zeros_like(state_ref)
        wait()
        gains_ref[...] = weights(3 * D, 3 * D + 128).astype(f32).T[:8]

    gain = gains_ref[0:1]

    @pl.when(step < halo)
    def _():
        x = xh_ref[...].astype(f32)
        h1 = (x * rms_scale(x) * gain).astype(bf16)
        chosen = flag(as_column(seg_ref[0]) == ends_ref[halo * subs - 1])
        kvs = [dot(h1, weights(384 * p + 128, 384 * (p + 1))).astype(bf16) for p in range(PAIRS)]
        for p in range(PAIRS):
            pk_ref[:, 512 * p : 512 * (p + 1)] = features(kvs[p][:, :128], spread_ref[...])
        for p in range(PAIRS):
            vw = jnp.concatenate([kvs[p][:, 128:], ones], axis=1) * chosen
            state_ref[p] = state_ref[p] + dot(pk_ref[:, 512 * p : 512 * (p + 1)], vw, 0, 0)

    @pl.when(step >= halo)
    def _():
        x = xo_ref[...].astype(f32)
        h1 = (x * rms_scale(x) * gain).astype(bf16)
        h1_ref[...] = h1
        qkv_ref[...] = dot(h1, weights(0, 3 * D)).astype(bf16)
        for p in range(PAIRS):
            wide = slice(512 * p, 512 * (p + 1))
            pq_ref[:, wide] = features(qkv_ref[:, 384 * p : 384 * p + 128], spread_ref[...])
            pk_ref[:, wide] = features(qkv_ref[:, 384 * p + 128 : 384 * p + 256], spread_ref[...])
        seg = seg_ref[0]
        for j in range(subs):
            rows = slice(CHUNK * j, CHUNK * (j + 1))
            _, allowed = chunk_mask(seg[:, rows])
            for h in range(2 * PAIRS):
                cut = slice(FEATS * h, FEATS * (h + 1))
                p_ref[rows, CHUNK * h : CHUNK * (h + 1)] = (
                    dot(pq_ref[rows, cut], pk_ref[rows, cut], 1, 1).astype(bf16) * allowed
                )
        seg_col = as_column(seg)
        for j in range(subs):
            rows = slice(CHUNK * j, CHUNK * (j + 1))
            before = ends_ref[step * subs + j - 1]
            last = ends_ref[step * subs + j]
            chosen = flag(seg_col[rows] == last)
            follows = flag(seg_col[rows] == before)
            keep = (last == before).astype(f32)
            for p in range(PAIRS):
                cut = slice(128 * p, 128 * (p + 1))
                wide = slice(512 * p, 512 * (p + 1))
                v2 = qkv_ref[rows, 384 * p + 256 : 384 * p + 384]
                v1 = jnp.concatenate([v2, ones[:CHUNK]], axis=1)
                state = state_ref[p]
                narrow = state.astype(bf16)
                narrow = masked_pair(narrow[:FEATS], narrow[FEATS:], 256)
                t_ref[j, p] = narrow[:FEATS] + narrow[FEATS:]
                both = dot(p_ref[rows, wide], masked_pair(v1, v1, 256)) + dot(
                    pq_ref[rows, wide] * follows, narrow
                )
                state_ref[p] = keep * state + dot(pk_ref[rows, wide], v1 * chosen, 0, 0)
                rden = 1.0 / both[:, 128:]
                rden_ref[rows, cut] = rden
                o_ref[rows, cut] = (both[:, :128] * rden).astype(bf16)


def middle_kernel(
    group, runs,
    ends_ref, core_ref, dest_ref, x_ref, g_ref, o_ref, rden_ref, pq_ref, seg_ref, gains_ref,
    *refs,
):
    count = 1 + max(piece for piece, _, _ in runs)
    pieces = refs[:count]
    out_ref, dy1_ref, dn_ref, sent_up_ref, sent_rest_ref, kept_up_ref, kept_rest_ref, back_ref = refs[
        count : count + 8
    ]
    up_acc, down_acc, out_acc, back_acc, act_ref, dup_ref, w_ref, in_sem = refs[count + 8 :]
    step = pl.program_id(0)
    steps = pl.num_programs(0)
    cut = 512
    blocks = w_ref.shape[0] // (FF // cut)

    @pl.when(step == 0)
    def _():
        wait = copy_blocks(runs, pieces, dest_ref, w_ref, in_sem)
        back_acc[...] = jnp.zeros_like(back_acc)
        wait()

    def so_far(value):
        return jnp.where(step == 0, 0.0, value)

    o = o_ref[...]
    g = g_ref[...]
    gain = gains_ref[1:2]
    wo = w_ref[:, 128:144].reshape(D, D)
    y1 = x_ref[...].astype(f32) + dot(o, wo, 1, 1)
    r2 = rms_scale(y1)
    n2 = y1 * r2
    h2 = (n2 * gain).astype(bf16)
    for f in range(FF // cut):
        fs = slice(cut * f, cut * (f + 1))
        wd = w_ref[blocks * f : blocks * (f + 1), 64:128].reshape(cut, D)
        up = dot(h2, w_ref[:, 16 * f : 16 * (f + 1)].reshape(D, cut))
        d_act = dot(g, wd, 1, 1)
        cdf = 0.5 * (1.0 + lax.erf(up * math.sqrt(0.5)))
        density = jnp.exp(up * up * -0.5) * (1.0 / math.sqrt(2.0 * math.pi))
        act = (up * cdf).astype(bf16)
        d_up = (d_act * (cdf + up * density)).astype(bf16)
        act_ref[:, fs] = act
        dup_ref[:, fs] = d_up
        down_acc[fs, :] = so_far(down_acc[fs, :]) + dot(act, g, 0, 0)
        up_acc[:, fs] = so_far(up_acc[:, fs]) + dot(h2, d_up, 0, 0)
    out_ref[...] = (y1 + dot(act_ref[...], w_ref[:, 64:128].reshape(FF, D))).astype(bf16)
    d_h2 = dot(dup_ref[:, :cut], w_ref[:, :16].reshape(D, cut), 1, 1)
    for f in range(1, FF // cut):
        d_h2 = d_h2 + dot(
            dup_ref[:, cut * f : cut * (f + 1)],
            w_ref[:, 16 * f : 16 * (f + 1)].reshape(D, cut),
            1,
            1,
        )
    e2 = d_h2 * gain
    dy1 = g.astype(f32) + r2 * (e2 - n2 * jnp.mean(e2 * n2, axis=-1, keepdims=True))
    dy1_ref[...] = dy1
    da = dy1.astype(bf16)
    out_acc[...] = so_far(out_acc[...]) + dot(da, o, 0, 0)
    d_o = dot(da, wo)
    product = d_o * o.astype(f32)
    high = product.astype(bf16)
    low = (product - high.astype(f32)).astype(bf16)
    rden = rden_ref[...]
    ma, mb = half_masks(128)
    same = jnp.concatenate(
        [jnp.broadcast_to(ma, (HD, 128)), jnp.broadcast_to(mb, (HD, 128))], axis=0
    )
    same = jnp.concatenate([same, same], axis=0)
    lane = lanes(128) % HD
    m0 = (lane == 0).astype(f32).astype(bf16)
    m1 = (lane == 1).astype(f32).astype(bf16)
    for p in range(PAIRS):
        ps = slice(128 * p, 128 * (p + 1))
        total = dot(jnp.concatenate([high[:, ps], low[:, ps]], axis=1), same)
        d_den = -total * rden[:, ps]
        d_hi = d_den.astype(bf16)
        d_lo = (d_den - d_hi.astype(f32)).astype(bf16)
        d_num = (d_o[:, ps] * rden[:, ps]).astype(bf16)
        dn = jnp.concatenate([d_num, d_hi * m0 + d_lo * m1], axis=1)
        dn_ref[:, 256 * p : 256 * (p + 1)] = dn

    @pl.when(step < SPAN // ROWS)
    def _():
        follows = flag(as_column(seg_ref[0]) == ends_ref[SPAN // CHUNK - 1])
        for p in range(PAIRS):
            back_acc[p] = back_acc[p] + dot(
                pq_ref[:, 512 * p : 512 * (p + 1)], dn_ref[:, 256 * p : 256 * (p + 1)] * follows, 0, 0
            )

    @pl.when(step == steps - 1)
    def _():
        core = core_ref[0]
        for ups, others, side in (
            (sent_up_ref, sent_rest_ref, 1 - core),
            (kept_up_ref, kept_rest_ref, core),
        ):
            for far in range(ups.shape[0] // group):
                at = (2 * far + side) * group
                here = slice(group * far, group * (far + 1))
                thin = pl.ds(pl.multiple_of(at * 16, 16), group * 16)
                tall = pl.ds(pl.multiple_of(at * 64, 64), group * 64)
                for f in range(FF // cut):
                    piece = up_acc[thin, cut * f : cut * (f + 1)].astype(bf16)
                    ups[here, 16 * f : 16 * (f + 1)] = piece.reshape(group, 16, cut)
                others[here, :64] = down_acc[tall].astype(bf16).reshape(group, 64, D)
                others[here, 64:] = out_acc[thin].astype(bf16).reshape(group, 16, D)
        ma, mb = half_masks(128)
        for p in range(PAIRS):
            first, second = back_acc[p, :FEATS], back_acc[p, FEATS:]
            back_ref[p, :FEATS] = first[:, :128].astype(bf16) * ma + second[:, :128].astype(bf16) * mb
            rows = []
            for side, lane in ((first, 0), (second, HD)):
                turned = side[:, 128:].T
                total = turned[lane : lane + 1] + turned[lane + 1 : lane + 2]
                high = total.astype(bf16).astype(f32)
                for part in (high, total - high):
                    rows += [part[:, :128], part[:, 128:]]
            rows.append(jnp.zeros((8, 128), f32))
            back_ref[p, FEATS:] = jnp.concatenate(rows, axis=0).astype(bf16)


def backward_kernel(pairs, ends_ref, seg_ref, gather_ref, *refs):
    refs = refs[: 7 * pairs] + refs[-4:]
    subs = ROWS // CHUNK
    step = pl.program_id(0)
    steps = pl.num_programs(0)
    at = (SPAN // ROWS + steps - 1 - step) * subs
    dqkv_ref, state_ref, grad_ref, logit_ref = refs[7 * pairs :]
    p_refs, pq_refs, pk_refs, qkv_refs, dn_refs, t_refs, back_refs = [
        refs[i * pairs : (i + 1) * pairs] for i in range(7)
    ]

    @pl.when(step == 0)
    def _():
        lane = lanes(128)
        for p in range(pairs):
            extra = back_refs[p][0, FEATS:].astype(f32)
            for i, mask in enumerate(half_masks(128)):
                rows = slice(FEATS * i, FEATS * (i + 1))
                state_ref[p, rows, :128] = (back_refs[p][0, :FEATS] * mask).astype(f32)
                total = jnp.zeros((FEATS, 128), f32)
                for t in range(2):
                    at_row = 4 * i + 2 * t
                    row = jnp.concatenate([extra[at_row : at_row + 1], extra[at_row + 1 : at_row + 2]], axis=1)
                    total = jnp.where(lane == HD * i + t, as_column(row), total)
                state_ref[p, rows, 128:] = total

    seg = seg_ref[0]
    seg_col = as_column(seg)
    two = jnp.broadcast_to(flag(lanes(128) % HD < 2), (CHUNK, 128))
    ones = jnp.ones((CHUNK, 128), bf16)
    ma, mb = half_masks(128)
    for j in reversed(range(subs)):
        rows = slice(CHUNK * j, CHUNK * (j + 1))
        _, allowed = chunk_mask(seg[:, rows])
        before = ends_ref[at + j - 1]
        last = ends_ref[at + j]
        chosen = flag(seg_col[rows] == last)
        follows = flag(seg_col[rows] == before)
        keep = (last == before).astype(f32)
        for p in range(pairs):
            v1 = jnp.concatenate([qkv_refs[p][rows, 256:], two], axis=1)
            d_p = dot(dn_refs[p][rows], masked_pair(v1, v1, 256), 1, 1).astype(bf16)
            grad_ref[p, :, :CHUNK] = d_p[:, :CHUNK] * allowed
            grad_ref[p, :, CHUNK:] = d_p[:, CHUNK:] * allowed
        for p in range(pairs):
            pq, pk, dn = pq_refs[p][rows], pk_refs[p][rows], dn_refs[p][rows]
            scores = p_refs[p][rows]
            v2 = qkv_refs[p][rows, 256:]
            compact = t_refs[p][j, 0]
            narrow = masked_pair(compact, compact, 256)
            state = state_ref[p]
            back = state.astype(bf16)
            back = masked_pair(back[:FEATS], back[FEATS:], 256)
            d_pa = grad_ref[p, :, :CHUNK]
            d_pb = grad_ref[p, :, CHUNK:]
            dn_f = dn * follows
            d_pq = dot(dn_f, narrow, 1, 1) + jnp.concatenate(
                [dot(d_pa, pk[:, :FEATS]), dot(d_pb, pk[:, FEATS:])], axis=1
            )
            logit_ref[0, p, rows] = d_pq.astype(bf16) * pq
            vw = jnp.concatenate([v2, ones], axis=1) * chosen
            d_pk = dot(vw, back, 1, 1) + jnp.concatenate(
                [dot(d_pa, pq[:, :FEATS], 0, 0), dot(d_pb, pq[:, FEATS:], 0, 0)], axis=1
            )
            logit_ref[1, p, rows] = d_pk.astype(bf16) * pk
            d_num = dn[:, :128]
            d_v = (
                dot(pk * chosen, back[:, :128])
                + dot(scores[:, :CHUNK], d_num * ma, 0, 0)
                + dot(scores[:, CHUNK:], d_num * mb, 0, 0)
            )
            dqkv_ref[rows, 384 * p + 256 : 384 * p + 384] = d_v.astype(bf16)
            state_ref[p] = keep * state + dot(pq, dn_f, 0, 0)
    scale2 = feature_scale * feature_scale
    for p in range(pairs):
        for i in range(2):
            u = qkv_refs[p][:, 128 * i : 128 * (i + 1)].astype(f32)
            through = dot(logit_ref[i, p], gather_ref[...])
            d_u = through[:, :128] * feature_scale - u * through[:, 128:] * scale2
            dqkv_ref[:, 384 * p + 128 * i : 384 * p + 128 * (i + 1)] = d_u.astype(bf16)


def input_kernel(runs, dest_ref, dqkv_ref, x_ref, dy1_ref, gains_ref, *refs):
    *pieces, dx_ref, wq_ref, sem = refs

    @pl.when(pl.program_id(0) == 0)
    def _():
        copy_blocks(runs, pieces, dest_ref, wq_ref, sem)()

    d_h1 = dot(dqkv_ref[...], wq_ref[:, :, : 3 * D].reshape(D, 3 * D), 1, 1)
    x = x_ref[...].astype(f32)
    r1 = rms_scale(x)
    n1 = x * r1
    e1 = d_h1 * gains_ref[0:1]
    dx_ref[...] = dy1_ref[...] + r1 * (e1 - n1 * jnp.mean(e1 * n1, axis=-1, keepdims=True))


def finish_kernel(q_ref, kept_ref, came_ref, packed_ref, later_ref, sq_ref, sr_ref, gg_ref, spread_ref):
    share = q_ref.shape[1]
    sum_q = jnp.sum(q_ref[...].astype(f32), axis=0)
    sum_r = kept_ref[...].astype(f32) + came_ref[...].astype(f32)
    sq_ref[...] = sum_q
    sr_ref[...] = sum_r
    packed = packed_ref[...].astype(f32)
    tops = jnp.sum(packed[:, : 3 * D] * sum_q, axis=1, keepdims=True)
    rows = jnp.sum(later_ref[: 4 * share].astype(f32) * sum_r[: 4 * share], axis=1, keepdims=True)
    lows = rows[:share]
    for f in range(1, 4):
        lows = lows + rows[share * f : share * (f + 1)]
    gg = jnp.concatenate([tops, lows], axis=1) / packed[:, 3 * D : 3 * D + 2]
    gg_ref[...] = jnp.concatenate([gg, jnp.zeros((share, 126), f32)], axis=1).T[:2]
    total = jnp.sum(sum_q * sum_q) + jnp.sum(sum_r * sum_r) + jnp.sum(gg * gg)
    spread_ref[...] = jnp.full(spread_ref.shape, total, f32)


def axis_bits():
    row_bits = (lax.axis_size("row") - 1).bit_length()
    head_bits = (lax.axis_size("head") - 1).bit_length()
    row = [("row", b, b) for b in range(row_bits)]
    head = [("head", b, row_bits + b) for b in range(head_bits)]
    return row, head


def swap(value, axis, bit):
    return lax.ppermute(value, axis, [(i, i ^ (1 << bit)) for i in range(lax.axis_size(axis))])


def swap_far(value, mask):
    return lax.ppermute(value, AXES, [(i, i ^ mask) for i in range(lax.axis_size(AXES))])


def tied(value, *others):
    return lax.optimization_barrier((value,) + others)[0]


class Gather:
    def __init__(self, shard):
        self.buf = shard[None]
        self.offsets = [0]

    def start(self, axis, bit, place):
        self.came = swap(self.buf, axis, bit)
        self.mask = 1 << place

    def finish(self, *others):
        own = tied(self.buf, *others) if others else self.buf
        self.buf = jnp.concatenate([own, self.came], axis=0)
        self.offsets = self.offsets + [offset ^ self.mask for offset in self.offsets]


def device_index():
    return lax.axis_index("head") * lax.axis_size("row") + lax.axis_index("row")


def doubled(order, offsets=(0,)):
    offsets = list(offsets)
    for _, _, place in order:
        offsets += [offset ^ (1 << place) for offset in offsets]
    return offsets


def block_places(offsets):
    return (device_index() ^ jnp.asarray(offsets, jnp.int32)).astype(jnp.int32)


def in_order(pieces, offsets):
    slots = [0] * len(offsets)
    for slot, offset in enumerate(offsets):
        slots[offset] = slot
    every = jnp.arange(len(offsets), dtype=jnp.int32) ^ device_index()
    order = jnp.asarray(slots, jnp.int32)[every]
    return jnp.take(jnp.concatenate(pieces, axis=0), order, axis=0)


def single_runs(pieces):
    return [(i, k, 1) for i, piece in enumerate(pieces) for k in range(piece.shape[0])]


class Halving:
    def __init__(self, kept, came, places):
        self.places = sorted(places, reverse=True)
        self.parts = [kept] if came is None else [kept, came]
        self.parts = [self.split(part) for part in self.parts]

    def split(self, part):
        inner = part.shape[1:] if part.ndim == 3 else part.shape[-2:]
        return part.reshape((2,) * len(self.places) + inner)

    def take(self, index, at):
        total = sum(
            lax.dynamic_index_in_dim(part, index, at, keepdims=False).astype(f32)
            for part in self.parts
        )
        return total.astype(bf16)

    def after(self, *others):
        self.parts[0] = tied(self.parts[0], *others)
        return self

    def send(self, axis, bit, place):
        at = self.places.index(place)
        mine = (lax.axis_index(axis) >> bit) & 1
        sent = self.take(1 - mine, at)
        came = swap(sent, axis, bit)
        self.parts = [self.take(mine, at), came]
        self.places.remove(place)
        return sent

    def total(self):
        return sum(part.astype(f32) for part in self.parts)


def late_in_order(pieces, offsets, share):
    whole = in_order(pieces, offsets)
    parts = 16 // share
    whole = whole.reshape(D // 16, parts, 9 * share, 512)
    ups = whole[:, :, : 4 * share].reshape(D // 16, parts, 4, share, 512)
    ups = ups.transpose(0, 2, 1, 3, 4).reshape(D // 16, 64, 512)
    downs = whole[:, :, 4 * share : 8 * share].reshape(D // 16, 64, 512)
    outs = whole[:, :, 8 * share :].reshape(D // 16, 16, 512)
    return jnp.concatenate([ups, downs, outs], axis=1)


def ups_by_device(blocks, share):
    ups = blocks.reshape(-1, 4, 16 // share, share, 512)
    return ups.transpose(0, 2, 1, 3, 4).reshape(-1, 4 * share, 512)


def rest_by_device(blocks, share):
    downs = blocks[:, :64].reshape(-1, 4 * share, 512)
    outs = blocks[:, 64:].reshape(-1, share, 512)
    return jnp.concatenate([downs, outs], axis=1)


def core_groups():
    heads, rows = lax.axis_size("head"), lax.axis_size("row")
    return [[h * rows + r for h in range(c, heads, 2) for r in range(rows)] for c in (0, 1)]


def exchange(blocks):
    return lax.all_to_all(
        blocks, AXES, split_axis=0, concat_axis=0, axis_index_groups=core_groups(), tiled=True
    )


def total_of(spread):
    came = lax.all_to_all(spread, AXES, split_axis=0, concat_axis=0, tiled=True)
    return jnp.sum(came[:, 0, 0])


def adam_update(
    weight, gradient, first_moment, second_moment, clip_factor, step_value, step_rate, decay_rate
):
    clipped = gradient * clip_factor
    next_first = beta_first * first_moment + (1.0 - beta_first) * clipped
    next_second = beta_second * second_moment + (1.0 - beta_second) * clipped * clipped
    first_hat = next_first / (1.0 - beta_first**step_value)
    second_hat = next_second / (1.0 - beta_second**step_value)
    updated = weight - step_rate * (
        first_hat / (jnp.sqrt(second_hat) + adam_eps) + decay_rate * weight
    )
    return (clipped, next_first, next_second, updated)


def params(limit=60):
    return pltpu.CompilerParams(
        dimension_semantics=("arbitrary",), vmem_limit_bytes=limit << 20
    )


def cost(us):
    return pl.CostEstimate(flops=us * 50000000, transcendentals=0, bytes_accessed=us * 150000)


def fixed(shape):
    zeros = (0,) * len(shape)
    return pl.BlockSpec(shape, lambda *_: zeros, pipeline_mode=pl.Buffered(1))


def first_at(shape, offset):
    rest = (0,) * (len(shape) - 1)
    return pl.BlockSpec(shape, lambda c, *_: (jnp.maximum(c - offset, 0),) + rest)


def by_step(shape):
    return first_at(shape, 0)


def forward_call(runs, ends, dest, x_ahead, x, seg_rows, spread, pieces):
    length = x.shape[0]
    chunks, halo, wide = length // CHUNK, SPAN // ROWS, PAIRS * 2 * FEATS
    own = partial(first_at, offset=halo)
    outs = [
        ((ROWS, D), (length, D), bf16),
        ((ROWS, 3 * D), (length, 3 * D), bf16),
        ((ROWS, wide), (length, wide), bf16),
        ((ROWS, wide), (length, wide), bf16),
        ((ROWS, wide), (length, wide), bf16),
        ((ROWS // CHUNK, PAIRS, FEATS, 256), (chunks, PAIRS, FEATS, 256), bf16),
        ((ROWS, D), (length, D), bf16),
        ((ROWS, D), (length, D), f32),
    ]
    return pl.pallas_call(
        partial(forward_kernel, runs),
        grid_spec=pltpu.PrefetchScalarGridSpec(
            num_scalar_prefetch=2,
            grid=(halo + length // ROWS,),
            in_specs=[
                pl.BlockSpec((ROWS, D), lambda c, *_: (jnp.minimum(c, halo - 1), 0)),
                own((ROWS, D)),
                by_step((1, 1, ROWS)),
                fixed(spread.shape),
            ]
            + [pl.BlockSpec(memory_space=pl.ANY)] * len(pieces),
            out_specs=[own(block) for block, _, _ in outs] + [fixed((8, D))],
            scratch_shapes=[
                pltpu.VMEM((PAIRS, 2 * FEATS, 256), f32),
                pltpu.VMEM((D // 16, 16, 3 * D + 128), bf16),
                pltpu.SemaphoreType.DMA((len(runs),)),
            ],
        ),
        out_shape=[jax.ShapeDtypeStruct(shape, kind) for _, shape, kind in outs]
        + [jax.ShapeDtypeStruct((8, D), f32)],
        compiler_params=params(),
        cost_estimate=cost(35),
        name="forward",
    )(ends, dest, x_ahead, x, seg_rows, spread, *pieces)


def middle_call(group, runs, ends, core, dest, x, g, o, rden, pq, seg_rows, gain_rows, pieces):
    length, wide = x.shape[0], pq.shape[1]
    near_steps = SPAN // ROWS
    by_step_ahead = pl.BlockSpec((1, 1, ROWS), lambda c, *_: (c + near_steps, 0, 0))

    outs = [
        ((ROWS, D), (length, D), bf16),
        ((ROWS, D), (length, D), f32),
        ((ROWS, PAIRS * 256), (length, PAIRS * 256), bf16),
    ]
    sums = [(D // 32, 64, 512), (D // 32, 80, 512)] * 2 + [(PAIRS, FEATS + 16, 128)]
    return pl.pallas_call(
        partial(middle_kernel, group, runs),
        grid_spec=pltpu.PrefetchScalarGridSpec(
            num_scalar_prefetch=3,
            grid=(length // ROWS,),
            in_specs=[by_step((ROWS, D))] * 4
            + [
                pl.BlockSpec((ROWS, wide), lambda c, *_: (jnp.minimum(c, near_steps - 1), 0)),
                by_step_ahead,
                fixed((8, D)),
            ]
            + [pl.BlockSpec(memory_space=pl.ANY)] * len(pieces),
            out_specs=[by_step(block) for block, _, _ in outs] + [fixed(shape) for shape in sums],
            scratch_shapes=[
                pltpu.VMEM((D, FF), f32),
                pltpu.VMEM((FF, D), f32),
                pltpu.VMEM((D, D), f32),
                pltpu.VMEM((PAIRS, 2 * FEATS, 256), f32),
                pltpu.VMEM((ROWS, FF), bf16),
                pltpu.VMEM((ROWS, FF), bf16),
                pltpu.VMEM((D // 16, 144, 512), bf16),
                pltpu.SemaphoreType.DMA((len(runs),)),
            ],
        ),
        out_shape=[jax.ShapeDtypeStruct(shape, kind) for _, shape, kind in outs]
        + [jax.ShapeDtypeStruct(shape, bf16) for shape in sums],
        compiler_params=params(),
        cost_estimate=cost(48),
        name="middle",
    )(ends, core, dest, x, g, o, rden, pq, seg_rows, gain_rows, *pieces)


def backward_call(at, parts, ends, seg_rows, gather, arrays, *written):
    length = arrays[0].shape[0]
    steps, halo = length // ROWS, SPAN // ROWS
    count = PAIRS // parts
    chosen = range(at * count, (at + 1) * count)

    def falling(shape, at=0):
        rest = (0,) * (len(shape) - 2)
        return pl.BlockSpec(shape, lambda c, *_: (steps - 1 - c, at) + rest)

    def state(at):
        return pl.BlockSpec(
            (1, FEATS + 16, 128), lambda *_: (at, 0, 0), pipeline_mode=pl.Buffered(1)
        )

    specs = [pl.BlockSpec((1, 1, ROWS), lambda c, *_: (steps + halo - 1 - c, 0, 0))]
    specs += [fixed(gather.shape)]
    for shape in ((ROWS, 512),) * 3 + ((ROWS, 384), (ROWS, 256), (ROWS // CHUNK, 1, 256, 256)):
        specs += [falling(shape, p) for p in chosen]
    specs += [state(p) for p in chosen]
    operands = [array for array in arrays for _ in chosen]
    return pl.pallas_call(
        partial(backward_kernel, count),
        grid_spec=pltpu.PrefetchScalarGridSpec(
            num_scalar_prefetch=1,
            grid=(steps,),
            in_specs=specs + [pl.BlockSpec(memory_space=pl.ANY)] * len(written),
            out_specs=falling((ROWS, 384 * count), at),
            scratch_shapes=[
                pltpu.VMEM((count, 2 * FEATS, 256), f32),
                pltpu.VMEM((count, CHUNK, 2 * CHUNK), bf16),
                pltpu.VMEM((2, count, ROWS, 2 * FEATS), bf16),
            ],
        ),
        out_shape=jax.ShapeDtypeStruct((length, 3 * D), bf16),
        input_output_aliases={3 + len(operands): 0} if written else {},
        compiler_params=params(),
        cost_estimate=cost(8 * count),
        name="backward",
    )(ends, seg_rows, gather, *operands, *written)


def input_call(runs, dest, dqkv, x, dy1, gain_rows, pieces):
    length = x.shape[0]
    return pl.pallas_call(
        partial(input_kernel, runs),
        grid_spec=pltpu.PrefetchScalarGridSpec(
            num_scalar_prefetch=1,
            grid=(length // ROWS,),
            in_specs=[
                by_step((ROWS, 3 * D)),
                by_step((ROWS, D)),
                by_step((ROWS, D)),
                fixed((8, D)),
            ]
            + [pl.BlockSpec(memory_space=pl.ANY)] * len(pieces),
            out_specs=by_step((ROWS, D)),
            scratch_shapes=[
                pltpu.VMEM((D // 16, 16, 3 * D + 128), bf16),
                pltpu.SemaphoreType.DMA((len(runs),)),
            ],
        ),
        out_shape=jax.ShapeDtypeStruct((length, D), f32),
        compiler_params=params(),
        cost_estimate=cost(10),
        name="input_grad",
    )(dest, dqkv, x, dy1, gain_rows, *pieces)


def per_device(
    inputs,
    cotangent,
    segments,
    feature_matrix,
    w_qkv,
    w_out,
    w_up,
    w_down,
    gains,
    first_qkv,
    second_qkv,
    first_out,
    second_out,
    first_up,
    second_up,
    first_down,
    second_down,
    first_gains,
    second_gains,
    step_count,
):
    heads = lax.axis_size("head")
    row_bits, head_bits = axis_bits()
    x = inputs[0]
    g = cotangent[0]
    length = x.shape[0]
    share = w_qkv.shape[0]
    group = lax.axis_size("row") * share // 16

    packed = jnp.concatenate(
        [
            w_qkv.reshape(share, 3, PAIRS, 128).transpose(0, 2, 1, 3).reshape(share, 3 * D),
            gains,
            jnp.zeros((share, 126), f32),
        ],
        axis=1,
    ).astype(bf16)
    forward_pairs = [(i, i + 1) for i in range(heads - 1)]
    backward_pairs = [(i + 1, i) for i in range(heads - 1)]
    weights = Gather(packed)
    core_bit, *far_bits = head_bits
    order = row_bits[:0:-1] + far_bits + row_bits[:1] + [core_bit]
    tail = x[length - SPAN :]
    up, down, out = [tied(weight, tail) for weight in (w_up, w_down, w_out)]
    later_own = jnp.concatenate(
        [up[:, 512 * j : 512 * (j + 1)] for j in range(FF // 512)] + [down, out], axis=0
    ).astype(bf16)
    later = Gather(later_own)
    later_order = row_bits[:1:-1] + row_bits[:1] + far_bits[:-1]
    quad = [row_bits[1], far_bits[-1]]
    weights.buf = tied(weights.buf, tail)
    x_ahead = lax.ppermute(tail, "head", forward_pairs)
    weights.start(*order[0])
    later.start(*later_order[0])
    weights.finish()
    weights.start(*order[1])
    later.finish()
    later.start(*later_order[1])
    row_segments = tied(segments[0], weights.buf)
    padded = jnp.concatenate([jnp.full((SPAN,), -1, jnp.int32), row_segments])
    near = lax.dynamic_slice_in_dim(padded, lax.axis_index("head") * length, length + SPAN)
    ends = near[CHUNK - 1 :: CHUNK]
    seg_rows = near.astype(f32).reshape(-1, 1, ROWS)
    fm = feature_matrix
    nothing = jnp.zeros_like(fm.T)
    spread = jnp.concatenate(
        [
            jnp.concatenate([fm.T, nothing], axis=1),
            jnp.concatenate([nothing, fm.T], axis=1),
        ],
        axis=0,
    )
    zero = jnp.zeros((FEATS, HD), bf16)
    one = jnp.ones((FEATS, HD), bf16)
    gather = jnp.concatenate(
        [
            jnp.concatenate([fm, zero, one, zero], axis=1),
            jnp.concatenate([zero, fm, zero, one], axis=1),
        ],
        axis=0,
    )
    weights.finish(ends, seg_rows, later.buf)
    weights.start(*order[2])
    offsets = doubled(order)
    late_offsets = doubled(quad + [core_bit], doubled(later_order))
    dest, late_dest = block_places(offsets), block_places(late_offsets)
    weights.finish(spread, gather, x_ahead, dest, late_dest)
    for stage in later_order[1:]:
        later.finish()
        if stage != later_order[-1]:
            later.start(*later_order[later_order.index(stage) + 1])
    flips = [1 << place for _, _, place in quad]
    late = [later.buf] + [swap(later.buf, axis, bit) for axis, bit, _ in quad]
    late.append(swap_far(later.buf, sum(flips)))
    near = [swap(later.buf, "head", 0)]
    for stage in order[3:-1]:
        weights.start(*stage)
        weights.finish(later.buf)
    pieces = [weights.buf]
    weights.start(*order[-1])
    pieces.append(weights.came)
    if share == 16:
        runs = single_runs(pieces)
    else:
        pieces = [in_order(pieces, offsets).reshape(D // 16, 16, 3 * D + 128)]
        runs, dest = [(0, 0, D // 16)], jnp.zeros((1,), jnp.int32)
        late_dest = dest
    core = (lax.axis_index("head") & 1).reshape(1)

    h1, qkv, pq, pk, scores, states, o, rden, gain_rows = forward_call(
        runs, ends, dest, tied(x_ahead, later.buf, late_dest), x, seg_rows, spread, pieces
    )
    late[1:] = [tied(piece, o) for piece in late[1:]]
    near = [tied(near[0], o)] + [swap(piece, "head", 0) for piece in late[1:]]
    late = late + near
    late_runs = single_runs(late)
    if share != 16:
        late = [late_in_order(late, late_offsets, share)]
        late_runs = [(0, 0, D // 16)]
    out_act, dy1, dn, sent_up, sent_rest, kept_up, kept_rest, back = middle_call(
        group, late_runs, ends, core, late_dest, x, g, o, rden, pq, seg_rows, gain_rows, late
    )
    if share != 16:
        sent_up, kept_up = ups_by_device(sent_up, share), ups_by_device(kept_up, share)
        sent_rest, kept_rest = rest_by_device(sent_rest, share), rest_by_device(kept_rest, share)
    back_in = lax.ppermute(back, "head", backward_pairs)
    came_up = swap(sent_up, "head", 0)
    came_rest = swap(sent_rest, "head", 0)

    def attention_back(at, back_in, *written):
        arrays = (scores, pq, pk, qkv, dn, states, back_in)
        return backward_call(at, 1, ends, seg_rows, gather, arrays, *written)

    lower = [(axis, bit, place - (place > core_bit[2])) for axis, bit, place in far_bits]
    first_order = lower + row_bits[:1]
    second_order = row_bits[:1] + lower
    last_order = row_bits[1:]
    places = [place for _, _, place in first_order + last_order]
    cut = 4 * share

    kept_up, kept_rest = tied(kept_up, back_in), tied(kept_rest, back_in)
    first = Halving(kept_up, came_up, places)
    second = Halving(kept_rest, came_rest, places)
    back_in = tied(back_in, first.send(*first_order[0]), second.send(*second_order[0]))
    dqkv = attention_back(0, back_in)

    moved = []
    for i, (left, right) in enumerate(zip(first_order[1:], second_order[1:])):
        for half, stage in ((first, left), (second, right)):
            half.parts = [tied(part, dqkv) for part in half.parts]
            moved.append(half.send(*stage))
    g_qkv = dot(tied(h1, dqkv, *moved), dqkv, 0, 0).astype(bf16).reshape(heads // 2, 2, -1, 3 * D)
    left, right = [[tied(part, g_qkv) for part in half.parts] for half in (first, second)]
    rest = Halving(jnp.concatenate([left[0], right[0]], axis=-2), None, first.places)
    rest.parts.append(jnp.concatenate([left[1], right[1]], axis=-2))
    moved = rest.send(*last_order[0])
    g_qkv = tied(g_qkv, moved)
    sent_qkv = lax.dynamic_index_in_dim(g_qkv, 1 - core[0], 1, False)
    came_qkv = swap(sent_qkv, "head", 0)
    kept_qkv = tied(lax.dynamic_index_in_dim(g_qkv, core[0], 1, False), *rest.parts)
    merged_qkv = (kept_qkv.astype(f32) + came_qkv.astype(f32)).astype(bf16)
    all_qkv = exchange(merged_qkv.reshape(-1, share, 3 * D))
    dx = input_call(runs, dest, dqkv, x, tied(dy1, merged_qkv), gain_rows, pieces)
    for stage in last_order[1:]:
        rest.parts = [tied(part, dx) for part in rest.parts]
        rest.send(*stage)
    kept, came = rest.parts
    count = lax.axis_size(AXES)
    sum_qkv, sums, sum_gains, spread = pl.pallas_call(
        finish_kernel,
        out_shape=[
            jax.ShapeDtypeStruct((share, 3 * D), f32),
            jax.ShapeDtypeStruct((9 * share, 512), f32),
            jax.ShapeDtypeStruct((2, share), f32),
            jax.ShapeDtypeStruct((count, 8, 128), f32),
        ],
        name="finish",
    )(all_qkv, kept, came, packed, later_own)
    sum_qkv = sum_qkv.reshape(share, PAIRS, 3, 128).transpose(0, 2, 1, 3).reshape(share, 3, D)
    sum_up = sums[: 4 * share].reshape(4, share, 512).transpose(1, 0, 2).reshape(share, FF)
    sum_down = sums[4 * share : 8 * share]
    sum_out = sums[8 * share :]
    reduced = lax.optimization_barrier((sum_qkv, sum_out, sum_up, sum_down, sum_gains))
    reduced = reduced[:4] + (reduced[4].T,)
    total_squares = total_of(spread)
    grad_norm = jnp.sqrt(total_squares)
    clip_factor = jnp.minimum(1.0, max_norm / (grad_norm + 1e-06))
    step_value = step_count.astype(f32)
    update = partial(adam_update, clip_factor=clip_factor, step_value=step_value)
    qkv_parts = update(
        w_qkv, reduced[0], first_qkv, second_qkv, step_rate=matrix_rate, decay_rate=matrix_decay
    )
    out_parts = update(
        w_out, reduced[1], first_out, second_out, step_rate=output_rate, decay_rate=matrix_decay
    )
    up_parts = update(
        w_up, reduced[2], first_up, second_up, step_rate=matrix_rate, decay_rate=matrix_decay
    )
    down_parts = update(
        w_down, reduced[3], first_down, second_down, step_rate=matrix_rate, decay_rate=matrix_decay
    )
    gain_parts = update(
        gains, reduced[4], first_gains, second_gains, step_rate=gain_rate, decay_rate=0.0
    )
    return (
        (out_act[None], dx[None], grad_norm)
        + qkv_parts
        + out_parts
        + up_parts
        + down_parts
        + gain_parts
    )


def solution(mesh):
    token = P("row", "head", None)
    three = P(AXES, None, None)
    two = P(AXES, None)
    placed = (token, token, P("row", None), P(), three, two, two, two, two)
    placed = placed + (three, three) + (two,) * 8 + (P(),)
    return jax.shard_map(
        per_device,
        mesh=mesh,
        in_specs=placed,
        out_specs=(token, token, P()) + (three,) * 4 + (two,) * 16,
        check_vma=False,
    )
```
